32 devices in a mesh: ctx: 8 (over z, x), fsdp: 4 (over y, core).
Axes of the slice: x: 2, y: 2, z: 4, core: 2. Of those that a mesh axis runs over, the one named last changes fastest.
Arguments:
- inputs: bfloat16 [8, 512, 1024], P('fsdp', 'ctx'), may hold values from -6 to 6
- gain_one: bfloat16 [1024], P('fsdp'), may hold values from 0.25 to 1.75
- w_qkv: bfloat16 [1024, 3072], P('fsdp')
- w_attn: bfloat16 [1024, 1024], P('fsdp'), may hold values from -0.75 to 0.75
- gain_two: bfloat16 [1024], P('fsdp'), may hold values from 0.25 to 1.75
- w_in: bfloat16 [1024, 5248], P('fsdp'), may hold values from -0.1875 to 0.1875
- w_ffn: bfloat16 [2624, 1024], P('fsdp'), may hold values from -0.125 to 0.125
- cotangent: bfloat16 [8, 512, 1024], P('fsdp', 'ctx'), may hold values from -6 to 6
Outputs:
- output: bfloat16 [8, 512, 1024], P('fsdp', 'ctx')
- grad_input: float32 [8, 512, 1024], P('fsdp', 'ctx')
- grad_gain_one: float32 [1024], P('fsdp')
- grad_w_qkv: float32 [1024, 3072], P('fsdp')
- grad_w_attn: float32 [1024, 1024], P('fsdp')
- grad_gain_two: float32 [1024], P('fsdp')
- grad_w_in: float32 [1024, 5248], P('fsdp')
- grad_w_ffn: float32 [2624, 1024], P('fsdp')
The draws below stay inside these ranges and needn't reach their ends.
All inputs are finite; a program needn't handle non-finite values.
Results may differ from the reference program's by a relative error of at most 0.023.
Values may be sent and summed in bfloat16 or wider, within the bound.
A program may use at most 256 MiB of HBM per device.

```python
import math
import jax
import jax.numpy as jnp
from jax import lax

D = 1024
HEADS = 16
HEAD_DIM = 64
FF = 2624
LEN = 512
SEQS = 8


def draw_w_qkv(key, part):
    base_key = jax.random.fold_in(key, 11)
    keys_all = jax.random.split(base_key, 1)
    scale_in = D ** (-0.5)
    base_vals = jnp.clip(jax.random.normal(keys_all[0], (D, 3 * D), jnp.float32), -6.0, 6.0) * scale_in
    return base_vals.astype(jnp.bfloat16)


def steps_of(own_key, shape, cuts, smallest, high):
    level = 1.0
    for dim, parts in cuts:
        draws = jax.random.uniform(jax.random.fold_in(jax.random.fold_in(own_key, 6), dim), (parts,), jnp.float32, smallest / len(cuts), high / len(cuts))
        level = level * jnp.repeat(jnp.exp(draws), shape[dim] // parts).reshape((-1,) + (1,) * (len(shape) - 1 - dim))
    return level


def bell_draw(key, dims, scale, reach, pieces=(), held_as=jnp.bfloat16):
    values = scale * jax.random.normal(key, dims, jnp.float32)
    if pieces:
        values = values * steps_of(key, dims, pieces, -0.22, 0.18)
    return jnp.clip(values, -reach, reach).astype(held_as)


def setup_inputs(seed: int = 0) -> dict:
    key_of = jax.random.split(jax.random.key(seed), 9)
    return {
        "inputs": bell_draw(key_of[0], (SEQS, LEN, D), 1.0, 6.0, ((0, 4), (1, 8))),
        "gain_one": jnp.clip(1.0 + 0.15 * jax.random.normal(key_of[1], (D,), jnp.float32), 0.25, 1.75).astype(jnp.bfloat16),
        "w_qkv": draw_w_qkv(jax.random.fold_in(key_of[8], 71), 0),
        "w_attn": bell_draw(key_of[3], (D, D), (max(D * 32 // LEN, 1)) ** -0.5, 0.75, ((0, 4),)),
        "gain_two": jnp.clip(1.0 + 0.15 * jax.random.normal(key_of[4], (D,), jnp.float32), 0.25, 1.75).astype(jnp.bfloat16),
        "w_in": bell_draw(key_of[5], (D, 2 * FF), D ** -0.5, 0.1875, ((0, 4),)),
        "w_ffn": bell_draw(key_of[6], (FF, D), FF ** -0.5, 0.125, ((0, 4),)),
        "cotangent": bell_draw(key_of[7], (SEQS, LEN, D), 1.0, 6.0, ((0, 4), (1, 8))),
    }


EPSILON = 1e-05
ROPE_THETA = 160000.0

def to_half(values_in):
    return lax.optimization_barrier(values_in.astype(jnp.bfloat16))

def as_wide(values_in):
    return values_in.astype(jnp.float32)

def norm_parts(values_in):
    mean_val = lax.optimization_barrier(jnp.mean(values_in, axis=-1, keepdims=True))
    centred = values_in - mean_val
    variance = lax.optimization_barrier(jnp.mean(centred * centred, axis=-1, keepdims=True))
    inv_std = lax.rsqrt(variance + EPSILON)
    return (centred * inv_std, inv_std)

def norm_back(grad_normed, normed, inv_std):
    return inv_std * (grad_normed - lax.optimization_barrier(jnp.mean(grad_normed, axis=-1, keepdims=True)) - normed * lax.optimization_barrier(jnp.mean(grad_normed * normed, axis=-1, keepdims=True)))

def rotary_tables(positions):
    half_dim = HEAD_DIM // 2
    inv_freq = ROPE_THETA ** (-(jnp.arange(half_dim, dtype=jnp.float32) * 2.0) / HEAD_DIM)
    angles = positions.astype(jnp.float32)[:, None] * inv_freq[None, :]
    cosine = jnp.concatenate([jnp.cos(angles), jnp.cos(angles)], axis=-1)[:, None, :]
    sine_part = jnp.concatenate([jnp.sin(angles), jnp.sin(angles)], axis=-1)[:, None, :]
    return (cosine, sine_part)

def rotate(values_in, cosine, sine_part):
    half_dim = values_in.shape[-1] // 2
    turned = jnp.concatenate([-values_in[..., half_dim:], values_in[..., :half_dim]], axis=-1)
    return values_in * cosine + turned * sine_part

def rotate_back(grads, cosine, sine_part):
    half_dim = grads.shape[-1] // 2
    scaled = grads * sine_part
    turned = jnp.concatenate([scaled[..., half_dim:], -scaled[..., :half_dim]], axis=-1)
    return grads * cosine + turned

def gelu_slope(inner_part):
    cumulative = 0.5 * (1.0 + jax.scipy.special.erf(inner_part * 0.7071067811865476))
    density = jnp.exp(-0.5 * inner_part * inner_part) * 0.3989422804014327
    return cumulative + inner_part * density

def sequence_pass(tokens, grad_out, gain_one, w_qkv, w_attn, gain_two, w_in, w_ffn):
    length = tokens.shape[0]
    scale_factor = HEAD_DIM ** (-0.5)
    tokens_f = tokens.astype(jnp.float32)
    normed_one, inv_one = norm_parts(tokens_f)
    input_one = to_half(normed_one * gain_one.astype(jnp.float32))
    project = jnp.dot(input_one, w_qkv, preferred_element_type=jnp.float32)
    cosine, sine_part = rotary_tables(jnp.arange(length, dtype=jnp.int32))
    shaped = project.reshape(length, 3, HEADS, HEAD_DIM)
    queries = to_half(rotate(shaped[:, 0], cosine, sine_part))
    key_rows = to_half(rotate(shaped[:, 1], cosine, sine_part))
    value_rows = to_half(shaped[:, 2])
    keys_wide = as_wide(key_rows)
    values_wide = as_wide(value_rows)
    block_len = math.gcd(length, 512)
    blocks_num = length // block_len
    query_blocks = queries.reshape(blocks_num, block_len, HEADS, HEAD_DIM)

    def attend(query_block):
        scores = jnp.einsum('thd,shd->ths', as_wide(query_block), keys_wide) * scale_factor
        row_max = lax.optimization_barrier(jnp.max(scores, axis=-1))
        exp_vals = jnp.exp(scores - row_max[..., None])
        row_sum = lax.optimization_barrier(jnp.sum(exp_vals, axis=-1))
        weighted = jnp.einsum('ths,shd->thd', as_wide(to_half(exp_vals)), values_wide)
        return (weighted / row_sum[..., None], row_max + jnp.log(row_sum))
    attn_f, log_sum = lax.map(attend, query_blocks)
    attn_f = attn_f.reshape(length, HEADS, HEAD_DIM)
    log_sum = log_sum.reshape(length, HEADS)
    attn_b = to_half(attn_f.reshape(length, D))
    resid = tokens_f + jnp.dot(attn_b, w_attn, preferred_element_type=jnp.float32)
    normed_two, inv_two = norm_parts(resid)
    input_two = to_half(normed_two * gain_two.astype(jnp.float32))
    widened = jnp.dot(input_two, w_in, preferred_element_type=jnp.float32)
    inner_part = widened[:, :FF]
    gating = widened[:, FF:]
    activated = jax.nn.gelu(inner_part, approximate=False)
    hidden = to_half(activated * gating)
    output = (resid + jnp.dot(hidden, w_ffn, preferred_element_type=jnp.float32)).astype(jnp.bfloat16)
    grad_ffn = jnp.dot(hidden.T, grad_out, preferred_element_type=jnp.float32)
    grad_hidden = jnp.dot(grad_out, w_ffn.T, preferred_element_type=jnp.float32)
    grad_inner = grad_hidden * gating * gelu_slope(inner_part)
    grad_gating = grad_hidden * activated
    grad_wide = to_half(jnp.concatenate([grad_inner, grad_gating], axis=-1))
    grad_in = jnp.dot(input_two.T, grad_wide, preferred_element_type=jnp.float32)
    grad_normed_two = jnp.dot(grad_wide, w_in.T, preferred_element_type=jnp.float32)
    grad_g2 = lax.optimization_barrier(jnp.sum(grad_normed_two * normed_two, axis=0))
    grad_resid = grad_out.astype(jnp.float32) + norm_back(grad_normed_two * gain_two.astype(jnp.float32), normed_two, inv_two)
    resid_b = to_half(grad_resid)
    grad_attn_w = jnp.dot(attn_b.T, resid_b, preferred_element_type=jnp.float32)
    grad_mixed = to_half(jnp.dot(resid_b, w_attn.T, preferred_element_type=jnp.float32)).reshape(length, HEADS, HEAD_DIM)
    row_delta = lax.optimization_barrier(jnp.sum(as_wide(grad_mixed) * attn_f, axis=-1))

    def back(state_in, block_items):
        grad_key_all, grad_value_all = state_in
        query_block, grad_block, lse_block, delta_block = block_items
        scores = jnp.einsum('thd,shd->ths', as_wide(query_block), keys_wide) * scale_factor
        probs = jnp.exp(scores - lse_block[..., None])
        grad_value_all = grad_value_all + jnp.einsum('ths,thd->shd', as_wide(to_half(probs)), as_wide(grad_block))
        grad_probs = jnp.einsum('thd,shd->ths', as_wide(grad_block), values_wide)
        grad_scores = as_wide(to_half(probs * (grad_probs - delta_block[..., None])))
        grad_query = jnp.einsum('ths,shd->thd', grad_scores, keys_wide) * scale_factor
        grad_key_all = grad_key_all + jnp.einsum('ths,thd->shd', grad_scores, as_wide(query_block)) * scale_factor
        return ((grad_key_all, grad_value_all), grad_query)
    zero_kv = jnp.zeros((length, HEADS, HEAD_DIM), jnp.float32)
    block_items = (query_blocks, grad_mixed.reshape(blocks_num, block_len, HEADS, HEAD_DIM), log_sum.reshape(blocks_num, block_len, HEADS), row_delta.reshape(blocks_num, block_len, HEADS))
    (grad_key_all, grad_value_all), grad_query = lax.scan(back, (zero_kv, zero_kv), block_items)
    grad_query = grad_query.reshape(length, HEADS, HEAD_DIM)
    grad_q_rot = rotate_back(grad_query, cosine, sine_part).reshape(length, D)
    grad_k_rot = rotate_back(grad_key_all, cosine, sine_part).reshape(length, D)
    grad_joint = to_half(jnp.concatenate([grad_q_rot, grad_k_rot, grad_value_all.reshape(length, D)], axis=-1))
    grad_qkv = jnp.dot(input_one.T, grad_joint, preferred_element_type=jnp.float32)
    grad_normed_one = jnp.dot(grad_joint, w_qkv.T, preferred_element_type=jnp.float32)
    grad_g1 = lax.optimization_barrier(jnp.sum(grad_normed_one * normed_one, axis=0))
    grad_input = grad_resid + norm_back(grad_normed_one * gain_one.astype(jnp.float32), normed_one, inv_one)
    return (output, grad_input, (grad_g1, grad_qkv, grad_attn_w, grad_g2, grad_in, grad_ffn))

def reference(inputs, gain_one, w_qkv, w_attn, gain_two, w_in, w_ffn, cotangent):

    def step(state_in, pair):
        output, grad_input, grads = sequence_pass(pair[0], pair[1], gain_one, w_qkv, w_attn, gain_two, w_in, w_ffn)
        return (tuple((before + added for before, added in zip(state_in, grads))), (output, grad_input))
    zeros_all = (jnp.zeros((D,), jnp.float32), jnp.zeros((D, 3 * D), jnp.float32), jnp.zeros((D, D), jnp.float32), jnp.zeros((D,), jnp.float32), jnp.zeros((D, 2 * FF), jnp.float32), jnp.zeros((FF, D), jnp.float32))
    grads, (outputs, grad_inputs) = lax.scan(step, zeros_all, (inputs, cotangent))
    return (outputs, grad_inputs, grads[0], grads[1], grads[2], grads[3], grads[4], grads[5])
```

```python
import math

import jax
import jax.numpy as jnp
import numpy as np
from jax import lax
from jax.experimental import pallas as pl
from jax.experimental.pallas import tpu as pltpu
from jax.sharding import PartitionSpec as P

D = 1024
HEADS = 16
HEAD_DIM = 64
FF = 2624


EPSILON = 1e-05
ROPE_THETA = 160000.0


def norm_parts(values_in):
    mean_val = jnp.mean(values_in, axis=-1, keepdims=True)
    centred = values_in - mean_val
    variance = jnp.mean(centred * centred, axis=-1, keepdims=True)
    inv_std = lax.rsqrt(variance + EPSILON)
    return (centred * inv_std, inv_std)


def norm_back(grad_normed, normed, inv_std):
    return inv_std * (
        grad_normed
        - jnp.mean(grad_normed, axis=-1, keepdims=True)
        - normed * jnp.mean(grad_normed * normed, axis=-1, keepdims=True)
    )


def rotary_tables(positions):
    half_dim = HEAD_DIM // 2
    inv_freq = ROPE_THETA ** (-(jnp.arange(half_dim, dtype=jnp.float32) * 2.0) / HEAD_DIM)
    angles = positions.astype(jnp.float32)[:, None] * inv_freq[None, :]
    cosine = jnp.concatenate([jnp.cos(angles), jnp.cos(angles)], axis=-1)[:, None, :]
    sine_part = jnp.concatenate([jnp.sin(angles), jnp.sin(angles)], axis=-1)[:, None, :]
    return (cosine, sine_part)


def rotate(values_in, cosine, sine_part):
    half_dim = values_in.shape[-1] // 2
    turned = jnp.concatenate([-values_in[..., half_dim:], values_in[..., :half_dim]], axis=-1)
    return values_in * cosine + turned * sine_part


def rotate_back(grads, cosine, sine_part):
    half_dim = grads.shape[-1] // 2
    scaled = grads * sine_part
    turned = jnp.concatenate([scaled[..., half_dim:], -scaled[..., :half_dim]], axis=-1)
    return grads * cosine + turned


def gelu_slope(inner_part):
    cumulative = 0.5 * (1.0 + jax.scipy.special.erf(inner_part * 0.7071067811865476))
    density = jnp.exp(-0.5 * inner_part * inner_part) * 0.3989422804014327
    return cumulative + inner_part * density


def attend_piece(state_in, queries, key_piece, value_piece, scale_factor):
    row_max, row_sum, weighted = state_in
    scores = (
        jnp.einsum("bthd,bshd->bths", queries, key_piece, preferred_element_type=jnp.float32)
        * scale_factor
    )
    new_max = jnp.maximum(row_max, jnp.max(scores, axis=-1))
    rescale = jnp.exp(row_max - new_max)
    exp_vals = jnp.exp(scores - new_max[..., None])
    row_sum = row_sum * rescale + jnp.sum(exp_vals, axis=-1)
    weighted = weighted * rescale[..., None] + jnp.einsum(
        "bths,bshd->bthd",
        exp_vals.astype(jnp.bfloat16),
        value_piece,
        preferred_element_type=jnp.float32,
    )
    return (new_max, row_sum, weighted)


def back_piece(queries, grad_mixed, log_sum, row_delta, key_piece, value_piece, scale_factor):
    scores = (
        jnp.einsum("bthd,bshd->bths", queries, key_piece, preferred_element_type=jnp.float32)
        * scale_factor
    )
    probs = jnp.exp(scores - log_sum[..., None])
    grad_values = jnp.einsum(
        "bths,bthd->bshd",
        probs.astype(jnp.bfloat16),
        grad_mixed,
        preferred_element_type=jnp.float32,
    )
    grad_probs = jnp.einsum(
        "bthd,bshd->bths", grad_mixed, value_piece, preferred_element_type=jnp.float32
    )
    grad_scores = (probs * (grad_probs - row_delta[..., None])).astype(jnp.bfloat16)
    grad_query = (
        jnp.einsum("bths,bshd->bthd", grad_scores, key_piece, preferred_element_type=jnp.float32)
        * scale_factor
    )
    grad_keys = (
        jnp.einsum("bths,bthd->bshd", grad_scores, queries, preferred_element_type=jnp.float32)
        * scale_factor
    )
    return (grad_query, grad_keys, grad_values)


def add_at(whole_grads, piece_grads, offset):
    old_part = lax.dynamic_slice_in_dim(whole_grads, offset, piece_grads.shape[1], 1)
    return lax.dynamic_update_slice_in_dim(whole_grads, old_part + piece_grads, offset, 1)


def on_device(inputs, gain_one, w_qkv, w_attn, gain_two, w_in, w_ffn, cotangent):
    seq_dev = inputs.shape[0]
    tok_seq = inputs.shape[1]
    row_count = seq_dev * tok_seq
    seq_len = tok_seq * lax.axis_size("ctx")
    tokens_f = inputs.reshape(row_count, D).astype(jnp.float32)
    grad_out = cotangent.reshape(row_count, D)
    scale_factor = HEAD_DIM ** (-0.5)
    block_len = math.gcd(seq_len, 512)
    blocks_num = seq_len // block_len
    gathered = (
        lax.all_gather(gain_one, "fsdp", axis=0, tiled=True),
        lax.all_gather(w_qkv, "fsdp", axis=0, tiled=True),
        lax.all_gather(w_attn, "fsdp", axis=0, tiled=True),
        lax.all_gather(gain_two, "fsdp", axis=0, tiled=True),
        lax.all_gather(w_in, "fsdp", axis=0, tiled=True),
        lax.all_gather(w_ffn, "fsdp", axis=0, tiled=True),
    )
    full_g1, full_qkv, full_attn, full_g2, full_in, full_ffn = gathered
    normed_one, inv_one = norm_parts(tokens_f)
    input_one = (normed_one * full_g1.astype(jnp.float32)).astype(jnp.bfloat16)
    project = jnp.dot(input_one, full_qkv, preferred_element_type=jnp.float32)
    positions = lax.axis_index("ctx") * tok_seq + jnp.arange(tok_seq, dtype=jnp.int32)
    cosine, sine_part = rotary_tables(positions)
    shaped = project.reshape(seq_dev, tok_seq, 3, HEADS, HEAD_DIM)
    queries = rotate(shaped[:, :, 0], cosine, sine_part).astype(jnp.bfloat16)
    key_rows = rotate(shaped[:, :, 1], cosine, sine_part).astype(jnp.bfloat16)
    value_rows = shaped[:, :, 2].astype(jnp.bfloat16)
    start_state = (
        jnp.full((seq_dev, tok_seq, HEADS), -jnp.inf, jnp.float32),
        jnp.zeros((seq_dev, tok_seq, HEADS), jnp.float32),
        jnp.zeros((seq_dev, tok_seq, HEADS, HEAD_DIM), jnp.float32),
    )
    whole_keys, whole_values = (
        lax.all_gather(key_rows, "ctx", axis=1, tiled=True),
        lax.all_gather(value_rows, "ctx", axis=1, tiled=True),
    )

    def forward_step(state_in, block_index):
        begin = block_index * block_len
        key_piece = lax.dynamic_slice_in_dim(whole_keys, begin, block_len, 1)
        value_piece = lax.dynamic_slice_in_dim(whole_values, begin, block_len, 1)
        return (attend_piece(state_in, queries, key_piece, value_piece, scale_factor), None)

    state_out, unused = lax.scan(forward_step, start_state, jnp.arange(blocks_num, dtype=jnp.int32))
    row_max, row_sum, weighted = state_out
    attn_f = weighted / row_sum[..., None]
    log_sum = row_max + jnp.log(row_sum)
    attn_b = attn_f.reshape(row_count, D).astype(jnp.bfloat16)
    resid = tokens_f + jnp.dot(attn_b, full_attn, preferred_element_type=jnp.float32)
    normed_two, inv_two = norm_parts(resid)
    input_two = (normed_two * full_g2.astype(jnp.float32)).astype(jnp.bfloat16)
    widened = jnp.dot(input_two, full_in, preferred_element_type=jnp.float32)
    inner_part = widened[:, :FF]
    gating = widened[:, FF:]
    activated = jax.nn.gelu(inner_part, approximate=False)
    hidden = (activated * gating).astype(jnp.bfloat16)
    output = (resid + jnp.dot(hidden, full_ffn, preferred_element_type=jnp.float32)).astype(
        jnp.bfloat16
    )
    back_g1, back_qkv, back_attn, back_g2, back_in, back_ffn = gathered
    grad_ffn = jnp.dot(hidden.T, grad_out, preferred_element_type=jnp.float32)
    grad_hidden = jnp.dot(grad_out, back_ffn.T, preferred_element_type=jnp.float32)
    grad_inner = grad_hidden * gating * gelu_slope(inner_part)
    grad_gating = grad_hidden * activated
    grad_wide = jnp.concatenate([grad_inner, grad_gating], axis=-1).astype(jnp.bfloat16)
    grad_in = jnp.dot(input_two.T, grad_wide, preferred_element_type=jnp.float32)
    grad_normed_two = jnp.dot(grad_wide, back_in.T, preferred_element_type=jnp.float32)
    grad_g2 = jnp.sum(grad_normed_two * normed_two, axis=0)
    grad_resid = grad_out.astype(jnp.float32) + norm_back(
        grad_normed_two * back_g2.astype(jnp.float32), normed_two, inv_two
    )
    part_g2, part_in, part_ffn = (
        lax.psum_scatter(
            grad_g2.astype(jnp.bfloat16), "fsdp", scatter_dimension=0, tiled=True
        ).astype(jnp.float32),
        lax.psum_scatter(
            grad_in.astype(jnp.bfloat16), "fsdp", scatter_dimension=0, tiled=True
        ).astype(jnp.float32),
        lax.psum_scatter(
            grad_ffn.astype(jnp.bfloat16), "fsdp", scatter_dimension=0, tiled=True
        ).astype(jnp.float32),
    )
    resid_b = grad_resid.astype(jnp.bfloat16)
    grad_attn_w = jnp.dot(attn_b.T, resid_b, preferred_element_type=jnp.float32)
    grad_mixed = (
        jnp.dot(resid_b, back_attn.T, preferred_element_type=jnp.float32)
        .astype(jnp.bfloat16)
        .reshape(seq_dev, tok_seq, HEADS, HEAD_DIM)
    )
    row_delta = jnp.sum(grad_mixed.astype(jnp.float32) * attn_f, axis=-1)
    zero_q = jnp.zeros((seq_dev, tok_seq, HEADS, HEAD_DIM), jnp.float32)
    zero_kv = jnp.zeros((seq_dev, seq_len, HEADS, HEAD_DIM), jnp.float32)

    def backward_step(state_in, block_index):
        grad_q_sum, grad_key_all, grad_value_all = state_in
        begin = block_index * block_len
        key_piece = lax.dynamic_slice_in_dim(whole_keys, begin, block_len, 1)
        value_piece = lax.dynamic_slice_in_dim(whole_values, begin, block_len, 1)
        grad_query, grad_keys, grad_values = back_piece(
            queries, grad_mixed, log_sum, row_delta, key_piece, value_piece, scale_factor
        )
        return (
            (
                grad_q_sum + grad_query,
                add_at(grad_key_all, grad_keys, begin),
                add_at(grad_value_all, grad_values, begin),
            ),
            None,
        )

    back_state, unused_back = lax.scan(
        backward_step, (zero_q, zero_kv, zero_kv), jnp.arange(blocks_num, dtype=jnp.int32)
    )
    grad_q_sum, grad_key_all, grad_value_all = back_state
    own_keys, own_values = (
        lax.psum_scatter(
            grad_key_all.astype(jnp.bfloat16), "ctx", scatter_dimension=1, tiled=True
        ).astype(jnp.float32),
        lax.psum_scatter(
            grad_value_all.astype(jnp.bfloat16), "ctx", scatter_dimension=1, tiled=True
        ).astype(jnp.float32),
    )
    grad_q_rot = rotate_back(grad_q_sum, cosine, sine_part).reshape(row_count, D)
    grad_k_rot = rotate_back(own_keys, cosine, sine_part).reshape(row_count, D)
    grad_joint = jnp.concatenate(
        [grad_q_rot, grad_k_rot, own_values.reshape(row_count, D)], axis=-1
    ).astype(jnp.bfloat16)
    grad_qkv = jnp.dot(input_one.T, grad_joint, preferred_element_type=jnp.float32)
    grad_normed_one = jnp.dot(grad_joint, back_qkv.T, preferred_element_type=jnp.float32)
    grad_g1 = jnp.sum(grad_normed_one * normed_one, axis=0)
    grad_input = grad_resid + norm_back(
        grad_normed_one * back_g1.astype(jnp.float32), normed_one, inv_one
    )
    part_g1, part_qkv, part_attn = (
        lax.psum_scatter(
            grad_g1.astype(jnp.bfloat16), "fsdp", scatter_dimension=0, tiled=True
        ).astype(jnp.float32),
        lax.psum_scatter(
            grad_qkv.astype(jnp.bfloat16), "fsdp", scatter_dimension=0, tiled=True
        ).astype(jnp.float32),
        lax.psum_scatter(
            grad_attn_w.astype(jnp.bfloat16), "fsdp", scatter_dimension=0, tiled=True
        ).astype(jnp.float32),
    )
    totals = (
        lax.psum(part_g1.astype(jnp.bfloat16), "ctx").astype(jnp.float32),
        lax.psum(part_qkv.astype(jnp.bfloat16), "ctx").astype(jnp.float32),
        lax.psum(part_attn.astype(jnp.bfloat16), "ctx").astype(jnp.float32),
        lax.psum(part_g2.astype(jnp.bfloat16), "ctx").astype(jnp.float32),
        lax.psum(part_in.astype(jnp.bfloat16), "ctx").astype(jnp.float32),
        lax.psum(part_ffn.astype(jnp.bfloat16), "ctx").astype(jnp.float32),
    )
    return (
        output.reshape(seq_dev, tok_seq, D),
        grad_input.reshape(seq_dev, tok_seq, D),
        totals[0],
        totals[1],
        totals[2],
        totals[3],
        totals[4],
        totals[5],
    )


RING = 8
OWNERS = 4
HALF = RING // 2
PAIR = 2 * HEAD_DIM
UNITS = FF // RING
UNITS_PAD = 384
MESH = pl.DeviceIdType.MESH
VMEM_BYTES = 56 * 1024 * 1024
F32 = jnp.float32
BF16 = jnp.bfloat16


def contract(left, right, left_dim, right_dim):
    return lax.dot_general(
        left, right, (((left_dim,), (right_dim,)), ((), ())), preferred_element_type=F32
    )


def ring_place(block):
    z, x = block // 2, block % 2
    return z + x * (RING - 1 - 2 * z)


def ring_at(place, shift):
    p = (place + shift + RING) % RING
    late = p // HALF
    return late * (2 * (RING - 1 - p) + 1) + (1 - late) * 2 * p


class RingGather:
    def __init__(self, buf, send, recv, block, own):
        self.buf, self.send_sem, self.recv_sem = buf, send, recv
        self.place, self.own = ring_place(block), own
        self.rows = buf.shape[1]

    def copy(self, way, step, back, half=False):
        sign = 1 - 2 * way
        ref = self.buf.at[ring_at(self.place, -sign * (step - back))]
        if half:
            ref = ref.at[pl.ds(way * (self.rows // 2), self.rows // 2)]
        return pltpu.make_async_remote_copy(
            src_ref=ref,
            dst_ref=ref,
            send_sem=self.send_sem.at[way, step - 1],
            recv_sem=self.recv_sem.at[way, step - 1],
            device_id=(ring_at(self.place, sign), self.own),
            device_id_type=MESH,
        )

    def send(self, step, half=False):
        for way in range(2):
            self.copy(way, step, 1, half).start()

    def arrive(self, step, half=False):
        for way in range(2):
            self.copy(way, step, 0, half).wait_recv()

    def relay(self, step):
        for way in range(2):
            self.copy(way, step, 0).wait_recv()
            self.copy(way, step + 1, 1, step == HALF - 1).start()

    def found(self, way, step):
        return ring_at(self.place, -(1 - 2 * way) * step)

    def sent(self):
        for step in range(1, HALF + 1):
            for way in range(2):
                self.copy(way, step, 1, step == HALF).wait_send()


class RingScatter:
    def __init__(self, terms, out, inn, send, recv, block, own):
        self.terms, self.out, self.inn = terms, out, inn
        self.send_sem, self.recv_sem = send, recv
        self.block, self.place, self.own = block, ring_place(block), own
        self.rows = out.shape[2]

    def copy(self, way, step):
        src, dst = self.out.at[way, step], self.inn.at[way, step]
        if step == 0:
            src = src.at[pl.ds(0, self.rows // 2)]
            dst = dst.at[pl.ds(0, self.rows // 2)]
        return pltpu.make_async_remote_copy(
            src_ref=src,
            dst_ref=dst,
            send_sem=self.send_sem.at[way, step],
            recv_sem=self.recv_sem.at[way, step],
            device_id=(ring_at(self.place, 1 - 2 * way), self.own),
            device_id_type=MESH,
        )

    def begin(self):
        half = self.rows // 2
        for way in range(2):
            rows = pl.ds(way * half, half)
            term = self.terms[ring_at(self.place, HALF), rows, :]
            self.out[way, 0, pl.ds(0, half), :] = term.astype(BF16)
            self.copy(way, 0).start()

    def step(self, step):
        half = self.rows // 2
        for way in range(2):
            target = ring_at(self.place, (1 - 2 * way) * (HALF - step))
            self.copy(way, step - 1).wait_recv()
            if step == 1:
                rows = pl.ds(way * half, half)
                other = pl.ds((1 - way) * half, half)
                came = self.inn[way, 0, pl.ds(0, half), :].astype(F32)
                term = self.terms[target, rows, :].astype(F32)
                self.out[way, 1, rows, :] = (came + term).astype(BF16)
                self.out[way, 1, other, :] = self.terms[target, other, :].astype(BF16)
            else:
                came = self.inn[way, step - 1].astype(F32)
                term = self.terms[target].astype(F32)
                self.out[way, step] = (came + term).astype(BF16)
            self.copy(way, step).start()

    def finish(self):
        for way in range(2):
            self.copy(way, HALF - 1).wait_recv()
        total = self.terms[self.block].astype(F32) + (
            self.inn[0, HALF - 1].astype(F32) + self.inn[1, HALF - 1].astype(F32)
        )
        for step in range(HALF):
            for way in range(2):
                self.copy(way, step).wait_send()
        return total


def core_of(own):
    return own + 1 - 2 * (own % 2)


def far_of(own):
    return (own + 2) % OWNERS


def push(src, dst, send, recv, block, own):
    return pltpu.make_async_remote_copy(
        src_ref=src,
        dst_ref=dst,
        send_sem=send,
        recv_sem=recv,
        device_id=(block, own),
        device_id_type=MESH,
    )


def greet(block, own, all_blocks):
    barrier = pltpu.get_barrier_semaphore()
    place = ring_place(block)
    shifts = range(1, RING) if all_blocks else (1, RING - 1)
    for shift in shifts:
        pl.semaphore_signal(
            barrier, inc=1, device_id=(ring_at(place, shift), own), device_id_type=MESH
        )
    for other in (core_of(own), far_of(own)):
        pl.semaphore_signal(barrier, inc=1, device_id=(block, other), device_id_type=MESH)
    pl.semaphore_wait(barrier, len(shifts) + 2)


def row_norm(rows):
    mean = jnp.mean(rows, axis=-1, keepdims=True)
    centred = rows - mean
    inv = lax.rsqrt(jnp.mean(centred * centred, axis=-1, keepdims=True) + EPSILON)
    return centred * inv, inv


def first_half():
    lane = lax.broadcasted_iota(jnp.int32, (1, PAIR), 1)
    return lane % HEAD_DIM < HEAD_DIM // 2


def first_head():
    return lax.broadcasted_iota(jnp.int32, (1, PAIR), 1) < HEAD_DIM


def swap_halves(rows):
    up = pltpu.roll(rows, PAIR - HEAD_DIM // 2, 1)
    down = pltpu.roll(rows, HEAD_DIM // 2, 1)
    return jnp.where(first_half(), up, down)


def only(rows, head):
    keep = first_head() if head == 0 else jnp.logical_not(first_head())
    return jnp.where(keep, rows, jnp.zeros_like(rows))


def front_kernel(
    x_ref, cot_ref, gain_ref, qkv_ref, attn_ref, in_ref, ffn_ref, cos_ref, sin_ref,
    q_o, k_o, v_o, of_o, lse_o, a1_o, gain_o, qkv_o, attn_o, in_o, ffn_o, cot_o, ob_o, own_o,
    xs, proj, x_send, x_recv, c_send, c_recv, w_send, w_recv, f_send, f_recv, a_send, a_recv,
):
    block, own = lax.axis_index("ctx"), lax.axis_index("fsdp")
    core, far = core_of(own), far_of(own)
    place = ring_place(block)
    greet(block, own, True)

    xs[block] = x_ref[...]
    x_ring = RingGather(xs, x_send, x_recv, block, own)
    x_ring.send(1)

    parts = ((gain_ref, gain_o), (qkv_ref, qkv_o), (attn_ref, attn_o), (in_ref, in_o))

    def part_of(i, owner):
        if i == 0:
            return gain_o.at[:, pl.ds(pl.multiple_of(owner * 256, 256), 256)]
        rows = parts[i][0].shape[0]
        return parts[i][1].at[pl.ds(pl.multiple_of(owner * rows, rows), rows)]

    def to_core(i):
        return push(parts[i][0], part_of(i, own), w_send.at[i, 0], w_recv.at[i, 0], block, core)

    def to_far(i):
        return push(parts[i][0], part_of(i, own), w_send.at[i, 1], w_recv.at[i, 1], block, far)

    def pass_on(i):
        ref = part_of(i, far)
        return push(ref, ref, w_send.at[i, 2], w_recv.at[i, 2], block, core)

    def arrived(i, kind, owner):
        ref = part_of(i, owner)
        push(ref, ref, w_send.at[i, kind], w_recv.at[i, kind], block, core).wait_recv()

    def begin_part(i):
        to_far(i).start()
        to_core(i).start()

    def relay_part(i):
        arrived(i, 1, far)
        pass_on(i).start()

    def end_part(i):
        arrived(i, 0, core)
        arrived(i, 2, far_of(core))
        to_core(i).wait_send()
        to_far(i).wait_send()
        pass_on(i).wait_send()

    begin_part(0)
    begin_part(1)
    for i in range(2, 4):
        begin_part(i)
    gain_o[:, pl.ds(pl.multiple_of(own * 256, 256), 256)] = gain_ref[...]
    for i in range(1, 4):
        rows = parts[i][0].shape[0]
        parts[i][1][pl.ds(pl.multiple_of(own * rows, rows), rows), :] = parts[i][0][...]

    holder = block // 2

    def ffn_to(src, kind, to_own):
        return push(src, ffn_o, f_send.at[kind], f_recv.at[kind], block, to_own)

    @pl.when(own == holder)
    def _():
        ffn_to(ffn_ref, 1, far).start()
        ffn_to(ffn_ref, 0, core).start()
        ffn_o[...] = ffn_ref[...]

    relay_part(0)
    relay_part(1)
    end_part(0)
    end_part(1)

    def project(index):
        normed, _ = row_norm(xs[index].astype(F32))
        a1 = (normed * gain_o[0:1, :]).astype(BF16)
        a1_o[index] = a1
        proj[index] = contract(a1, qkv_o[...], 1, 0)

    project(block)

    def hop(step, carry):
        x_ring.relay(step)
        project(x_ring.found(0, step))
        project(x_ring.found(1, step))
        return carry

    x_ring.relay(1)
    cot_o[block] = cot_ref[...]
    project(x_ring.found(0, 1))
    project(x_ring.found(1, 1))
    relay_part(2)
    x_ring.relay(2)
    project(x_ring.found(0, 2))
    project(x_ring.found(1, 2))
    x_ring.relay(3)
    project(x_ring.found(0, 3))
    project(x_ring.found(1, 3))
    relay_part(3)
    x_ring.arrive(HALF, True)
    c_ring = RingGather(cot_o, c_send, c_recv, block, own)
    c_ring.send(1)
    project(x_ring.found(0, HALF))

    @pl.when(far == holder)
    def _():
        ffn_to(ffn_o, 1, far).wait_recv()
        ffn_to(ffn_o, 2, core).start()

    seqs, tok = 2, xs.shape[1] // 2
    length = tok * RING
    scale = HEAD_DIM ** (-0.5)
    done = 1
    for s in range(seqs):
        rows = slice(s * tok, (s + 1) * tok)

        def columns(i):
            return proj[:, rows, i * PAIR : (i + 1) * PAIR].reshape(length, PAIR)

        cos, sin = cos_ref[...], sin_ref[...]
        query, key = columns(0), columns(1)
        q = (query * cos + swap_halves(query) * sin).astype(BF16)
        k = (key * cos + swap_halves(key) * sin).astype(BF16)
        v = columns(2).astype(BF16)
        q_o[s] = q
        k_o[s] = k
        v_o[s] = v
        outs, lses = [], []
        for head in range(2):
            scores = contract(only(q, head), k, 1, 1) * scale
            top = jnp.max(scores, axis=-1, keepdims=True)
            e = jnp.exp(scores - top)
            total = jnp.sum(e, axis=-1, keepdims=True)
            outs.append(contract(e.astype(BF16), v, 1, 0) / total)
            lses.append(top + jnp.log(total))
            if done < HALF:
                c_ring.relay(done)
            done += 1
        of = jnp.where(first_head(), outs[0], outs[1])
        of_o[s] = of
        lse_o[s] = jnp.where(first_head(), lses[0], lses[1])
        ob_o[:, rows, :] = of.astype(BF16).reshape(RING, tok, PAIR)

    def exchange(shift):
        return push(
            ob_o.at[ring_at(place, shift)], own_o.at[block],
            a_send.at[shift - 1], a_recv.at[shift - 1], ring_at(place, shift), own,
        )

    for shift in range(1, RING):
        exchange(shift).start()
    own_o[block] = ob_o[block]
    c_ring.arrive(HALF, True)
    end_part(2)
    end_part(3)

    @pl.when(own == holder)
    def _():
        ffn_to(ffn_ref, 0, core).wait_send()
        ffn_to(ffn_ref, 1, far).wait_send()

    @pl.when(far == holder)
    def _():
        ffn_to(ffn_o, 2, core).wait_send()

    @pl.when(core == holder)
    def _():
        ffn_to(ffn_o, 0, core).wait_recv()

    @pl.when(far_of(core) == holder)
    def _():
        ffn_to(ffn_o, 2, core).wait_recv()

    for shift in range(1, RING):
        source = own_o.at[ring_at(place, -shift)]
        push(
            source, source, a_send.at[shift - 1], a_recv.at[shift - 1], ring_at(place, shift), own
        ).wait_recv()
        exchange(shift).wait_send()
    x_ring.sent()
    c_ring.sent()


class OwnerSum:
    def __init__(self, g, from_core, to_far, from_far, send, recv, block, own):
        self.g, self.from_core, self.to_far, self.from_far = g, from_core, to_far, from_far
        self.send_sem, self.recv_sem = send, recv
        self.block, self.own = block, own

    def core_copy(self):
        return push(
            self.g.at[1 - self.own % 2], self.from_core,
            self.send_sem.at[0], self.recv_sem.at[0], self.block, core_of(self.own),
        )

    def far_copy(self):
        return push(
            self.to_far, self.from_far,
            self.send_sem.at[1], self.recv_sem.at[1], self.block, far_of(self.own),
        )

    def begin(self):
        self.core_copy().start()

    def middle(self):
        self.core_copy().wait_recv()
        y = 1 - self.own // 2
        self.to_far[...] = (
            self.g[self.own % 2, y].astype(F32) + self.from_core[y].astype(F32)
        ).astype(BF16)
        self.far_copy().start()

    def finish(self):
        y = self.own // 2
        near = self.g[self.own % 2, y].astype(F32) + self.from_core[y].astype(F32)
        self.far_copy().wait_recv()
        total = (near + self.from_far[...].astype(F32)).astype(BF16)
        self.core_copy().wait_send()
        self.far_copy().wait_send()
        return total


UNIT_ROWS = 336
FFN_ROWS = 1024
ATTN_ROWS = 512


def quarter(ref, j):
    tile = ref[:, :, j * 256 : (j + 1) * 256]
    return tile.reshape(tile.shape[0] * tile.shape[1], 256)


def flat(ref):
    rows = ref[...]
    return rows.reshape(rows.shape[0] * rows.shape[1], rows.shape[2])


def middle_kernel(
    x_ref, own_ref, attn_ref, gain_ref, in_ref, ffn_ref, cot_ref,
    resid_o, grad_o, all_o, mixed_o, outp_o, total_o,
    a2s, fs, dus, n2s, terms, s_out, s_in, g, g_core, g_to, g_from,
    a_send, a_recv, s_send, s_recv, r_send, r_recv, g_send, g_recv,
):
    block, own = lax.axis_index("ctx"), lax.axis_index("fsdp")
    greet(block, own, False)
    g2 = gain_ref[1:2, :]

    mixed_heads = jnp.concatenate([own_ref[d] for d in range(RING)], axis=1)
    resid = x_ref[...].astype(F32) + contract(mixed_heads, attn_ref[...], 1, 0)
    resid_o[...] = resid
    normed, inv_two = row_norm(resid)
    n2s[...] = normed
    a2s[block] = (normed * g2).astype(BF16)
    ring = RingGather(a2s, a_send, a_recv, block, own)
    ring.send(1)

    def feed(index):
        widened = contract(a2s[index], in_ref[...], 1, 0)
        inner, gating = widened[:, :UNITS_PAD], widened[:, UNITS_PAD:]
        below = 0.5 * (1.0 + lax.erf(inner * 0.7071067811865476))
        density = jnp.exp(-0.5 * inner * inner) * 0.3989422804014327
        active = inner * below
        fs[index] = (active * gating).astype(BF16)
        grad_hidden = contract(cot_ref[index], ffn_ref[...], 1, 1)
        du = jnp.concatenate(
            [grad_hidden * gating * (below + inner * density), grad_hidden * active], axis=1
        ).astype(BF16)
        dus[index] = du
        terms[index] = contract(du, in_ref[...], 1, 1)

    feed(block)
    for step in range(1, HALF):
        ring.relay(step)
        feed(ring.found(0, step))
        feed(ring.found(1, step))
    ring.arrive(HALF, True)
    feed(ring.found(0, HALF))

    summed = RingScatter(terms, s_out, s_in, s_send, s_recv, block, own)
    summed.begin()
    owners = OwnerSum(g, g_core, g_to, g_from, g_send, g_recv, block, own)
    for j in range(OWNERS):
        c, y = j % 2, j // 2
        g[c, y, 0:UNIT_ROWS, :] = contract(flat(fs), quarter(cot_ref, j), 0, 0)[:UNIT_ROWS].astype(
            BF16
        )
        grad_in = contract(flat(dus), quarter(a2s, j), 0, 0).astype(BF16)
        g[c, y, UNIT_ROWS : 2 * UNIT_ROWS, :] = grad_in[:UNIT_ROWS]
        g[c, y, 2 * UNIT_ROWS : 3 * UNIT_ROWS, :] = grad_in[UNITS_PAD : UNITS_PAD + UNIT_ROWS]
        g[c, y, 3 * UNIT_ROWS :, :] = jnp.zeros((FFN_ROWS - 3 * UNIT_ROWS, 256), BF16)
        if j < HALF - 1:
            summed.step(j + 1)
    owners.begin()
    grad_two = summed.finish()

    b = grad_two * g2
    normed = n2s[...]
    own_grad = cot_ref[block].astype(F32) + inv_two * (
        b
        - jnp.mean(b, axis=-1, keepdims=True)
        - normed * jnp.mean(b * normed, axis=-1, keepdims=True)
    )
    grad_o[...] = own_grad
    all_o[block] = own_grad.astype(BF16)
    back = RingGather(all_o, r_send, r_recv, block, own)
    back.send(1)

    attn_c = attn_ref.at[pl.ds(pl.multiple_of(block * PAIR, PAIR), PAIR)]

    def mix(index):
        mixed_o[index] = contract(all_o[index], attn_c[...], 1, 1).astype(BF16)
        outp_o[index] = contract(fs[index], ffn_ref[...], 1, 0).astype(BF16)

    mix(block)
    owners.middle()
    for step in range(1, HALF):
        back.relay(step)
        mix(back.found(0, step))
        mix(back.found(1, step))
    total_o[...] = owners.finish()
    back.arrive(HALF, True)
    mix(back.found(0, HALF))
    ring.sent()
    back.sent()


def last_kernel(
    q_ref, k_ref, v_ref, of_ref, lse_ref, mixed_ref, cos_ref, sin_ref, a1_ref, qkv_ref, gain_ref,
    x_ref, grad_ref, resid_ref, outp_ref, all_ref, ob_ref, total_ref,
    out_o, gin_o, gff_o, gat_o,
    joint, terms, o_out, o_in, s_out, s_in, g, g_core, g_to, g_from,
    o_send, o_recv, s_send, s_recv, f_send, f_recv, t_send, t_recv, g_send, g_recv,
):
    block, own = lax.axis_index("ctx"), lax.axis_index("fsdp")
    greet(block, own, False)
    outs = RingScatter(outp_ref, o_out, o_in, o_send, o_recv, block, own)
    outs.begin()
    gff_o[block] = total_ref[...]
    f_ring = RingGather(gff_o, f_send, f_recv, block, own)

    seqs, length = q_ref.shape[0], q_ref.shape[1]
    tok = length // RING
    scale = HEAD_DIM ** (-0.5)
    done = 1
    for s in range(seqs):
        rows = slice(s * tok, (s + 1) * tok)
        q, k, v = q_ref[s], k_ref[s], v_ref[s]
        do = mixed_ref[:, rows, :].reshape(length, PAIR)
        weighed = do.astype(F32) * of_ref[s]
        dqs, dks, dvs = [], [], []
        for head in range(2):
            delta = jnp.sum(only(weighed, head), axis=-1, keepdims=True)
            lse = lse_ref[s, :, head * HEAD_DIM : head * HEAD_DIM + 1]
            probs = jnp.exp(contract(only(q, head), k, 1, 1) * scale - lse)
            dvs.append(contract(probs.astype(BF16), do, 0, 0))
            grad_probs = contract(only(do, head), v, 1, 1)
            ds = (probs * (grad_probs - delta)).astype(BF16)
            dqs.append(contract(ds, k, 1, 0) * scale)
            dks.append(contract(ds, q, 0, 0) * scale)
            if done < HALF:
                outs.step(done)
            done += 1
        cos, sin = cos_ref[...], sin_ref[...]
        dq = jnp.where(first_head(), dqs[0], dqs[1])
        dk = jnp.where(first_head(), dks[0], dks[1])
        dv = jnp.where(first_head(), dvs[0], dvs[1])
        for i, part in enumerate(
            (dq * cos - swap_halves(dq) * sin, dk * cos - swap_halves(dk) * sin, dv)
        ):
            joint[:, rows, i * PAIR : (i + 1) * PAIR] = part.astype(BF16).reshape(RING, tok, PAIR)

    def term(i, carry):
        terms[i] = contract(joint[i], qkv_ref[...], 1, 1)
        return carry

    lax.fori_loop(0, RING, term, 0)
    ones = RingScatter(terms, s_out, s_in, s_send, s_recv, block, own)
    ones.begin()
    out_o[...] = (resid_ref[...] + outs.finish()).astype(BF16)
    f_ring.send(1)
    owners = OwnerSum(g, g_core, g_to, g_from, g_send, g_recv, block, own)
    for j in range(OWNERS):
        c, y = j % 2, j // 2
        g[c, y, 0 : 3 * PAIR, :] = contract(flat(joint), quarter(a1_ref, j), 0, 0).astype(BF16)
        g[c, y, 3 * PAIR :, :] = contract(flat(ob_ref), quarter(all_ref, j), 0, 0).astype(BF16)
        if j < HALF - 1:
            ones.step(j + 1)
    owners.begin()
    owners.middle()
    f_ring.relay(1)
    gat_o[block] = owners.finish()
    t_ring = RingGather(gat_o, t_send, t_recv, block, own)
    t_ring.send(1)
    normed, inv_one = row_norm(x_ref[...].astype(F32))
    b = ones.finish() * gain_ref[0:1, :]
    gin_o[...] = grad_ref[...] + inv_one * (
        b
        - jnp.mean(b, axis=-1, keepdims=True)
        - normed * jnp.mean(b * normed, axis=-1, keepdims=True)
    )
    f_ring.relay(2)
    t_ring.relay(1)
    f_ring.relay(3)
    t_ring.relay(2)
    t_ring.relay(3)
    f_ring.arrive(HALF, True)
    t_ring.arrive(HALF, True)
    f_ring.sent()
    t_ring.sent()


def rotary_rows(length):
    half = HEAD_DIM // 2
    freq = (np.float32(ROPE_THETA) ** (-(np.arange(half, dtype=np.float32) * 2.0) / HEAD_DIM)).astype(
        np.float32
    )
    angles = np.arange(length, dtype=np.float32)[:, None] * freq[None, :]
    cos, sin = np.cos(angles), np.sin(angles)
    return np.tile(cos, (1, 4)), np.tile(np.concatenate([-sin, sin], axis=1), (1, 2))


def run(body, ident, outs, scratch, *args):
    vmem = pl.BlockSpec(memory_space=pltpu.VMEM)
    return pl.pallas_call(
        body,
        out_shape=[jax.ShapeDtypeStruct(shape, dtype) for shape, dtype in outs],
        in_specs=[vmem] * len(args),
        out_specs=[vmem] * len(outs),
        scratch_shapes=scratch,
        compiler_params=pltpu.CompilerParams(
            collective_id=ident, has_side_effects=True, vmem_limit_bytes=VMEM_BYTES
        ),
    )(*args)


def by_rings(inputs, gain_one, w_qkv, w_attn, gain_two, w_in, w_ffn, cotangent):
    block = lax.axis_index("ctx")
    seqs, tok, _ = inputs.shape
    rows = seqs * tok
    length = tok * RING
    part = w_qkv.shape[0]
    sem = pltpu.SemaphoreType.DMA
    vmem = pltpu.VMEM
    ring_sems = [sem((2, HALF)), sem((2, HALF))]
    whole = (RING, rows, D)

    x = inputs.reshape(rows, D)
    cot = cotangent.reshape(rows, D)
    qkv_part = lax.dynamic_slice_in_dim(w_qkv.reshape(part, 3, D), block * PAIR, PAIR, 2)
    qkv_part = qkv_part.reshape(part, 3 * PAIR)
    in_part = jnp.concatenate(
        [
            jnp.pad(
                lax.dynamic_slice_in_dim(w_in, start + block * UNITS, UNITS, 1),
                ((0, 0), (0, UNITS_PAD - UNITS)),
            )
            for start in (0, FF)
        ],
        axis=1,
    )
    ffn_part = jnp.pad(
        lax.dynamic_slice_in_dim(w_ffn, block % 2 * UNITS, UNITS, 0),
        ((0, UNITS_PAD - UNITS), (0, 0)),
    )
    gains = jnp.pad(jnp.stack([gain_one, gain_two]).astype(F32), ((0, 6), (0, 0)))
    cos, sin = (jnp.asarray(t, F32) for t in rotary_rows(length))

    front = run(
        front_kernel,
        0,
        [
            ((seqs, length, PAIR), BF16),
            ((seqs, length, PAIR), BF16),
            ((seqs, length, PAIR), BF16),
            ((seqs, length, PAIR), F32),
            ((seqs, length, PAIR), F32),
            (whole, BF16),
            ((8, D), F32),
            ((D, 3 * PAIR), BF16),
            ((D, D), BF16),
            ((D, 2 * UNITS_PAD), BF16),
            ((UNITS_PAD, D), BF16),
            (whole, BF16),
            ((RING, rows, PAIR), BF16),
            ((RING, rows, PAIR), BF16),
        ],
        [
            vmem(whole, BF16),
            vmem((RING, rows, 3 * PAIR), F32),
            *ring_sems,
            *ring_sems,
            sem((4, 3)),
            sem((4, 3)),
            sem((3,)),
            sem((3,)),
            sem((RING - 1,)),
            sem((RING - 1,)),
        ],
        x, cot, gains, qkv_part, w_attn, in_part, ffn_part, cos, sin,
    )
    q, k, v, of, lse, a1, gain_all, qkv_c, attn_all, in_c, ffn_c, all_cot, ob, own_heads = front

    def owner_scratch(height):
        return [
            vmem((2, 2, height, part), BF16),
            vmem((2, height, part), BF16),
            vmem((height, part), BF16),
            vmem((height, part), BF16),
        ]

    sums = [vmem((2, HALF, rows, D), BF16), vmem((2, HALF, rows, D), BF16)]
    resid, own_grad, all_resid, mixed, outp, total = run(
        middle_kernel,
        1,
        [
            ((rows, D), F32),
            ((rows, D), F32),
            (whole, BF16),
            ((RING, rows, PAIR), BF16),
            (whole, BF16),
            ((FFN_ROWS, part), BF16),
        ],
        [
            vmem(whole, BF16),
            vmem((RING, rows, UNITS_PAD), BF16),
            vmem((RING, rows, 2 * UNITS_PAD), BF16),
            vmem((rows, D), F32),
            vmem(whole, F32),
            *sums,
            *owner_scratch(FFN_ROWS),
            *ring_sems,
            *ring_sems,
            *ring_sems,
            sem((2,)),
            sem((2,)),
        ],
        x, own_heads, attn_all, gain_all, in_c, ffn_c, all_cot,
    )

    output, grad_input, gff, gat = run(
        last_kernel,
        2,
        [
            ((rows, D), BF16),
            ((rows, D), F32),
            ((RING, FFN_ROWS, part), BF16),
            ((RING, ATTN_ROWS, part), BF16),
        ],
        [
            vmem((RING, rows, 3 * PAIR), BF16),
            vmem(whole, F32),
            *sums,
            *sums,
            *owner_scratch(ATTN_ROWS),
            *ring_sems,
            *ring_sems,
            *ring_sems,
            *ring_sems,
            sem((2,)),
            sem((2,)),
        ],
        q, k, v, of, lse, mixed, cos, sin, a1, qkv_c, gain_all,
        x, own_grad, resid, outp, all_resid, ob, total,
    )

    grad_ffn = gff[:, :UNITS].reshape(FF, part)
    grad_in = jnp.stack(
        [gff[:, UNIT_ROWS : UNIT_ROWS + UNITS], gff[:, 2 * UNIT_ROWS : 2 * UNIT_ROWS + UNITS]]
    )
    grad_in = grad_in.reshape(2 * FF, part).T.astype(F32)
    grad_qkv = gat[:, : 3 * PAIR].reshape(RING, 3, PAIR, part).transpose(1, 0, 2, 3)
    grad_qkv = grad_qkv.reshape(3 * D, part).T.astype(F32)
    grad_attn = gat[:, 3 * PAIR :].reshape(D, part)
    grad_ffn = lax.all_to_all(grad_ffn, "fsdp", split_axis=0, concat_axis=1, tiled=True)
    grad_attn = lax.all_to_all(grad_attn, "fsdp", split_axis=0, concat_axis=1, tiled=True)
    grad_g1 = jnp.sum(w_qkv.astype(F32) * grad_qkv, axis=1) / gain_one.astype(F32)
    grad_g2 = jnp.sum(w_in.astype(F32) * grad_in, axis=1) / gain_two.astype(F32)
    return (
        output.reshape(seqs, tok, D),
        grad_input.reshape(seqs, tok, D),
        grad_g1,
        grad_qkv,
        grad_attn.astype(F32),
        grad_g2,
        grad_in,
        grad_ffn.astype(F32),
    )


def solution(mesh):
    split_ok = mesh.shape["ctx"] == RING and mesh.shape["fsdp"] == OWNERS

    return jax.shard_map(
        by_rings if split_ok else on_device,
        mesh=mesh,
        in_specs=(
            P("fsdp", "ctx", None),
            P("fsdp"),
            P("fsdp", None),
            P("fsdp", None),
            P("fsdp"),
            P("fsdp", None),
            P("fsdp", None),
            P("fsdp", "ctx", None),
        ),
        out_specs=(
            P("fsdp", "ctx", None),
            P("fsdp", "ctx", None),
            P("fsdp"),
            P("fsdp", None),
            P("fsdp", None),
            P("fsdp"),
            P("fsdp", None),
            P("fsdp", None),
        ),
        check_vma=False,
    )
```

```python
import math

import jax
import jax.numpy as jnp
import numpy as np
from jax import lax
from jax.experimental import pallas as pl
from jax.experimental.pallas import tpu as pltpu
from jax.sharding import PartitionSpec as P

D = 1024
HEADS = 16
HEAD_DIM = 64
FF = 2624


EPSILON = 1e-05
ROPE_THETA = 160000.0


def norm_parts(values_in):
    mean_val = jnp.mean(values_in, axis=-1, keepdims=True)
    centred = values_in - mean_val
    variance = jnp.mean(centred * centred, axis=-1, keepdims=True)
    inv_std = lax.rsqrt(variance + EPSILON)
    return (centred * inv_std, inv_std)


def norm_back(grad_normed, normed, inv_std):
    return inv_std * (
        grad_normed
        - jnp.mean(grad_normed, axis=-1, keepdims=True)
        - normed * jnp.mean(grad_normed * normed, axis=-1, keepdims=True)
    )


def rotary_tables(positions):
    half_dim = HEAD_DIM // 2
    inv_freq = ROPE_THETA ** (-(jnp.arange(half_dim, dtype=jnp.float32) * 2.0) / HEAD_DIM)
    angles = positions.astype(jnp.float32)[:, None] * inv_freq[None, :]
    cosine = jnp.concatenate([jnp.cos(angles), jnp.cos(angles)], axis=-1)[:, None, :]
    sine_part = jnp.concatenate([jnp.sin(angles), jnp.sin(angles)], axis=-1)[:, None, :]
    return (cosine, sine_part)


def rotate(values_in, cosine, sine_part):
    half_dim = values_in.shape[-1] // 2
    turned = jnp.concatenate([-values_in[..., half_dim:], values_in[..., :half_dim]], axis=-1)
    return values_in * cosine + turned * sine_part


def rotate_back(grads, cosine, sine_part):
    half_dim = grads.shape[-1] // 2
    scaled = grads * sine_part
    turned = jnp.concatenate([scaled[..., half_dim:], -scaled[..., :half_dim]], axis=-1)
    return grads * cosine + turned


def gelu_slope(inner_part):
    cumulative = 0.5 * (1.0 + jax.scipy.special.erf(inner_part * 0.7071067811865476))
    density = jnp.exp(-0.5 * inner_part * inner_part) * 0.3989422804014327
    return cumulative + inner_part * density


def attend_piece(state_in, queries, key_piece, value_piece, scale_factor):
    row_max, row_sum, weighted = state_in
    scores = (
        jnp.einsum("bthd,bshd->bths", queries, key_piece, preferred_element_type=jnp.float32)
        * scale_factor
    )
    new_max = jnp.maximum(row_max, jnp.max(scores, axis=-1))
    rescale = jnp.exp(row_max - new_max)
    exp_vals = jnp.exp(scores - new_max[..., None])
    row_sum = row_sum * rescale + jnp.sum(exp_vals, axis=-1)
    weighted = weighted * rescale[..., None] + jnp.einsum(
        "bths,bshd->bthd",
        exp_vals.astype(jnp.bfloat16),
        value_piece,
        preferred_element_type=jnp.float32,
    )
    return (new_max, row_sum, weighted)


def back_piece(queries, grad_mixed, log_sum, row_delta, key_piece, value_piece, scale_factor):
    scores = (
        jnp.einsum("bthd,bshd->bths", queries, key_piece, preferred_element_type=jnp.float32)
        * scale_factor
    )
    probs = jnp.exp(scores - log_sum[..., None])
    grad_values = jnp.einsum(
        "bths,bthd->bshd",
        probs.astype(jnp.bfloat16),
        grad_mixed,
        preferred_element_type=jnp.float32,
    )
    grad_probs = jnp.einsum(
        "bthd,bshd->bths", grad_mixed, value_piece, preferred_element_type=jnp.float32
    )
    grad_scores = (probs * (grad_probs - row_delta[..., None])).astype(jnp.bfloat16)
    grad_query = (
        jnp.einsum("bths,bshd->bthd", grad_scores, key_piece, preferred_element_type=jnp.float32)
        * scale_factor
    )
    grad_keys = (
        jnp.einsum("bths,bthd->bshd", grad_scores, queries, preferred_element_type=jnp.float32)
        * scale_factor
    )
    return (grad_query, grad_keys, grad_values)


def add_at(whole_grads, piece_grads, offset):
    old_part = lax.dynamic_slice_in_dim(whole_grads, offset, piece_grads.shape[1], 1)
    return lax.dynamic_update_slice_in_dim(whole_grads, old_part + piece_grads, offset, 1)


def on_device(inputs, gain_one, w_qkv, w_attn, gain_two, w_in, w_ffn, cotangent):
    seq_dev = inputs.shape[0]
    tok_seq = inputs.shape[1]
    row_count = seq_dev * tok_seq
    seq_len = tok_seq * lax.axis_size("ctx")
    tokens_f = inputs.reshape(row_count, D).astype(jnp.float32)
    grad_out = cotangent.reshape(row_count, D)
    scale_factor = HEAD_DIM ** (-0.5)
    block_len = math.gcd(seq_len, 512)
    blocks_num = seq_len // block_len
    gathered = (
        lax.all_gather(gain_one, "fsdp", axis=0, tiled=True),
        lax.all_gather(w_qkv, "fsdp", axis=0, tiled=True),
        lax.all_gather(w_attn, "fsdp", axis=0, tiled=True),
        lax.all_gather(gain_two, "fsdp", axis=0, tiled=True),
        lax.all_gather(w_in, "fsdp", axis=0, tiled=True),
        lax.all_gather(w_ffn, "fsdp", axis=0, tiled=True),
    )
    full_g1, full_qkv, full_attn, full_g2, full_in, full_ffn = gathered
    normed_one, inv_one = norm_parts(tokens_f)
    input_one = (normed_one * full_g1.astype(jnp.float32)).astype(jnp.bfloat16)
    project = jnp.dot(input_one, full_qkv, preferred_element_type=jnp.float32)
    positions = lax.axis_index("ctx") * tok_seq + jnp.arange(tok_seq, dtype=jnp.int32)
    cosine, sine_part = rotary_tables(positions)
    shaped = project.reshape(seq_dev, tok_seq, 3, HEADS, HEAD_DIM)
    queries = rotate(shaped[:, :, 0], cosine, sine_part).astype(jnp.bfloat16)
    key_rows = rotate(shaped[:, :, 1], cosine, sine_part).astype(jnp.bfloat16)
    value_rows = shaped[:, :, 2].astype(jnp.bfloat16)
    start_state = (
        jnp.full((seq_dev, tok_seq, HEADS), -jnp.inf, jnp.float32),
        jnp.zeros((seq_dev, tok_seq, HEADS), jnp.float32),
        jnp.zeros((seq_dev, tok_seq, HEADS, HEAD_DIM), jnp.float32),
    )
    whole_keys, whole_values = (
        lax.all_gather(key_rows, "ctx", axis=1, tiled=True),
        lax.all_gather(value_rows, "ctx", axis=1, tiled=True),
    )

    def forward_step(state_in, block_index):
        begin = block_index * block_len
        key_piece = lax.dynamic_slice_in_dim(whole_keys, begin, block_len, 1)
        value_piece = lax.dynamic_slice_in_dim(whole_values, begin, block_len, 1)
        return (attend_piece(state_in, queries, key_piece, value_piece, scale_factor), None)

    state_out, unused = lax.scan(forward_step, start_state, jnp.arange(blocks_num, dtype=jnp.int32))
    row_max, row_sum, weighted = state_out
    attn_f = weighted / row_sum[..., None]
    log_sum = row_max + jnp.log(row_sum)
    attn_b = attn_f.reshape(row_count, D).astype(jnp.bfloat16)
    resid = tokens_f + jnp.dot(attn_b, full_attn, preferred_element_type=jnp.float32)
    normed_two, inv_two = norm_parts(resid)
    input_two = (normed_two * full_g2.astype(jnp.float32)).astype(jnp.bfloat16)
    widened = jnp.dot(input_two, full_in, preferred_element_type=jnp.float32)
    inner_part = widened[:, :FF]
    gating = widened[:, FF:]
    activated = jax.nn.gelu(inner_part, approximate=False)
    hidden = (activated * gating).astype(jnp.bfloat16)
    output = (resid + jnp.dot(hidden, full_ffn, preferred_element_type=jnp.float32)).astype(
        jnp.bfloat16
    )
    back_g1, back_qkv, back_attn, back_g2, back_in, back_ffn = gathered
    grad_ffn = jnp.dot(hidden.T, grad_out, preferred_element_type=jnp.float32)
    grad_hidden = jnp.dot(grad_out, back_ffn.T, preferred_element_type=jnp.float32)
    grad_inner = grad_hidden * gating * gelu_slope(inner_part)
    grad_gating = grad_hidden * activated
    grad_wide = jnp.concatenate([grad_inner, grad_gating], axis=-1).astype(jnp.bfloat16)
    grad_in = jnp.dot(input_two.T, grad_wide, preferred_element_type=jnp.float32)
    grad_normed_two = jnp.dot(grad_wide, back_in.T, preferred_element_type=jnp.float32)
    grad_g2 = jnp.sum(grad_normed_two * normed_two, axis=0)
    grad_resid = grad_out.astype(jnp.float32) + norm_back(
        grad_normed_two * back_g2.astype(jnp.float32), normed_two, inv_two
    )
    part_g2, part_in, part_ffn = (
        lax.psum_scatter(
            grad_g2.astype(jnp.bfloat16), "fsdp", scatter_dimension=0, tiled=True
        ).astype(jnp.float32),
        lax.psum_scatter(
            grad_in.astype(jnp.bfloat16), "fsdp", scatter_dimension=0, tiled=True
        ).astype(jnp.float32),
        lax.psum_scatter(
            grad_ffn.astype(jnp.bfloat16), "fsdp", scatter_dimension=0, tiled=True
        ).astype(jnp.float32),
    )
    resid_b = grad_resid.astype(jnp.bfloat16)
    grad_attn_w = jnp.dot(attn_b.T, resid_b, preferred_element_type=jnp.float32)
    grad_mixed = (
        jnp.dot(resid_b, back_attn.T, preferred_element_type=jnp.float32)
        .astype(jnp.bfloat16)
        .reshape(seq_dev, tok_seq, HEADS, HEAD_DIM)
    )
    row_delta = jnp.sum(grad_mixed.astype(jnp.float32) * attn_f, axis=-1)
    zero_q = jnp.zeros((seq_dev, tok_seq, HEADS, HEAD_DIM), jnp.float32)
    zero_kv = jnp.zeros((seq_dev, seq_len, HEADS, HEAD_DIM), jnp.float32)

    def backward_step(state_in, block_index):
        grad_q_sum, grad_key_all, grad_value_all = state_in
        begin = block_index * block_len
        key_piece = lax.dynamic_slice_in_dim(whole_keys, begin, block_len, 1)
        value_piece = lax.dynamic_slice_in_dim(whole_values, begin, block_len, 1)
        grad_query, grad_keys, grad_values = back_piece(
            queries, grad_mixed, log_sum, row_delta, key_piece, value_piece, scale_factor
        )
        return (
            (
                grad_q_sum + grad_query,
                add_at(grad_key_all, grad_keys, begin),
                add_at(grad_value_all, grad_values, begin),
            ),
            None,
        )

    back_state, unused_back = lax.scan(
        backward_step, (zero_q, zero_kv, zero_kv), jnp.arange(blocks_num, dtype=jnp.int32)
    )
    grad_q_sum, grad_key_all, grad_value_all = back_state
    own_keys, own_values = (
        lax.psum_scatter(
            grad_key_all.astype(jnp.bfloat16), "ctx", scatter_dimension=1, tiled=True
        ).astype(jnp.float32),
        lax.psum_scatter(
            grad_value_all.astype(jnp.bfloat16), "ctx", scatter_dimension=1, tiled=True
        ).astype(jnp.float32),
    )
    grad_q_rot = rotate_back(grad_q_sum, cosine, sine_part).reshape(row_count, D)
    grad_k_rot = rotate_back(own_keys, cosine, sine_part).reshape(row_count, D)
    grad_joint = jnp.concatenate(
        [grad_q_rot, grad_k_rot, own_values.reshape(row_count, D)], axis=-1
    ).astype(jnp.bfloat16)
    grad_qkv = jnp.dot(input_one.T, grad_joint, preferred_element_type=jnp.float32)
    grad_normed_one = jnp.dot(grad_joint, back_qkv.T, preferred_element_type=jnp.float32)
    grad_g1 = jnp.sum(grad_normed_one * normed_one, axis=0)
    grad_input = grad_resid + norm_back(
        grad_normed_one * back_g1.astype(jnp.float32), normed_one, inv_one
    )
    part_g1, part_qkv, part_attn = (
        lax.psum_scatter(
            grad_g1.astype(jnp.bfloat16), "fsdp", scatter_dimension=0, tiled=True
        ).astype(jnp.float32),
        lax.psum_scatter(
            grad_qkv.astype(jnp.bfloat16), "fsdp", scatter_dimension=0, tiled=True
        ).astype(jnp.float32),
        lax.psum_scatter(
            grad_attn_w.astype(jnp.bfloat16), "fsdp", scatter_dimension=0, tiled=True
        ).astype(jnp.float32),
    )
    totals = (
        lax.psum(part_g1.astype(jnp.bfloat16), "ctx").astype(jnp.float32),
        lax.psum(part_qkv.astype(jnp.bfloat16), "ctx").astype(jnp.float32),
        lax.psum(part_attn.astype(jnp.bfloat16), "ctx").astype(jnp.float32),
        lax.psum(part_g2.astype(jnp.bfloat16), "ctx").astype(jnp.float32),
        lax.psum(part_in.astype(jnp.bfloat16), "ctx").astype(jnp.float32),
        lax.psum(part_ffn.astype(jnp.bfloat16), "ctx").astype(jnp.float32),
    )
    return (
        output.reshape(seq_dev, tok_seq, D),
        grad_input.reshape(seq_dev, tok_seq, D),
        totals[0],
        totals[1],
        totals[2],
        totals[3],
        totals[4],
        totals[5],
    )


RING = 8
OWNERS = 4
PAIR = 2 * HEAD_DIM
UNITS = FF // RING
UNITS_PAD = 384
UNIT_ROWS = 336
ATTN_ROWS = 128
MESH = pl.DeviceIdType.MESH
VMEM_BYTES = 60 * 1024 * 1024
F32 = jnp.float32
BF16 = jnp.bfloat16


def contract(left, right, left_dim, right_dim):
    return lax.dot_general(
        left, right, (((left_dim,), (right_dim,)), ((), ())), preferred_element_type=F32
    )


class Here:
    def __init__(self):
        b, f = lax.axis_index("ctx"), lax.axis_index("fsdp")
        x, low = b % 2, (b // 2) % 2
        self.b, self.f = b, f
        self.c, self.y, self.q, self.high, self.x, self.low = f % 2, f // 2, b % 4, b // 4, x, low
        self.bx, self.bz = b + 1 - 2 * x, b + 2 - 4 * low
        self.bd, self.bh = self.bx + 2 - 4 * low, (b + 4) % RING
        self.qx, self.qz = self.q + 1 - 2 * x, self.q + 2 - 4 * low
        self.qd = self.qx + 2 - 4 * low
        self.core = f + 1 - 2 * self.c
        self.far = (f + 2) % OWNERS
        self.diag = (self.core + 2) % OWNERS
        self.p = self.c * 4 + self.q

    def mine(self, q):
        return self.c * 4 + q

    def other(self, q):
        return (1 - self.c) * 4 + q

    def greet(self):
        barrier = pltpu.get_barrier_semaphore()
        peers = [(b, f) for b in (self.b, self.bx, self.bz, self.bd) for f in (self.f, self.core)]
        peers = peers[1:] + [
            (self.b, self.far), (self.b, self.diag), (self.bh, self.f), (self.bh, self.core),
        ]
        for peer in peers:
            pl.semaphore_signal(barrier, inc=1, device_id=peer, device_id_type=MESH)
        pl.semaphore_wait(barrier, len(peers))


def push(src, dst, send, recv, device):
    return pltpu.make_async_remote_copy(
        src_ref=src, dst_ref=dst, send_sem=send, recv_sem=recv, device_id=device, device_id_type=MESH
    )


class Gather:
    def __init__(self, here, buf, send, recv):
        h = here
        self.h, self.send_sem, self.recv_sem = h, send, recv
        half = buf.shape[1] // 2
        top, bottom = pl.ds(0, half), pl.ds(half, half)
        own, near_x, near_z = buf.at[h.p], buf.at[h.mine(h.qx)], buf.at[h.mine(h.qz)]
        across = buf.at[h.mine(h.qd)]
        to_x, to_z, to_core = (h.bx, h.f), (h.bz, h.f), (h.b, h.core)
        self.out = [
            (own, to_x), (own, to_z), (near_z.at[top], to_x), (near_x.at[bottom], to_z),
            (own, to_core), (near_x, to_core), (near_z, to_core), (across, to_core),
        ]
        self.inn = [
            near_x, near_z, across.at[top], across.at[bottom],
            buf.at[h.other(h.q)], buf.at[h.other(h.qx)], buf.at[h.other(h.qz)], buf.at[h.other(h.qd)],
        ]

    def copy(self, kind):
        ref, device = self.out[kind]
        return push(ref, ref, self.send_sem.at[kind], self.recv_sem.at[kind], device)

    def wait(self, kind):
        ref = self.inn[kind]
        device = self.out[kind][1]
        push(ref, ref, self.send_sem.at[kind], self.recv_sem.at[kind], device).wait_recv()

    def begin(self):
        for kind in (0, 1, 4):
            self.copy(kind).start()

    def near(self):
        self.wait(0)
        self.copy(3).start()
        self.copy(5).start()
        self.wait(1)
        self.copy(2).start()
        self.copy(6).start()

    def across(self):
        self.wait(2)
        self.wait(3)
        self.copy(7).start()

    def sent(self):
        for kind in range(8):
            self.copy(kind).wait_send()

    def each(self, work):
        h = self.h
        work(h.p)
        self.wait(4)
        work(h.other(h.q))
        self.near()
        work(h.mine(h.qx))
        work(h.mine(h.qz))
        self.wait(5)
        work(h.other(h.qx))
        self.wait(6)
        work(h.other(h.qz))
        self.across()
        work(h.mine(h.qd))
        self.wait(7)
        work(h.other(h.qd))


class Scatter:
    def __init__(self, here, terms, core_out, near_out, across_out, core_in, near_in, across_in, send, recv):
        h = here
        self.h, self.terms, self.send_sem, self.recv_sem = h, terms, send, recv
        self.core_out, self.near_out, self.across_out = core_out, near_out, across_out
        self.core_in, self.near_in, self.across_in = core_in, near_in, across_in
        to_x, to_z, to_core = (h.bx, h.f), (h.bz, h.f), (h.b, h.core)
        self.out = [(core_out.at[i], core_in.at[i], to_core) for i in range(4)] + [
            (across_out.at[0], across_in.at[0], to_x),
            (across_out.at[1], across_in.at[1], to_z),
            (near_out.at[0], near_in.at[0], to_x),
            (near_out.at[1], near_in.at[1], to_z),
        ]
        self.half = terms.shape[1] // 2

    def copy(self, kind):
        src, dst, device = self.out[kind]
        return push(src, dst, self.send_sem.at[kind], self.recv_sem.at[kind], device)

    def wait(self, kind):
        self.copy(kind).wait_recv()

    def begin(self):
        h = self.h
        for i, q in enumerate((h.qd, h.qz, h.qx, h.q)):
            self.core_out[i] = self.terms[h.other(q)].astype(BF16)
            self.copy(i).start()

    def pair(self, i, q):
        return self.terms[self.h.mine(q)] + self.core_in[i].astype(F32)

    def first(self):
        self.wait(0)
        part = self.pair(0, self.h.qd).astype(BF16)
        self.across_out[0] = part[: self.half]
        self.copy(4).start()
        self.across_out[1] = part[self.half :]
        self.copy(5).start()

    def second(self):
        half = self.half
        self.wait(2)
        self.wait(5)
        part = self.pair(2, self.h.qx)
        self.near_out[0, :half] = part[:half].astype(BF16)
        self.near_out[0, half:] = (part[half:] + self.across_in[1].astype(F32)).astype(BF16)
        self.copy(6).start()
        self.wait(1)
        self.wait(4)
        part = self.pair(1, self.h.qz)
        self.near_out[1, :half] = (part[:half] + self.across_in[0].astype(F32)).astype(BF16)
        self.near_out[1, half:] = part[half:].astype(BF16)
        self.copy(7).start()

    def finish(self):
        self.wait(3)
        total = self.pair(3, self.h.q)
        self.wait(6)
        self.wait(7)
        total = total + self.near_in[0].astype(F32) + self.near_in[1].astype(F32)
        for kind in range(8):
            self.copy(kind).wait_send()
        return total


class Grads:
    def __init__(self, here, g, far_in, high_in, core_out, whole, send, recv):
        h = here
        self.h, self.g, self.far_in, self.high_in = h, g, far_in, high_in
        self.core_out, self.whole, self.send_sem, self.recv_sem = core_out, whole, send, recv
        self.out = [
            (g.at[1 - h.y], far_in, (h.b, h.far)),
            (g.at[h.y], high_in, (h.bh, h.f)),
            (core_out, whole.at[h.q, h.c], (h.b, h.core)),
            (whole.at[h.q], whole.at[h.q], (h.bx, h.f)),
            (whole.at[h.q], whole.at[h.q], (h.bz, h.f)),
            (whole.at[h.qz], whole.at[h.qz], (h.bx, h.f)),
        ]
        self.inn = [
            far_in, high_in, whole.at[h.q, 1 - h.c], whole.at[h.qx], whole.at[h.qz], whole.at[h.qd],
        ]

    def copy(self, kind):
        src, dst, device = self.out[kind]
        return push(src, dst, self.send_sem.at[kind], self.recv_sem.at[kind], device)

    def wait(self, kind):
        ref, device = self.inn[kind], self.out[kind][2]
        push(ref, ref, self.send_sem.at[kind], self.recv_sem.at[kind], device).wait_recv()

    def to_far(self):
        self.copy(0).start()

    def to_high(self):
        self.wait(0)
        y = self.h.y
        self.g[y] = (self.g[y].astype(F32) + self.far_in[...].astype(F32)).astype(BF16)
        self.copy(1).start()

    def total(self, c):
        return (self.g[self.h.y, c].astype(F32) + self.high_in[c].astype(F32)).astype(BF16)

    def to_core(self):
        self.wait(1)
        h = self.h
        self.core_out[...] = self.total(1 - h.c)
        self.copy(2).start()
        self.whole[h.q, h.c] = self.total(h.c)

    def to_near(self):
        self.wait(2)
        self.copy(3).start()
        self.copy(4).start()

    def to_across(self):
        self.wait(4)
        self.copy(5).start()
        self.wait(3)

    def finish(self):
        self.wait(5)

    def sent(self):
        for kind in range(6):
            self.copy(kind).wait_send()


class Rows:
    def __init__(self, here, whole, rows, send, recv):
        self.h, self.whole, self.rows, self.send_sem, self.recv_sem = here, whole, rows, send, recv

    def place(self, half, owner):
        return self.rows.at[half, :, pl.ds(pl.multiple_of(owner * 256, 256), 256)]

    def copy(self, q, c):
        h = self.h
        return push(
            self.whole.at[q, c], self.place(q % 2, h.f),
            self.send_sem.at[q, c], self.recv_sem.at[h.f, q % 2], (h.b, 2 * c + q // 2),
        )

    def begin(self):
        h = self.h
        for q in range(4):
            for c in range(2):
                owner = 2 * c + q // 2

                @pl.when(h.f != owner)
                def _(q=q, c=c):
                    self.copy(q, c).start()

                @pl.when(h.f == owner)
                def _(q=q, c=c, owner=owner):
                    self.rows[q % 2, :, owner * 256 : (owner + 1) * 256] = self.whole[q, c]

    def finish(self):
        h = self.h
        for owner in range(OWNERS):

            @pl.when(h.f != owner)
            def _(owner=owner):
                for half in range(2):
                    ref = self.place(half, owner)
                    push(
                        ref, ref, self.send_sem.at[0, 0], self.recv_sem.at[owner, half],
                        (h.b, owner),
                    ).wait_recv()

        for q in range(4):
            for c in range(2):

                @pl.when(h.f != 2 * c + q // 2)
                def _(q=q, c=c):
                    self.copy(q, c).wait_send()


def row_norm(rows):
    mean = jnp.mean(rows, axis=-1, keepdims=True)
    centred = rows - mean
    inv = lax.rsqrt(jnp.mean(centred * centred, axis=-1, keepdims=True) + EPSILON)
    return centred * inv, inv


def row_back(grad, normed, inv):
    return inv * (
        grad
        - jnp.mean(grad, axis=-1, keepdims=True)
        - normed * jnp.mean(grad * normed, axis=-1, keepdims=True)
    )


def first_half():
    lane = lax.broadcasted_iota(jnp.int32, (1, PAIR), 1)
    return lane % HEAD_DIM < HEAD_DIM // 2


def first_head():
    return lax.broadcasted_iota(jnp.int32, (1, PAIR), 1) < HEAD_DIM


def swap_halves(rows):
    up = pltpu.roll(rows, PAIR - HEAD_DIM // 2, 1)
    down = pltpu.roll(rows, HEAD_DIM // 2, 1)
    return jnp.where(first_half(), up, down)


def only(rows, head):
    keep = first_head() if head == 0 else jnp.logical_not(first_head())
    return jnp.where(keep, rows, jnp.zeros_like(rows))


def quarter(ref, j):
    tile = ref[:, :, j * 256 : (j + 1) * 256]
    return tile.reshape(tile.shape[0] * tile.shape[1], 256)


def flat(ref):
    rows = ref[...]
    return rows.reshape(rows.shape[0] * rows.shape[1], rows.shape[2])


class Box:
    pass


GATHERS = ("xg", "cg", "ag", "rg")
SCATTERS = ("two", "out", "one")
CHUNKS = (
    ("ffn", UNIT_ROWS), ("ing", UNIT_ROWS), ("inz", UNIT_ROWS),
    ("att", ATTN_ROWS), ("que", ATTN_ROWS), ("key", ATTN_ROWS), ("val", ATTN_ROWS),
)


def layout(seqs, tok):
    rows, length = seqs * tok, tok * RING
    whole = (RING, rows, D)
    half = rows // 2
    ins = [
        "x", "cot", "gain", "qkv_w", "attn_w", "in_w", "ffn_w", "cos", "sin",
    ]
    outs = {
        "output": ((rows, D), BF16),
        "grad_x": ((rows, D), F32),
        "gains": ((8, 256), F32),
        "ffn_rows": ((2, UNIT_ROWS, D), BF16),
        "att_rows": ((2, ATTN_ROWS, D), BF16),
    }
    for name, high in CHUNKS:
        if name not in ("ffn", "att"):
            outs[name + "_all"] = ((4, 2, high, 256), BF16)
    sem = pltpu.SemaphoreType.DMA
    vm = pltpu.VMEM
    scratch = {
        "xs": vm(whole, BF16), "cots": vm(whole, BF16), "a1": vm(whole, BF16), "a2": vm(whole, BF16),
        "resids": vm(whole, BF16), "terms": vm(whole, F32),
        "gain_all": vm((8, D), F32), "qkv_c": vm((D, 3 * PAIR), BF16), "attn_all": vm((D, D), BF16),
        "in_c": vm((D, 2 * UNITS_PAD), BF16), "ffn_c": vm((UNITS_PAD, D), BF16),
        "qs": vm((seqs, length, PAIR), BF16), "ks": vm((seqs, length, PAIR), BF16),
        "vs": vm((seqs, length, PAIR), BF16), "os": vm((seqs, length, PAIR), F32),
        "lse": vm((seqs, length, PAIR), F32), "heads": vm((RING, rows, PAIR), BF16),
        "own_heads": vm((RING, rows, PAIR), BF16), "mixed": vm((RING, rows, PAIR), BF16),
        "joint": vm((RING, rows, 3 * PAIR), BF16),
        "fs": vm((RING, rows, UNITS_PAD), BF16), "dus": vm((RING, rows, 2 * UNITS_PAD), BF16),
        "n2": vm((rows, D), F32), "resid": vm((rows, D), F32), "dy": vm((rows, D), F32),
        "core_out": vm((4, rows, D), BF16), "near_out": vm((2, rows, D), BF16),
        "across_out": vm((2, half, D), BF16),
        "back_out": vm((2, rows, D), BF16), "back_in": vm((2, rows, D), BF16),
        "sums": vm((6, 8, D), F32), "sums_in": vm((5, 8, D), F32),
        "ffn_all": vm((4, 2, UNIT_ROWS, 256), BF16), "att_all": vm((4, 2, ATTN_ROWS, 256), BF16),
    }
    for name in GATHERS:
        scratch[name + "_sems"] = (sem((8,)), sem((8,)))
    for name in SCATTERS:
        scratch[name + "_core"] = vm((4, rows, D), BF16)
        scratch[name + "_near"] = vm((2, rows, D), BF16)
        scratch[name + "_across"] = vm((2, half, D), BF16)
        scratch[name + "_sems"] = (sem((8,)), sem((8,)))
    for name, high in CHUNKS:
        scratch[name + "_g"] = vm((2, 2, high, 256), BF16)
        scratch[name + "_far"] = vm((2, high, 256), BF16)
        scratch[name + "_high"] = vm((2, high, 256), BF16)
        scratch[name + "_core"] = vm((high, 256), BF16)
        scratch[name + "_sems"] = (sem((6,)), sem((6,)))
    for name, count in (("swap", 4), ("part", 12), ("head", RING - 1), ("sum", 5)):
        scratch[name + "_sems"] = (sem((count,)), sem((count,)))
    scratch["ffn_w_sems"] = (sem((2,)), sem((1,)))
    for name in ("ffn_rows", "att_rows"):
        scratch[name + "_sems"] = (sem((4, 2)), sem((4, 2)))
    return ins, outs, scratch


def layer_kernel(names, *refs):
    r = Box()
    for name, ref in zip(names, refs):
        setattr(r, name, ref)
    h = Here()
    seqs, length = r.qs.shape[0], r.qs.shape[1]
    tok = length // RING
    scale = HEAD_DIM ** (-0.5)
    moved = h.high != h.c
    there = (h.bh, h.core)
    there_p = h.high * 4 + h.q
    h.greet()

    def swap(i, src, dst, back):
        send, recv = r.swap_sems
        return push(src, dst, send.at[i], recv.at[i], there)

    def swap_in(i, src, whole):
        @pl.when(moved)
        def _():
            swap(i, src, whole.at[there_p], False).start()

        @pl.when(jnp.logical_not(moved))
        def _():
            whole[h.p] = src[...]

    def swap_got(i, src, whole):
        @pl.when(moved)
        def _():
            swap(i, whole.at[h.p], whole.at[h.p], False).wait_recv()

    def swap_sent(i, src, whole):
        @pl.when(moved)
        def _():
            swap(i, src, whole.at[there_p], False).wait_send()

    swap_in(0, r.x, r.xs)

    p_send, p_recv = r.part_sems
    peers = (h.far, h.core, h.diag)

    def part_at(whole, owner, lanes):
        if lanes:
            return whole.at[:, pl.ds(pl.multiple_of(owner * 256, 256), 256)]
        return whole.at[pl.ds(pl.multiple_of(owner * 256, 256), 256)]

    def part(i, src, whole, lanes, sliced):
        def copy(k):
            mine = (h.c, 1 - h.c, 1 - h.c)[k]
            return push(
                src.at[mine] if sliced else src, part_at(whole, h.f, lanes),
                p_send.at[3 * i + k], p_recv.at[3 * i + k], (h.b, peers[k]),
            )

        box = Box()

        def begin():
            for k in range(3):
                copy(k).start()
            place = part_at(whole, h.f, lanes)
            place[...] = src[h.c] if sliced else src[...]

        def got():
            for k in range(3):
                ref = part_at(whole, peers[k], lanes)
                push(ref, ref, p_send.at[3 * i + k], p_recv.at[3 * i + k], (h.b, peers[k])).wait_recv()

        def sent():
            for k in range(3):
                copy(k).wait_send()

        box.begin, box.got, box.sent = begin, got, sent
        return box

    gain_p = part(0, r.gain, r.gain_all, True, False)
    qkv_p = part(1, r.qkv_w, r.qkv_c, False, True)
    in_p = part(2, r.in_w, r.in_c, False, True)

    def attn_copy(k):
        if k == 2:
            ref = part_at(r.attn_all, h.far, False)
            return push(ref, ref, p_send.at[9 + k], p_recv.at[9 + k], (h.b, h.core))
        return push(
            r.attn_w, part_at(r.attn_all, h.f, False),
            p_send.at[9 + k], p_recv.at[9 + k], (h.b, peers[k]),
        )

    def attn_wait(k):
        ref = part_at(r.attn_all, (h.far, h.core, h.diag)[k], False)
        push(ref, ref, p_send.at[9 + k], p_recv.at[9 + k], (h.b, h.core)).wait_recv()

    f_send, f_recv = r.ffn_w_sems
    active = h.c == h.low
    near_own = 2 * h.y + h.y
    far_own = 2 * (1 - h.y) + h.y
    ffn_owner = 2 * h.c + h.low
    unit_rows = pl.ds(0, UNIT_ROWS)

    def ffn_copy(k):
        return push(
            r.ffn_w.at[unit_rows], r.ffn_c.at[unit_rows],
            f_send.at[k], f_recv.at[0], (h.b, (near_own, far_own)[k]),
        )

    gain_p.begin()
    qkv_p.begin()
    swap_got(0, r.x, r.xs)
    swap_in(1, r.cot, r.cots)
    xg = Gather(h, r.xs, *r.xg_sems)
    xg.begin()
    gain_p.got()
    qkv_p.got()
    attn_copy(0).start()
    attn_copy(1).start()
    at_own = part_at(r.attn_all, h.f, False)
    at_own[...] = r.attn_w[...]
    in_p.begin()
    r.ffn_c[UNIT_ROWS:, :] = jnp.zeros((UNITS_PAD - UNIT_ROWS, D), BF16)

    @pl.when(active)
    def _():
        ffn_copy(1).start()

    @pl.when(jnp.logical_and(active, near_own != h.f))
    def _():
        ffn_copy(0).start()

    @pl.when(ffn_owner == h.f)
    def _():
        r.ffn_c[unit_rows, :] = r.ffn_w[unit_rows, :]

    def project(index):
        normed, _ = row_norm(r.xs[index].astype(F32))
        a1 = (normed * r.gain_all[0:1, :]).astype(BF16)
        r.a1[index] = a1
        r.terms[index, :, : 3 * PAIR] = contract(a1, r.qkv_c[...], 1, 0)

    xg.each(project)
    swap_got(1, r.cot, r.cots)
    cg = Gather(h, r.cots, *r.cg_sems)
    cg.begin()

    for s in range(seqs):
        rows = slice(s * tok, (s + 1) * tok)

        def columns(i):
            return r.terms[:, rows, i * PAIR : (i + 1) * PAIR].reshape(length, PAIR)

        cos, sin = r.cos[...], r.sin[...]
        query, key = columns(0), columns(1)
        q = (query * cos + swap_halves(query) * sin).astype(BF16)
        k = (key * cos + swap_halves(key) * sin).astype(BF16)
        v = columns(2).astype(BF16)
        r.qs[s] = q
        r.ks[s] = k
        r.vs[s] = v
        outs, lses = [], []
        for head in range(2):
            scores = contract(only(q, head), k, 1, 1) * scale
            top = jnp.max(scores, axis=-1, keepdims=True)
            e = jnp.exp(scores - top)
            total = jnp.sum(e, axis=-1, keepdims=True)
            outs.append(contract(e.astype(BF16), v, 1, 0) / total)
            lses.append(top + jnp.log(total))
        of = jnp.where(first_head(), outs[0], outs[1])
        r.os[s] = of
        r.lse[s] = jnp.where(first_head(), lses[0], lses[1])
        r.heads[:, rows, :] = of.astype(BF16).reshape(RING, tok, PAIR)

    h_send, h_recv = r.head_sems
    around = []
    for b, q in ((h.b, h.q), (h.bx, h.qx), (h.bz, h.qz), (h.bd, h.qd)):
        around += [((b, h.f), h.mine(q)), ((b, h.core), h.other(q))]

    def exchange(i):
        device, p = around[i + 1]
        return push(r.heads.at[p], r.own_heads.at[h.p], h_send.at[i], h_recv.at[i], device)

    for i in range(RING - 1):
        exchange(i).start()
    r.own_heads[h.p] = r.heads[h.p]
    attn_wait(0)
    attn_copy(2).start()
    cg.near()
    attn_wait(1)
    attn_wait(2)
    for i in range(RING - 1):
        device, p = around[i + 1]
        ref = r.own_heads.at[p]
        push(ref, ref, h_send.at[i], h_recv.at[i], device).wait_recv()

    g2 = r.gain_all[1:2, :]
    mixed_heads = jnp.concatenate([r.own_heads[d] for d in range(RING)], axis=1)
    resid = r.xs[h.p].astype(F32) + contract(mixed_heads, r.attn_all[...], 1, 0)
    r.resid[...] = resid
    normed, inv_two = row_norm(resid)
    r.n2[...] = normed
    r.a2[h.p] = (normed * g2).astype(BF16)
    ag = Gather(h, r.a2, *r.ag_sems)
    ag.begin()
    cg.across()
    in_p.got()

    @pl.when(ffn_owner != h.f)
    def _():
        ffn_copy(0).wait_recv()

    for kind in range(4, 8):
        cg.wait(kind)

    def feed(index):
        widened = contract(r.a2[index], r.in_c[...], 1, 0)
        inner, gating = widened[:, :UNITS_PAD], widened[:, UNITS_PAD:]
        below = 0.5 * (1.0 + lax.erf(inner * 0.7071067811865476))
        density = jnp.exp(-0.5 * inner * inner) * 0.3989422804014327
        active = inner * below
        r.fs[index] = (active * gating).astype(BF16)
        grad_hidden = contract(r.cots[index], r.ffn_c[...], 1, 1)
        du = jnp.concatenate(
            [grad_hidden * gating * (below + inner * density), grad_hidden * active], axis=1
        ).astype(BF16)
        r.dus[index] = du
        r.terms[index] = contract(du, r.in_c[...], 1, 1)

    ag.each(feed)

    def scatter(name):
        return Scatter(
            h, r.terms, r.core_out, r.near_out, r.across_out,
            getattr(r, name + "_core"), getattr(r, name + "_near"), getattr(r, name + "_across"),
            *getattr(r, name + "_sems"),
        )

    ch = {}
    for name, _ in CHUNKS:
        ch[name] = Grads(
            h, getattr(r, name + "_g"), getattr(r, name + "_far"), getattr(r, name + "_high"),
            getattr(r, name + "_core"), getattr(r, name + "_all"), *getattr(r, name + "_sems"),
        )

    two = scatter("two")
    two.begin()
    for j in range(OWNERS):
        c, y = j % 2, j // 2
        r.ffn_g[y, c] = contract(flat(r.fs), quarter(r.cots, j), 0, 0)[:UNIT_ROWS].astype(BF16)
        if j == 0:
            two.first()
        grad_in = contract(flat(r.dus), quarter(r.a2, j), 0, 0).astype(BF16)
        r.ing_g[y, c] = grad_in[:UNIT_ROWS]
        r.inz_g[y, c] = grad_in[UNITS_PAD : UNITS_PAD + UNIT_ROWS]
        if j == 1:
            two.second()
    ch["ffn"].to_far()
    ch["ing"].to_far()
    ch["inz"].to_far()
    grad_two = two.finish()

    normed = r.n2[...]
    r.sums[0, 1:2, :] = jnp.sum(grad_two * normed, axis=0, keepdims=True)
    own_grad = r.cots[h.p].astype(F32) + row_back(grad_two * g2, normed, inv_two)
    r.dy[...] = own_grad
    r.resids[h.p] = own_grad.astype(BF16)
    rg = Gather(h, r.resids, *r.rg_sems)
    rg.begin()

    attn_c = r.attn_all.at[pl.ds(pl.multiple_of(h.p * PAIR, PAIR), PAIR)]

    def mix(index):
        r.mixed[index] = contract(r.resids[index], attn_c[...], 1, 1).astype(BF16)
        r.terms[index] = contract(r.fs[index], r.ffn_c[...], 1, 0)

    rg.each(mix)
    out = scatter("out")
    out.begin()
    ch["ffn"].to_high()
    for j in range(OWNERS):
        r.att_g[j // 2, j % 2] = contract(flat(r.heads), quarter(r.resids, j), 0, 0).astype(BF16)
    out.first()
    ch["att"].to_far()

    for s in range(seqs):
        rows = slice(s * tok, (s + 1) * tok)
        q, k, v = r.qs[s], r.ks[s], r.vs[s]
        do = r.mixed[:, rows, :].reshape(length, PAIR)
        weighed = do.astype(F32) * r.os[s]
        dqs, dks, dvs = [], [], []
        for head in range(2):
            delta = jnp.sum(only(weighed, head), axis=-1, keepdims=True)
            lse = r.lse[s, :, head * HEAD_DIM : head * HEAD_DIM + 1]
            probs = jnp.exp(contract(only(q, head), k, 1, 1) * scale - lse)
            dvs.append(contract(probs.astype(BF16), do, 0, 0))
            grad_probs = contract(only(do, head), v, 1, 1)
            ds = (probs * (grad_probs - delta)).astype(BF16)
            dqs.append(contract(ds, k, 1, 0) * scale)
            dks.append(contract(ds, q, 0, 0) * scale)
            if s == 0 and head == 1:
                out.second()
            if s == 0 and head == 0:
                ch["ing"].to_high()
            if s == 1 and head == 0:
                ch["inz"].to_high()
        cos, sin = r.cos[...], r.sin[...]
        dq = jnp.where(first_head(), dqs[0], dqs[1])
        dk = jnp.where(first_head(), dks[0], dks[1])
        dv = jnp.where(first_head(), dvs[0], dvs[1])
        for i, item in enumerate(
            (dq * cos - swap_halves(dq) * sin, dk * cos - swap_halves(dk) * sin, dv)
        ):
            r.joint[:, rows, i * PAIR : (i + 1) * PAIR] = item.astype(BF16).reshape(RING, tok, PAIR)

    r.back_out[0] = (r.resid[...] + out.finish()).astype(BF16)

    def back(i):
        return swap(2 + i, r.back_out.at[i], r.back_in.at[i], True)

    @pl.when(moved)
    def _():
        back(0).start()

    ch["att"].to_high()

    def term(i, carry):
        r.terms[i] = contract(r.joint[i], r.qkv_c[...], 1, 1)
        return carry

    lax.fori_loop(0, RING, term, 0)
    one = scatter("one")
    one.begin()
    for j in range(OWNERS):
        grad_qkv = contract(flat(r.joint), quarter(r.a1, j), 0, 0).astype(BF16)
        for i, name in enumerate(("que", "key", "val")):
            getattr(r, name + "_g")[j // 2, j % 2] = grad_qkv[i * PAIR : (i + 1) * PAIR]
        if j == 0:
            one.first()
        if j == 2:
            one.second()
    for name in ("que", "key", "val"):
        ch[name].to_far()
    ch["ffn"].to_core()
    ch["ffn"].to_near()

    grad_one = one.finish()
    normed, inv_one = row_norm(r.xs[h.p].astype(F32))
    r.sums[0, 0:1, :] = jnp.sum(grad_one * normed, axis=0, keepdims=True)
    r.sums[0, 2:, :] = jnp.zeros((6, D), F32)
    s_send, s_recv = r.sum_sems
    partners = ((h.b, h.core), (h.b, h.far), (h.bx, h.f), (h.bz, h.f), (h.bh, h.f))

    def sum_copy(i):
        return push(r.sums.at[i], r.sums_in.at[i], s_send.at[i], s_recv.at[i], partners[i])

    def sum_step(i):
        sum_copy(i).wait_recv()
        r.sums[i + 1] = r.sums[i] + r.sums_in[i]
        if i < 4:
            sum_copy(i + 1).start()

    sum_copy(0).start()
    grad_x = r.dy[...] + row_back(grad_one * r.gain_all[0:1, :], normed, inv_one)
    r.grad_x[...] = grad_x
    r.back_out[1] = grad_x.astype(BF16)

    @pl.when(moved)
    def _():
        back(1).start()

    for name in ("que", "key", "val"):
        ch[name].to_high()
    sum_step(0)
    ch["ing"].to_core()
    ch["ing"].to_near()
    ch["ffn"].to_across()
    sum_step(1)
    ch["inz"].to_core()
    ch["inz"].to_near()
    ch["ing"].to_across()
    sum_step(2)
    ch["att"].to_core()
    ch["att"].to_near()
    ch["inz"].to_across()
    ch["ffn"].finish()
    ffn_rows = Rows(h, r.ffn_all, r.ffn_rows, *r.ffn_rows_sems)
    ffn_rows.begin()
    sum_step(3)
    ch["que"].to_core()
    ch["que"].to_near()
    ch["att"].to_across()
    ch["key"].to_core()
    ch["key"].to_near()
    ch["que"].to_across()
    ch["val"].to_core()
    ch["val"].to_near()
    ch["key"].to_across()
    sum_step(4)
    r.gains[...] = r.sums[5, :, pl.ds(pl.multiple_of(h.f * 256, 256), 256)]
    ch["val"].to_across()
    ch["att"].finish()
    att_rows = Rows(h, r.att_all, r.att_rows, *r.att_rows_sems)
    att_rows.begin()

    @pl.when(moved)
    def _():
        for i in range(2):
            back(i).wait_recv()
            back(i).wait_send()
        r.output[...] = r.back_in[0]
        r.grad_x[...] = r.back_in[1].astype(F32)

    @pl.when(jnp.logical_not(moved))
    def _():
        r.output[...] = r.back_out[0]

    for name in ("ing", "inz", "que", "key", "val"):
        ch[name].finish()
    ffn_rows.finish()
    att_rows.finish()

    swap_sent(0, r.x, r.xs)
    swap_sent(1, r.cot, r.cots)
    for item in (xg, cg, ag, rg):
        item.sent()
    for item in (gain_p, qkv_p, in_p):
        item.sent()
    for k in range(3):
        attn_copy(k).wait_send()

    @pl.when(active)
    def _():
        ffn_copy(1).wait_send()

    @pl.when(jnp.logical_and(active, near_own != h.f))
    def _():
        ffn_copy(0).wait_send()

    for i in range(RING - 1):
        exchange(i).wait_send()
    for i in range(5):
        sum_copy(i).wait_send()
    for name, _ in CHUNKS:
        ch[name].sent()


def finish_kernel(ing, inz, que, key, val, ffn, att, in_o, qkv_o, ffn_o, att_o):
    for q in range(4):
        for c in range(2):
            p = 4 * c + q
            for i, ref in enumerate((ing, inz)):
                start = i * FF + p * UNITS
                in_o[:, start : start + UNITS] = ref[q, c].astype(F32).T[:, :UNITS]
            for i, ref in enumerate((que, key, val)):
                start = i * D + p * PAIR
                qkv_o[:, start : start + PAIR] = ref[q, c].astype(F32).T
    for half in range(2):
        ffn_o[half * UNITS : (half + 1) * UNITS, :] = ffn[half, :UNITS, :].astype(F32)
        att_o[half * ATTN_ROWS : (half + 1) * ATTN_ROWS, :] = att[half].astype(F32)


def finish(ing, inz, que, key, val, ffn, att):
    def slices(high):
        return pl.BlockSpec((4, 2, high, 128), lambda i: (0, 0, 0, i))

    def rows(high):
        return pl.BlockSpec((2, high, D // 2), lambda i: (0, 0, i))

    return pl.pallas_call(
        finish_kernel,
        grid=(2,),
        out_shape=[
            jax.ShapeDtypeStruct((256, 2 * FF), F32),
            jax.ShapeDtypeStruct((256, 3 * D), F32),
            jax.ShapeDtypeStruct((2 * UNITS, D), F32),
            jax.ShapeDtypeStruct((2 * ATTN_ROWS, D), F32),
        ],
        in_specs=[slices(UNIT_ROWS)] * 2 + [slices(ATTN_ROWS)] * 3 + [rows(UNIT_ROWS), rows(ATTN_ROWS)],
        out_specs=[
            pl.BlockSpec((128, 2 * FF), lambda i: (i, 0)),
            pl.BlockSpec((128, 3 * D), lambda i: (i, 0)),
            pl.BlockSpec((2 * UNITS, D // 2), lambda i: (0, i)),
            pl.BlockSpec((2 * ATTN_ROWS, D // 2), lambda i: (0, i)),
        ],
        compiler_params=pltpu.CompilerParams(vmem_limit_bytes=VMEM_BYTES),
    )(ing, inz, que, key, val, ffn, att)


def rotary_rows(length):
    half = HEAD_DIM // 2
    freq = (np.float32(ROPE_THETA) ** (-(np.arange(half, dtype=np.float32) * 2.0) / HEAD_DIM)).astype(
        np.float32
    )
    angles = np.arange(length, dtype=np.float32)[:, None] * freq[None, :]
    cos, sin = np.cos(angles), np.sin(angles)
    return np.tile(cos, (1, 4)), np.tile(np.concatenate([-sin, sin], axis=1), (1, 2))


def by_squares(inputs, gain_one, w_qkv, w_attn, gain_two, w_in, w_ffn, cotangent):
    block = lax.axis_index("ctx")
    chip = block % 4
    seqs, tok, _ = inputs.shape
    rows = seqs * tok
    part = w_qkv.shape[0]

    by_kind = w_qkv.reshape(part, 3, D)
    qkv_w = jnp.stack(
        [
            lax.dynamic_slice_in_dim(by_kind, (4 * c + chip) * PAIR, PAIR, 2).reshape(part, 3 * PAIR)
            for c in range(2)
        ]
    )

    def units(start):
        cut = lax.dynamic_slice_in_dim(w_in, start, UNITS, 1)
        return jnp.pad(cut, ((0, 0), (0, UNITS_PAD - UNITS)))

    in_w = jnp.stack(
        [
            jnp.concatenate([units((4 * c + chip) * UNITS + start) for start in (0, FF)], axis=1)
            for c in range(2)
        ]
    )
    ffn_w = lax.dynamic_slice_in_dim(w_ffn, block % 2 * UNITS, UNITS, 0)
    ffn_w = jnp.pad(ffn_w, ((0, UNIT_ROWS - UNITS), (0, 0)))
    gains = jnp.pad(jnp.stack([gain_one, gain_two]).astype(F32), ((0, 6), (0, 0)))
    cos, sin = (jnp.asarray(t, F32) for t in rotary_rows(tok * RING))

    ins, outs, scratch = layout(seqs, tok)
    names, shapes = [], []
    for name, item in scratch.items():
        pair = item if isinstance(item, tuple) else (item,)
        names.append((name, len(pair)))
        shapes += pair

    def body(*refs):
        count = len(ins) + len(outs)
        rest = list(refs[count:])
        found = list(refs[:count])
        for _, size in names:
            taken = tuple(rest[:size])
            rest = rest[size:]
            found.append(taken if size > 1 else taken[0])
        layer_kernel(ins + list(outs) + [name for name, _ in names], *found)

    vmem = pl.BlockSpec(memory_space=pltpu.VMEM)
    done = pl.pallas_call(
        body,
        out_shape=[jax.ShapeDtypeStruct(shape, dtype) for shape, dtype in outs.values()],
        in_specs=[vmem] * len(ins),
        out_specs=[vmem] * len(outs),
        scratch_shapes=shapes,
        compiler_params=pltpu.CompilerParams(
            collective_id=0, has_side_effects=True, vmem_limit_bytes=VMEM_BYTES
        ),
    )(
        inputs.reshape(rows, D), cotangent.reshape(rows, D),
        gains, qkv_w, w_attn, in_w, ffn_w, cos, sin,
    )
    done = dict(zip(outs, done))
    grad_in, grad_qkv, grad_ffn, grad_attn = finish(
        done["ing_all"], done["inz_all"], done["que_all"], done["key_all"], done["val_all"],
        done["ffn_rows"], done["att_rows"],
    )
    return (
        done["output"].reshape(seqs, tok, D),
        done["grad_x"].reshape(seqs, tok, D),
        done["gains"][0],
        grad_qkv,
        grad_attn,
        done["gains"][1],
        grad_in,
        grad_ffn,
    )


def solution(mesh):
    split_ok = mesh.shape["ctx"] == RING and mesh.shape["fsdp"] == OWNERS

    return jax.shard_map(
        by_squares if split_ok else on_device,
        mesh=mesh,
        in_specs=(
            P("fsdp", "ctx", None),
            P("fsdp"),
            P("fsdp", None),
            P("fsdp", None),
            P("fsdp"),
            P("fsdp", None),
            P("fsdp", None),
            P("fsdp", "ctx", None),
        ),
        out_specs=(
            P("fsdp", "ctx", None),
            P("fsdp", "ctx", None),
            P("fsdp"),
            P("fsdp", None),
            P("fsdp", None),
            P("fsdp"),
            P("fsdp", None),
            P("fsdp", None),
        ),
        check_vma=False,
    )
```

```python
import math

import jax
import jax.numpy as jnp
import numpy as np
from jax import lax
from jax.experimental import pallas as pl
from jax.experimental.pallas import tpu as pltpu
from jax.sharding import PartitionSpec as P

D = 1024
HEADS = 16
HEAD_DIM = 64
FF = 2624


EPSILON = 1e-05
ROPE_THETA = 160000.0


def norm_parts(values_in):
    mean_val = jnp.mean(values_in, axis=-1, keepdims=True)
    centred = values_in - mean_val
    variance = jnp.mean(centred * centred, axis=-1, keepdims=True)
    inv_std = lax.rsqrt(variance + EPSILON)
    return (centred * inv_std, inv_std)


def norm_back(grad_normed, normed, inv_std):
    return inv_std * (
        grad_normed
        - jnp.mean(grad_normed, axis=-1, keepdims=True)
        - normed * jnp.mean(grad_normed * normed, axis=-1, keepdims=True)
    )


def rotary_tables(positions):
    half_dim = HEAD_DIM // 2
    inv_freq = ROPE_THETA ** (-(jnp.arange(half_dim, dtype=jnp.float32) * 2.0) / HEAD_DIM)
    angles = positions.astype(jnp.float32)[:, None] * inv_freq[None, :]
    cosine = jnp.concatenate([jnp.cos(angles), jnp.cos(angles)], axis=-1)[:, None, :]
    sine_part = jnp.concatenate([jnp.sin(angles), jnp.sin(angles)], axis=-1)[:, None, :]
    return (cosine, sine_part)


def rotate(values_in, cosine, sine_part):
    half_dim = values_in.shape[-1] // 2
    turned = jnp.concatenate([-values_in[..., half_dim:], values_in[..., :half_dim]], axis=-1)
    return values_in * cosine + turned * sine_part


def rotate_back(grads, cosine, sine_part):
    half_dim = grads.shape[-1] // 2
    scaled = grads * sine_part
    turned = jnp.concatenate([scaled[..., half_dim:], -scaled[..., :half_dim]], axis=-1)
    return grads * cosine + turned


def gelu_slope(inner_part):
    cumulative = 0.5 * (1.0 + jax.scipy.special.erf(inner_part * 0.7071067811865476))
    density = jnp.exp(-0.5 * inner_part * inner_part) * 0.3989422804014327
    return cumulative + inner_part * density


def attend_piece(state_in, queries, key_piece, value_piece, scale_factor):
    row_max, row_sum, weighted = state_in
    scores = (
        jnp.einsum("bthd,bshd->bths", queries, key_piece, preferred_element_type=jnp.float32)
        * scale_factor
    )
    new_max = jnp.maximum(row_max, jnp.max(scores, axis=-1))
    rescale = jnp.exp(row_max - new_max)
    exp_vals = jnp.exp(scores - new_max[..., None])
    row_sum = row_sum * rescale + jnp.sum(exp_vals, axis=-1)
    weighted = weighted * rescale[..., None] + jnp.einsum(
        "bths,bshd->bthd",
        exp_vals.astype(jnp.bfloat16),
        value_piece,
        preferred_element_type=jnp.float32,
    )
    return (new_max, row_sum, weighted)


def back_piece(queries, grad_mixed, log_sum, row_delta, key_piece, value_piece, scale_factor):
    scores = (
        jnp.einsum("bthd,bshd->bths", queries, key_piece, preferred_element_type=jnp.float32)
        * scale_factor
    )
    probs = jnp.exp(scores - log_sum[..., None])
    grad_values = jnp.einsum(
        "bths,bthd->bshd",
        probs.astype(jnp.bfloat16),
        grad_mixed,
        preferred_element_type=jnp.float32,
    )
    grad_probs = jnp.einsum(
        "bthd,bshd->bths", grad_mixed, value_piece, preferred_element_type=jnp.float32
    )
    grad_scores = (probs * (grad_probs - row_delta[..., None])).astype(jnp.bfloat16)
    grad_query = (
        jnp.einsum("bths,bshd->bthd", grad_scores, key_piece, preferred_element_type=jnp.float32)
        * scale_factor
    )
    grad_keys = (
        jnp.einsum("bths,bthd->bshd", grad_scores, queries, preferred_element_type=jnp.float32)
        * scale_factor
    )
    return (grad_query, grad_keys, grad_values)


def add_at(whole_grads, piece_grads, offset):
    old_part = lax.dynamic_slice_in_dim(whole_grads, offset, piece_grads.shape[1], 1)
    return lax.dynamic_update_slice_in_dim(whole_grads, old_part + piece_grads, offset, 1)


def on_device(inputs, gain_one, w_qkv, w_attn, gain_two, w_in, w_ffn, cotangent):
    seq_dev = inputs.shape[0]
    tok_seq = inputs.shape[1]
    row_count = seq_dev * tok_seq
    seq_len = tok_seq * lax.axis_size("ctx")
    tokens_f = inputs.reshape(row_count, D).astype(jnp.float32)
    grad_out = cotangent.reshape(row_count, D)
    scale_factor = HEAD_DIM ** (-0.5)
    block_len = math.gcd(seq_len, 512)
    blocks_num = seq_len // block_len
    gathered = (
        lax.all_gather(gain_one, "fsdp", axis=0, tiled=True),
        lax.all_gather(w_qkv, "fsdp", axis=0, tiled=True),
        lax.all_gather(w_attn, "fsdp", axis=0, tiled=True),
        lax.all_gather(gain_two, "fsdp", axis=0, tiled=True),
        lax.all_gather(w_in, "fsdp", axis=0, tiled=True),
        lax.all_gather(w_ffn, "fsdp", axis=0, tiled=True),
    )
    full_g1, full_qkv, full_attn, full_g2, full_in, full_ffn = gathered
    normed_one, inv_one = norm_parts(tokens_f)
    input_one = (normed_one * full_g1.astype(jnp.float32)).astype(jnp.bfloat16)
    project = jnp.dot(input_one, full_qkv, preferred_element_type=jnp.float32)
    positions = lax.axis_index("ctx") * tok_seq + jnp.arange(tok_seq, dtype=jnp.int32)
    cosine, sine_part = rotary_tables(positions)
    shaped = project.reshape(seq_dev, tok_seq, 3, HEADS, HEAD_DIM)
    queries = rotate(shaped[:, :, 0], cosine, sine_part).astype(jnp.bfloat16)
    key_rows = rotate(shaped[:, :, 1], cosine, sine_part).astype(jnp.bfloat16)
    value_rows = shaped[:, :, 2].astype(jnp.bfloat16)
    start_state = (
        jnp.full((seq_dev, tok_seq, HEADS), -jnp.inf, jnp.float32),
        jnp.zeros((seq_dev, tok_seq, HEADS), jnp.float32),
        jnp.zeros((seq_dev, tok_seq, HEADS, HEAD_DIM), jnp.float32),
    )
    whole_keys, whole_values = (
        lax.all_gather(key_rows, "ctx", axis=1, tiled=True),
        lax.all_gather(value_rows, "ctx", axis=1, tiled=True),
    )

    def forward_step(state_in, block_index):
        begin = block_index * block_len
        key_piece = lax.dynamic_slice_in_dim(whole_keys, begin, block_len, 1)
        value_piece = lax.dynamic_slice_in_dim(whole_values, begin, block_len, 1)
        return (attend_piece(state_in, queries, key_piece, value_piece, scale_factor), None)

    state_out, unused = lax.scan(forward_step, start_state, jnp.arange(blocks_num, dtype=jnp.int32))
    row_max, row_sum, weighted = state_out
    attn_f = weighted / row_sum[..., None]
    log_sum = row_max + jnp.log(row_sum)
    attn_b = attn_f.reshape(row_count, D).astype(jnp.bfloat16)
    resid = tokens_f + jnp.dot(attn_b, full_attn, preferred_element_type=jnp.float32)
    normed_two, inv_two = norm_parts(resid)
    input_two = (normed_two * full_g2.astype(jnp.float32)).astype(jnp.bfloat16)
    widened = jnp.dot(input_two, full_in, preferred_element_type=jnp.float32)
    inner_part = widened[:, :FF]
    gating = widened[:, FF:]
    activated = jax.nn.gelu(inner_part, approximate=False)
    hidden = (activated * gating).astype(jnp.bfloat16)
    output = (resid + jnp.dot(hidden, full_ffn, preferred_element_type=jnp.float32)).astype(
        jnp.bfloat16
    )
    back_g1, back_qkv, back_attn, back_g2, back_in, back_ffn = gathered
    grad_ffn = jnp.dot(hidden.T, grad_out, preferred_element_type=jnp.float32)
    grad_hidden = jnp.dot(grad_out, back_ffn.T, preferred_element_type=jnp.float32)
    grad_inner = grad_hidden * gating * gelu_slope(inner_part)
    grad_gating = grad_hidden * activated
    grad_wide = jnp.concatenate([grad_inner, grad_gating], axis=-1).astype(jnp.bfloat16)
    grad_in = jnp.dot(input_two.T, grad_wide, preferred_element_type=jnp.float32)
    grad_normed_two = jnp.dot(grad_wide, back_in.T, preferred_element_type=jnp.float32)
    grad_g2 = jnp.sum(grad_normed_two * normed_two, axis=0)
    grad_resid = grad_out.astype(jnp.float32) + norm_back(
        grad_normed_two * back_g2.astype(jnp.float32), normed_two, inv_two
    )
    part_g2, part_in, part_ffn = (
        lax.psum_scatter(
            grad_g2.astype(jnp.bfloat16), "fsdp", scatter_dimension=0, tiled=True
        ).astype(jnp.float32),
        lax.psum_scatter(
            grad_in.astype(jnp.bfloat16), "fsdp", scatter_dimension=0, tiled=True
        ).astype(jnp.float32),
        lax.psum_scatter(
            grad_ffn.astype(jnp.bfloat16), "fsdp", scatter_dimension=0, tiled=True
        ).astype(jnp.float32),
    )
    resid_b = grad_resid.astype(jnp.bfloat16)
    grad_attn_w = jnp.dot(attn_b.T, resid_b, preferred_element_type=jnp.float32)
    grad_mixed = (
        jnp.dot(resid_b, back_attn.T, preferred_element_type=jnp.float32)
        .astype(jnp.bfloat16)
        .reshape(seq_dev, tok_seq, HEADS, HEAD_DIM)
    )
    row_delta = jnp.sum(grad_mixed.astype(jnp.float32) * attn_f, axis=-1)
    zero_q = jnp.zeros((seq_dev, tok_seq, HEADS, HEAD_DIM), jnp.float32)
    zero_kv = jnp.zeros((seq_dev, seq_len, HEADS, HEAD_DIM), jnp.float32)

    def backward_step(state_in, block_index):
        grad_q_sum, grad_key_all, grad_value_all = state_in
        begin = block_index * block_len
        key_piece = lax.dynamic_slice_in_dim(whole_keys, begin, block_len, 1)
        value_piece = lax.dynamic_slice_in_dim(whole_values, begin, block_len, 1)
        grad_query, grad_keys, grad_values = back_piece(
            queries, grad_mixed, log_sum, row_delta, key_piece, value_piece, scale_factor
        )
        return (
            (
                grad_q_sum + grad_query,
                add_at(grad_key_all, grad_keys, begin),
                add_at(grad_value_all, grad_values, begin),
            ),
            None,
        )

    back_state, unused_back = lax.scan(
        backward_step, (zero_q, zero_kv, zero_kv), jnp.arange(blocks_num, dtype=jnp.int32)
    )
    grad_q_sum, grad_key_all, grad_value_all = back_state
    own_keys, own_values = (
        lax.psum_scatter(
            grad_key_all.astype(jnp.bfloat16), "ctx", scatter_dimension=1, tiled=True
        ).astype(jnp.float32),
        lax.psum_scatter(
            grad_value_all.astype(jnp.bfloat16), "ctx", scatter_dimension=1, tiled=True
        ).astype(jnp.float32),
    )
    grad_q_rot = rotate_back(grad_q_sum, cosine, sine_part).reshape(row_count, D)
    grad_k_rot = rotate_back(own_keys, cosine, sine_part).reshape(row_count, D)
    grad_joint = jnp.concatenate(
        [grad_q_rot, grad_k_rot, own_values.reshape(row_count, D)], axis=-1
    ).astype(jnp.bfloat16)
    grad_qkv = jnp.dot(input_one.T, grad_joint, preferred_element_type=jnp.float32)
    grad_normed_one = jnp.dot(grad_joint, back_qkv.T, preferred_element_type=jnp.float32)
    grad_g1 = jnp.sum(grad_normed_one * normed_one, axis=0)
    grad_input = grad_resid + norm_back(
        grad_normed_one * back_g1.astype(jnp.float32), normed_one, inv_one
    )
    part_g1, part_qkv, part_attn = (
        lax.psum_scatter(
            grad_g1.astype(jnp.bfloat16), "fsdp", scatter_dimension=0, tiled=True
        ).astype(jnp.float32),
        lax.psum_scatter(
            grad_qkv.astype(jnp.bfloat16), "fsdp", scatter_dimension=0, tiled=True
        ).astype(jnp.float32),
        lax.psum_scatter(
            grad_attn_w.astype(jnp.bfloat16), "fsdp", scatter_dimension=0, tiled=True
        ).astype(jnp.float32),
    )
    totals = (
        lax.psum(part_g1.astype(jnp.bfloat16), "ctx").astype(jnp.float32),
        lax.psum(part_qkv.astype(jnp.bfloat16), "ctx").astype(jnp.float32),
        lax.psum(part_attn.astype(jnp.bfloat16), "ctx").astype(jnp.float32),
        lax.psum(part_g2.astype(jnp.bfloat16), "ctx").astype(jnp.float32),
        lax.psum(part_in.astype(jnp.bfloat16), "ctx").astype(jnp.float32),
        lax.psum(part_ffn.astype(jnp.bfloat16), "ctx").astype(jnp.float32),
    )
    return (
        output.reshape(seq_dev, tok_seq, D),
        grad_input.reshape(seq_dev, tok_seq, D),
        totals[0],
        totals[1],
        totals[2],
        totals[3],
        totals[4],
        totals[5],
    )


RING = 8
OWNERS = 4
PAIR = 2 * HEAD_DIM
UNITS = FF // RING
UNITS_PAD = 384
UNIT_ROWS = 336
WINDOW = 512
ATTN_ROWS = 128
MESH = pl.DeviceIdType.MESH
VMEM_BYTES = 60 * 1024 * 1024
F32 = jnp.float32
BF16 = jnp.bfloat16


def contract(left, right, left_dim, right_dim):
    return lax.dot_general(
        left, right, (((left_dim,), (right_dim,)), ((), ())), preferred_element_type=F32
    )


class Here:
    def __init__(self):
        b, f = lax.axis_index("ctx"), lax.axis_index("fsdp")
        x, low = b % 2, (b // 2) % 2
        self.b, self.f = b, f
        self.c, self.y, self.q, self.high, self.x, self.low = f % 2, f // 2, b % 4, b // 4, x, low
        self.bx, self.bz = b + 1 - 2 * x, b + 2 - 4 * low
        self.bd, self.bh = self.bx + 2 - 4 * low, (b + 4) % RING
        self.qx, self.qz = self.q + 1 - 2 * x, self.q + 2 - 4 * low
        self.qd = self.qx + 2 - 4 * low
        self.core = f + 1 - 2 * self.c
        self.far = (f + 2) % OWNERS
        self.diag = (self.core + 2) % OWNERS
        self.p = self.c * 4 + self.q

    def mine(self, q):
        return self.c * 4 + q

    def other(self, q):
        return (1 - self.c) * 4 + q

    def mine_of(self, c):
        return c * 4 + self.q

    def greet(self):
        barrier = pltpu.get_barrier_semaphore()
        peers = [(b, f) for b in (self.b, self.bx, self.bz, self.bd) for f in (self.f, self.core)]
        peers = peers[1:] + [
            (self.b, self.far), (self.b, self.diag), (self.bh, self.f), (self.bh, self.core),
        ]
        for peer in peers:
            pl.semaphore_signal(barrier, inc=1, device_id=peer, device_id_type=MESH)
        pl.semaphore_wait(barrier, len(peers))


def push(src, dst, send, recv, device):
    return pltpu.make_async_remote_copy(
        src_ref=src, dst_ref=dst, send_sem=send, recv_sem=recv, device_id=device, device_id_type=MESH
    )


class Gather:
    def __init__(self, here, buf, send, recv):
        h = here
        self.h, self.send_sem, self.recv_sem = h, send, recv
        half = buf.shape[1] // 2
        top, bottom = pl.ds(0, half), pl.ds(half, half)
        own, near_x, near_z = buf.at[h.p], buf.at[h.mine(h.qx)], buf.at[h.mine(h.qz)]
        across = buf.at[h.mine(h.qd)]
        to_x, to_z, to_core = (h.bx, h.f), (h.bz, h.f), (h.b, h.core)
        self.out = [
            (own, to_x), (own, to_z), (near_z.at[top], to_x), (near_x.at[bottom], to_z),
            (own, to_core), (near_x, to_core), (near_z, to_core), (across, to_core),
        ]
        self.inn = [
            near_x, near_z, across.at[top], across.at[bottom],
            buf.at[h.other(h.q)], buf.at[h.other(h.qx)], buf.at[h.other(h.qz)], buf.at[h.other(h.qd)],
        ]

    def copy(self, kind):
        ref, device = self.out[kind]
        return push(ref, ref, self.send_sem.at[kind], self.recv_sem.at[kind], device)

    def wait(self, kind):
        ref = self.inn[kind]
        device = self.out[kind][1]
        push(ref, ref, self.send_sem.at[kind], self.recv_sem.at[kind], device).wait_recv()

    def begin(self):
        for kind in (0, 1, 4):
            self.copy(kind).start()

    def near(self):
        self.wait(0)
        self.copy(3).start()
        self.copy(5).start()
        self.wait(1)
        self.copy(2).start()
        self.copy(6).start()

    def across(self):
        self.wait(2)
        self.wait(3)
        self.copy(7).start()

    def sent(self):
        for kind in range(8):
            self.copy(kind).wait_send()

    def each(self, work, meanwhile=None, late=False):
        h = self.h
        work(h.p)
        self.wait(4)
        work(h.other(h.q))
        self.near()
        work(h.mine(h.qx))
        work(h.mine(h.qz))
        if meanwhile is not None and not late:
            meanwhile()
        self.wait(5)
        work(h.other(h.qx))
        self.wait(6)
        work(h.other(h.qz))
        self.across()
        if late:
            meanwhile()
        work(h.mine(h.qd))
        self.wait(7)
        work(h.other(h.qd))


class Scatter:
    def __init__(self, here, terms, core_out, near_out, across_out, core_in, near_in, across_in, send, recv):
        h = here
        self.h, self.terms, self.send_sem, self.recv_sem = h, terms, send, recv
        self.core_out, self.near_out, self.across_out = core_out, near_out, across_out
        self.core_in, self.near_in, self.across_in = core_in, near_in, across_in
        to_x, to_z, to_core = (h.bx, h.f), (h.bz, h.f), (h.b, h.core)
        self.out = [(core_out.at[i], core_in.at[i], to_core) for i in range(4)] + [
            (across_out.at[0], across_in.at[0], to_x),
            (across_out.at[1], across_in.at[1], to_z),
            (near_out.at[0], near_in.at[0], to_x),
            (near_out.at[1], near_in.at[1], to_z),
        ]
        self.half = terms.shape[1] // 2

    def copy(self, kind):
        src, dst, device = self.out[kind]
        return push(src, dst, self.send_sem.at[kind], self.recv_sem.at[kind], device)

    def wait(self, kind):
        self.copy(kind).wait_recv()

    def begin(self):
        h = self.h
        for i, q in enumerate((h.qd, h.qz, h.qx, h.q)):
            self.core_out[i] = self.terms[h.other(q)].astype(BF16)
            self.copy(i).start()

    def pair(self, i, q):
        return self.terms[self.h.mine(q)] + self.core_in[i].astype(F32)

    def first(self):
        self.wait(0)
        part = self.pair(0, self.h.qd).astype(BF16)
        self.across_out[0] = part[: self.half]
        self.copy(4).start()
        self.across_out[1] = part[self.half :]
        self.copy(5).start()

    def second(self):
        half = self.half
        self.wait(2)
        self.wait(5)
        part = self.pair(2, self.h.qx)
        self.near_out[0, :half] = part[:half].astype(BF16)
        self.near_out[0, half:] = (part[half:] + self.across_in[1].astype(F32)).astype(BF16)
        self.copy(6).start()
        self.wait(1)
        self.wait(4)
        part = self.pair(1, self.h.qz)
        self.near_out[1, :half] = (part[:half] + self.across_in[0].astype(F32)).astype(BF16)
        self.near_out[1, half:] = part[half:].astype(BF16)
        self.copy(7).start()

    def finish(self):
        self.wait(3)
        total = self.pair(3, self.h.q)
        self.wait(6)
        self.wait(7)
        total = total + self.near_in[0].astype(F32) + self.near_in[1].astype(F32)
        for kind in range(8):
            self.copy(kind).wait_send()
        return total


class Grads:
    def __init__(self, here, g, far_in, high_in, core_out, whole, send, recv, split=False):
        h = here
        self.kinds = 7 if split else 6
        high = g.shape[2]
        top = high // 32 * 16 if split else high
        self.h, self.g, self.far_in, self.high_in = h, g, far_in, high_in
        self.core_out, self.whole, self.send_sem, self.recv_sem = core_out, whole, send, recv
        self.out = [
            (g.at[1 - h.y], far_in, (h.b, h.far)),
            (g.at[h.y], high_in, (h.bh, h.f)),
            (core_out, whole.at[h.q, h.c], (h.b, h.core)),
            (whole.at[h.q], whole.at[h.q], (h.bx, h.f)),
            (whole.at[h.q], whole.at[h.q], (h.bz, h.f)),
        ]
        for q, device, rows in (
            (h.qz, (h.bx, h.f), pl.ds(0, top)), (h.qx, (h.bz, h.f), pl.ds(top, high - top)),
        )[: self.kinds - 5]:
            self.out.append((whole.at[q, :, rows], whole.at[q, :, rows], device))
        self.inn = [far_in, high_in, whole.at[h.q, 1 - h.c], whole.at[h.qx], whole.at[h.qz]]
        for rows in (pl.ds(0, top), pl.ds(top, high - top))[: self.kinds - 5]:
            self.inn.append(whole.at[h.qd, :, rows])

    def copy(self, kind):
        src, dst, device = self.out[kind]
        return push(src, dst, self.send_sem.at[kind], self.recv_sem.at[kind], device)

    def wait(self, kind):
        ref, device = self.inn[kind], self.out[kind][2]
        push(ref, ref, self.send_sem.at[kind], self.recv_sem.at[kind], device).wait_recv()

    def to_far(self):
        self.copy(0).start()

    def from_far(self):
        self.wait(0)
        y = self.h.y
        self.g[y] = (self.g[y].astype(F32) + self.far_in[...].astype(F32)).astype(BF16)

    def to_high(self):
        self.copy(1).start()

    def total(self, c):
        return (self.g[self.h.y, c].astype(F32) + self.high_in[c].astype(F32)).astype(BF16)

    def to_core(self):
        self.wait(1)
        h = self.h
        self.core_out[...] = self.total(1 - h.c)
        self.copy(2).start()
        self.whole[h.q, h.c] = self.total(h.c)

    def to_near(self):
        self.wait(2)
        self.copy(3).start()
        self.copy(4).start()

    def to_across(self):
        self.wait(4)
        self.copy(5).start()
        self.wait(3)
        if self.kinds == 7:
            self.copy(6).start()

    def finish(self):
        for kind in range(5, self.kinds):
            self.wait(kind)

    def sent(self):
        for kind in range(self.kinds):
            self.copy(kind).wait_send()


class Rows:
    def __init__(self, here, whole, rows, send, recv):
        self.h, self.whole, self.rows, self.send_sem, self.recv_sem = here, whole, rows, send, recv

    def place(self, half, owner):
        return self.rows.at[half, :, pl.ds(pl.multiple_of(owner * 256, 256), 256)]

    def copy(self, q, c):
        h = self.h
        return push(
            self.whole.at[q, c], self.place(q % 2, h.f),
            self.send_sem.at[q, c], self.recv_sem.at[h.f, q % 2], (h.b, 2 * c + q // 2),
        )

    def begin(self):
        h = self.h
        for q in range(4):
            for c in range(2):
                owner = 2 * c + q // 2

                @pl.when(h.f != owner)
                def _(q=q, c=c):
                    self.copy(q, c).start()

                @pl.when(h.f == owner)
                def _(q=q, c=c, owner=owner):
                    self.rows[q % 2, :, owner * 256 : (owner + 1) * 256] = self.whole[q, c]

    def finish(self):
        h = self.h
        for owner in range(OWNERS):

            @pl.when(h.f != owner)
            def _(owner=owner):
                for half in range(2):
                    ref = self.place(half, owner)
                    push(
                        ref, ref, self.send_sem.at[0, 0], self.recv_sem.at[owner, half],
                        (h.b, owner),
                    ).wait_recv()

        for q in range(4):
            for c in range(2):

                @pl.when(h.f != 2 * c + q // 2)
                def _(q=q, c=c):
                    self.copy(q, c).wait_send()


def row_norm(rows):
    mean = jnp.mean(rows, axis=-1, keepdims=True)
    centred = rows - mean
    inv = lax.rsqrt(jnp.mean(centred * centred, axis=-1, keepdims=True) + EPSILON)
    return centred * inv, inv


def row_back(grad, normed, inv):
    return inv * (
        grad
        - jnp.mean(grad, axis=-1, keepdims=True)
        - normed * jnp.mean(grad * normed, axis=-1, keepdims=True)
    )


def first_half():
    lane = lax.broadcasted_iota(jnp.int32, (1, PAIR), 1)
    return lane % HEAD_DIM < HEAD_DIM // 2


def first_head():
    return lax.broadcasted_iota(jnp.int32, (1, PAIR), 1) < HEAD_DIM


def swap_halves(rows):
    up = pltpu.roll(rows, PAIR - HEAD_DIM // 2, 1)
    down = pltpu.roll(rows, HEAD_DIM // 2, 1)
    return jnp.where(first_half(), up, down)


def only(rows, head):
    keep = first_head() if head == 0 else jnp.logical_not(first_head())
    return jnp.where(keep, rows, jnp.zeros_like(rows))


def quarter(ref, j):
    tile = ref[:, :, j * 256 : (j + 1) * 256]
    return tile.reshape(tile.shape[0] * tile.shape[1], 256)


def flat(ref):
    rows = ref[...]
    return rows.reshape(rows.shape[0] * rows.shape[1], rows.shape[2])


class Box:
    pass


IN_HBM = ("w_qkv", "w_in", "w_ffn")
GATHERS = ("xg", "cg", "ag", "rg")
SCATTERS = ("two", "out", "one")
CHUNKS = (
    ("ffn", UNIT_ROWS), ("ing", UNIT_ROWS), ("inz", UNIT_ROWS),
    ("att", ATTN_ROWS), ("que", ATTN_ROWS), ("key", ATTN_ROWS), ("val", ATTN_ROWS),
)


def layout(seqs, tok):
    rows, length = seqs * tok, tok * RING
    whole = (RING, rows, D)
    half = rows // 2
    ins = [
        "x", "cot", "gain", "w_qkv", "attn_w", "w_in", "w_ffn", "cos", "sin",
    ]
    outs = {
        "output": ((rows, D), BF16),
        "grad_x": ((rows, D), F32),
        "gains": ((8, 256), F32),
        "ffn_rows": ((2, UNIT_ROWS, D), BF16),
        "att_rows": ((2, ATTN_ROWS, D), BF16),
    }
    for name, high in CHUNKS:
        if name not in ("ffn", "att"):
            outs[name + "_all"] = ((4, 2, high, 256), BF16)
    sem = pltpu.SemaphoreType.DMA
    vm = pltpu.VMEM
    scratch = {
        "xs": vm(whole, BF16), "cots": vm(whole, BF16), "a1": vm(whole, BF16), "a2": vm(whole, BF16),
        "resids": vm(whole, BF16), "terms": vm(whole, F32),
        "qkv_w": vm((2, 256, 3 * PAIR), BF16), "in_w": vm((2, 256, 2 * UNITS_PAD), BF16),
        "ffn_w": vm((UNIT_ROWS, D), BF16), "windows": vm((2, 2, 256, WINDOW), BF16),
        "gain_all": vm((8, D), F32), "qkv_c": vm((D, 3 * PAIR), BF16), "attn_all": vm((D, D), BF16),
        "in_c": vm((D, 2 * UNITS_PAD), BF16), "ffn_c": vm((UNITS_PAD, D), BF16),
        "qs": vm((seqs, length, PAIR), BF16), "ks": vm((seqs, length, PAIR), BF16),
        "vs": vm((seqs, length, PAIR), BF16), "os": vm((seqs, length, PAIR), F32),
        "lse": vm((seqs, length, PAIR), F32), "heads": vm((RING, rows, PAIR), BF16),
        "own_heads": vm((RING, rows, PAIR), BF16), "mixed": vm((RING, rows, PAIR), BF16),
        "joint": vm((RING, rows, 3 * PAIR), BF16),
        "fs": vm((RING, rows, UNITS_PAD), BF16), "dus": vm((RING, rows, 2 * UNITS_PAD), BF16),
        "n2": vm((rows, D), F32), "resid": vm((rows, D), F32), "dy": vm((rows, D), F32),
        "core_out": vm((4, rows, D), BF16), "near_out": vm((2, rows, D), BF16),
        "across_out": vm((2, half, D), BF16),
        "back_out": vm((2, rows, D), BF16), "back_in": vm((2, rows, D), BF16),
        "sums": vm((6, 8, D), F32), "sums_in": vm((5, 8, D), F32),
        "ffn_all": vm((4, 2, UNIT_ROWS, 256), BF16), "att_all": vm((4, 2, ATTN_ROWS, 256), BF16),
    }
    for name in GATHERS:
        scratch[name + "_sems"] = (sem((8,)), sem((8,)))
    for name in SCATTERS:
        scratch[name + "_core"] = vm((4, rows, D), BF16)
        scratch[name + "_near"] = vm((2, rows, D), BF16)
        scratch[name + "_across"] = vm((2, half, D), BF16)
        scratch[name + "_sems"] = (sem((8,)), sem((8,)))
    for name, high in CHUNKS:
        scratch[name + "_g"] = vm((2, 2, high, 256), BF16)
        scratch[name + "_far"] = vm((2, high, 256), BF16)
        scratch[name + "_high"] = vm((2, high, 256), BF16)
        scratch[name + "_core"] = vm((high, 256), BF16)
        scratch[name + "_sems"] = (sem((7,)), sem((7,)))
    for name, count in (("swap", 4), ("part", 9), ("attn", 5), ("head", RING - 1), ("sum", 5)):
        scratch[name + "_sems"] = (sem((count,)), sem((count,)))
    scratch["ffn_w_sems"] = (sem((2,)), sem((1,)))
    scratch["cut_sems"] = (sem((2, 3)), sem((2, 2)), sem((1,)))
    for name in ("ffn_rows", "att_rows"):
        scratch[name + "_sems"] = (sem((4, 2)), sem((4, 2)))
    return ins, outs, scratch


def layer_kernel(names, *refs):
    r = Box()
    for name, ref in zip(names, refs):
        setattr(r, name, ref)
    h = Here()
    seqs, length = r.qs.shape[0], r.qs.shape[1]
    tok = length // RING
    scale = HEAD_DIM ** (-0.5)
    moved = h.high != h.c
    there = (h.bh, h.core)
    there_p = h.high * 4 + h.q
    cut_q, cut_i, cut_f = r.cut_sems

    def cut_qkv(c, i):
        start = i * D + h.mine_of(c) * PAIR
        return pltpu.make_async_copy(
            r.w_qkv.at[:, pl.ds(pl.multiple_of(start, PAIR), PAIR)],
            r.qkv_w.at[c, :, i * PAIR : (i + 1) * PAIR], cut_q.at[c, i],
        )

    def window(c, i):
        start = i * FF + h.mine_of(c) * UNITS
        return start, jnp.minimum(start // PAIR * PAIR, 2 * FF - WINDOW)

    def cut_in(c, i):
        return pltpu.make_async_copy(
            r.w_in.at[:, pl.ds(pl.multiple_of(window(c, i)[1], PAIR), WINDOW)],
            r.windows.at[c, i], cut_i.at[c, i],
        )

    cut_ffn = pltpu.make_async_copy(
        r.w_ffn.at[pl.ds(pl.multiple_of(h.x * (UNITS - 8), 16), UNIT_ROWS)], r.ffn_w, cut_f.at[0]
    )
    for c in range(2):
        for i in range(3):
            cut_qkv(c, i).start()
    for c in range(2):
        for i in range(2):
            cut_in(c, i).start()
    cut_ffn.start()

    h.greet()

    def swap(i, src, dst, back):
        send, recv = r.swap_sems
        return push(src, dst, send.at[i], recv.at[i], there)

    def swap_in(i, src, whole):
        @pl.when(moved)
        def _():
            swap(i, src, whole.at[there_p], False).start()

        @pl.when(jnp.logical_not(moved))
        def _():
            whole[h.p] = src[...]

    def swap_got(i, src, whole):
        @pl.when(moved)
        def _():
            swap(i, whole.at[h.p], whole.at[h.p], False).wait_recv()

    def swap_sent(i, src, whole):
        @pl.when(moved)
        def _():
            swap(i, src, whole.at[there_p], False).wait_send()

    swap_in(0, r.x, r.xs)

    p_send, p_recv = r.part_sems
    peers = (h.far, h.core, h.diag)

    def part_at(whole, owner, lanes):
        if lanes:
            return whole.at[:, pl.ds(pl.multiple_of(owner * 256, 256), 256)]
        return whole.at[pl.ds(pl.multiple_of(owner * 256, 256), 256)]

    def part(i, src, whole, lanes, sliced):
        def copy(k):
            mine = (h.c, 1 - h.c, 1 - h.c)[k]
            return push(
                src.at[mine] if sliced else src, part_at(whole, h.f, lanes),
                p_send.at[3 * i + k], p_recv.at[3 * i + k], (h.b, peers[k]),
            )

        box = Box()

        def begin():
            for k in range(3):
                copy(k).start()
            place = part_at(whole, h.f, lanes)
            place[...] = src[h.c] if sliced else src[...]

        def got():
            for k in range(3):
                ref = part_at(whole, peers[k], lanes)
                push(ref, ref, p_send.at[3 * i + k], p_recv.at[3 * i + k], (h.b, peers[k])).wait_recv()

        def sent():
            for k in range(3):
                copy(k).wait_send()

        box.begin, box.got, box.sent = begin, got, sent
        return box

    gain_p = part(0, r.gain, r.gain_all, True, False)
    qkv_p = part(1, r.qkv_w, r.qkv_c, False, True)
    in_p = part(2, r.in_w, r.in_c, False, True)

    def attn_half(owner, half):
        return r.attn_all.at[pl.ds(pl.multiple_of(owner * 256 + half * 128, 128), 128)]

    def attn_copy(k):
        own_half = pl.ds(pl.multiple_of(h.x * 128, 128), 128)
        came, later = attn_half(h.far, h.x), attn_half(h.far, 1 - h.x)
        src, dst, device = (
            (r.attn_w.at[own_half], attn_half(h.f, h.x), (h.b, h.far)),
            (r.attn_w, part_at(r.attn_all, h.f, False), (h.b, h.core)),
            (came, came, (h.bx, h.f)),
            (came, came, (h.b, h.core)),
            (later, later, (h.b, h.core)),
        )[k]
        return push(src, dst, a_send.at[k], a_recv.at[k], device)

    def attn_wait(k):
        ref = (
            attn_half(h.far, h.x), part_at(r.attn_all, h.core, False), attn_half(h.far, 1 - h.x),
            attn_half(h.diag, h.x), attn_half(h.diag, 1 - h.x),
        )[k]
        push(ref, ref, a_send.at[k], a_recv.at[k], (h.b, h.core)).wait_recv()

    a_send, a_recv = r.attn_sems
    f_send, f_recv = r.ffn_w_sems
    active = h.c == h.low
    near_own = 2 * h.y + h.y
    far_own = 2 * (1 - h.y) + h.y
    ffn_owner = 2 * h.c + h.low
    unit_rows = pl.ds(0, UNIT_ROWS)

    def ffn_copy(k):
        return push(
            r.ffn_w.at[unit_rows], r.ffn_c.at[unit_rows],
            f_send.at[k], f_recv.at[0], (h.b, (near_own, far_own)[k]),
        )

    gain_p.begin()
    for c in range(2):
        for i in range(3):
            cut_qkv(c, i).wait()
    qkv_p.begin()
    lane = lax.broadcasted_iota(jnp.int32, (1, WINDOW), 1)
    inside = jnp.logical_and(lane >= 8 * h.x, lane < 8 * h.x + UNITS)
    for c in range(2):
        for i in range(2):
            cut_in(c, i).wait()
            start, left = window(c, i)
            turned = pltpu.roll(
                r.windows[c, i].astype(F32), lax.rem(left - start + 8 * h.x + WINDOW, WINDOW), 1
            )
            kept = jnp.where(inside, turned, 0.0)[:, :UNITS_PAD]
            r.in_w[c, :, i * UNITS_PAD : (i + 1) * UNITS_PAD] = kept.astype(BF16)
    cut_ffn.wait()
    swap_got(0, r.x, r.xs)
    swap_in(1, r.cot, r.cots)
    xg = Gather(h, r.xs, *r.xg_sems)
    xg.begin()
    cg = Gather(h, r.cots, *r.cg_sems)

    @pl.when(jnp.logical_not(moved))
    def _():
        cg.begin()

    gain_p.got()
    qkv_p.got()
    attn_copy(0).start()
    attn_copy(1).start()
    at_own = part_at(r.attn_all, h.f, False)
    at_own[...] = r.attn_w[...]
    r.ffn_c[UNIT_ROWS:, :] = jnp.zeros((UNITS_PAD - UNIT_ROWS, D), BF16)

    @pl.when(ffn_owner == h.f)
    def _():
        r.ffn_c[unit_rows, :] = r.ffn_w[unit_rows, :]

    def project(index):
        normed, _ = row_norm(r.xs[index].astype(F32))
        a1 = (normed * r.gain_all[0:1, :]).astype(BF16)
        r.a1[index] = a1
        r.terms[index, :, : 3 * PAIR] = contract(a1, r.qkv_c[...], 1, 0)

    def more_weights():
        attn_wait(0)
        attn_copy(2).start()
        attn_copy(3).start()
        in_p.begin()

        @pl.when(active)
        def _():
            ffn_copy(1).start()

        @pl.when(jnp.logical_and(active, near_own != h.f))
        def _():
            ffn_copy(0).start()

        @pl.when(moved)
        def _():
            swap(1, r.cots.at[h.p], r.cots.at[h.p], False).wait_recv()
            cg.begin()

    xg.each(project, more_weights, True)

    for s in range(seqs):
        rows = slice(s * tok, (s + 1) * tok)

        def columns(i):
            return r.terms[:, rows, i * PAIR : (i + 1) * PAIR].reshape(length, PAIR)

        cos, sin = r.cos[...], r.sin[...]
        query, key = columns(0), columns(1)
        q = (query * cos + swap_halves(query) * sin).astype(BF16)
        k = (key * cos + swap_halves(key) * sin).astype(BF16)
        v = columns(2).astype(BF16)
        r.qs[s] = q
        r.ks[s] = k
        r.vs[s] = v
        outs, lses = [], []
        for head in range(2):
            scores = contract(only(q, head), k, 1, 1) * scale
            top = jnp.max(scores, axis=-1, keepdims=True)
            e = jnp.exp(scores - top)
            total = jnp.sum(e, axis=-1, keepdims=True)
            outs.append(contract(e.astype(BF16), v, 1, 0) / total)
            lses.append(top + jnp.log(total))
        of = jnp.where(first_head(), outs[0], outs[1])
        r.os[s] = of
        r.lse[s] = jnp.where(first_head(), lses[0], lses[1])
        r.heads[:, rows, :] = of.astype(BF16).reshape(RING, tok, PAIR)

    h_send, h_recv = r.head_sems
    around = []
    for b, q in ((h.b, h.q), (h.bx, h.qx), (h.bz, h.qz), (h.bd, h.qd)):
        around += [((b, h.f), h.mine(q)), ((b, h.core), h.other(q))]

    def exchange(i):
        device, p = around[i + 1]
        return push(r.heads.at[p], r.own_heads.at[h.p], h_send.at[i], h_recv.at[i], device)

    for i in range(RING - 1):
        exchange(i).start()
    r.own_heads[h.p] = r.heads[h.p]
    cg.near()
    attn_wait(2)
    attn_copy(4).start()
    attn_wait(1)
    attn_wait(3)
    attn_wait(4)
    for i in range(RING - 1):
        device, p = around[i + 1]
        ref = r.own_heads.at[p]
        push(ref, ref, h_send.at[i], h_recv.at[i], device).wait_recv()

    g2 = r.gain_all[1:2, :]
    mixed_heads = jnp.concatenate([r.own_heads[d] for d in range(RING)], axis=1)
    resid = r.xs[h.p].astype(F32) + contract(mixed_heads, r.attn_all[...], 1, 0)
    r.resid[...] = resid
    normed, inv_two = row_norm(resid)
    r.n2[...] = normed
    r.a2[h.p] = (normed * g2).astype(BF16)
    ag = Gather(h, r.a2, *r.ag_sems)
    ag.begin()
    cg.across()
    in_p.got()

    @pl.when(ffn_owner != h.f)
    def _():
        ffn_copy(0).wait_recv()

    for kind in range(4, 8):
        cg.wait(kind)

    def feed(index):
        widened = contract(r.a2[index], r.in_c[...], 1, 0)
        inner, gating = widened[:, :UNITS_PAD], widened[:, UNITS_PAD:]
        below = 0.5 * (1.0 + lax.erf(inner * 0.7071067811865476))
        density = jnp.exp(-0.5 * inner * inner) * 0.3989422804014327
        active = inner * below
        r.fs[index] = (active * gating).astype(BF16)
        grad_hidden = contract(r.cots[index], r.ffn_c[...], 1, 1)
        du = jnp.concatenate(
            [grad_hidden * gating * (below + inner * density), grad_hidden * active], axis=1
        ).astype(BF16)
        r.dus[index] = du
        r.terms[index] = contract(du, r.in_c[...], 1, 1)

    ag.each(feed)

    def scatter(name):
        return Scatter(
            h, r.terms, r.core_out, r.near_out, r.across_out,
            getattr(r, name + "_core"), getattr(r, name + "_near"), getattr(r, name + "_across"),
            *getattr(r, name + "_sems"),
        )

    ch = {}
    for name, _ in CHUNKS:
        ch[name] = Grads(
            h, getattr(r, name + "_g"), getattr(r, name + "_far"), getattr(r, name + "_high"),
            getattr(r, name + "_core"), getattr(r, name + "_all"), *getattr(r, name + "_sems"),
            name not in ("ffn", "ing"),
        )

    ffn, ing, inz, att = ch["ffn"], ch["ing"], ch["inz"], ch["att"]
    que, key, val = ch["que"], ch["key"], ch["val"]
    two = scatter("two")
    two.begin()
    for j in range(OWNERS):
        r.ffn_g[j // 2, j % 2] = contract(flat(r.fs), quarter(r.cots, j), 0, 0)[:UNIT_ROWS].astype(BF16)
    ffn.to_far()
    two.first()
    for j in range(OWNERS):
        c, y = j % 2, j // 2
        grad_in = contract(flat(r.dus), quarter(r.a2, j), 0, 0).astype(BF16)
        r.ing_g[y, c] = grad_in[:UNIT_ROWS]
        r.inz_g[y, c] = grad_in[UNITS_PAD : UNITS_PAD + UNIT_ROWS]
        if j == 1:
            two.second()
    ffn.from_far()
    ffn.to_high()
    ing.to_far()
    grad_two = two.finish()

    normed = r.n2[...]
    r.sums[0, 1:2, :] = jnp.sum(grad_two * normed, axis=0, keepdims=True)
    own_grad = r.cots[h.p].astype(F32) + row_back(grad_two * g2, normed, inv_two)
    r.dy[...] = own_grad
    r.resids[h.p] = own_grad.astype(BF16)
    rg = Gather(h, r.resids, *r.rg_sems)
    rg.begin()

    attn_c = r.attn_all.at[pl.ds(pl.multiple_of(h.p * PAIR, PAIR), PAIR)]

    def mix(index):
        r.mixed[index] = contract(r.resids[index], attn_c[...], 1, 1).astype(BF16)

    def ing_far():
        ing.from_far()
        inz.to_far()

    rg.each(mix, ing_far)
    ffn.to_core()
    ing.to_high()
    for j in range(OWNERS):
        r.att_g[j // 2, j % 2] = contract(flat(r.heads), quarter(r.resids, j), 0, 0).astype(BF16)
    ffn.to_near()

    for s in range(seqs):
        rows = slice(s * tok, (s + 1) * tok)
        q, k, v = r.qs[s], r.ks[s], r.vs[s]
        do = r.mixed[:, rows, :].reshape(length, PAIR)
        weighed = do.astype(F32) * r.os[s]
        dqs, dks, dvs = [], [], []
        for head in range(2):
            delta = jnp.sum(only(weighed, head), axis=-1, keepdims=True)
            lse = r.lse[s, :, head * HEAD_DIM : head * HEAD_DIM + 1]
            probs = jnp.exp(contract(only(q, head), k, 1, 1) * scale - lse)
            dvs.append(contract(probs.astype(BF16), do, 0, 0))
            grad_probs = contract(only(do, head), v, 1, 1)
            ds = (probs * (grad_probs - delta)).astype(BF16)
            dqs.append(contract(ds, k, 1, 0) * scale)
            dks.append(contract(ds, q, 0, 0) * scale)
        cos, sin = r.cos[...], r.sin[...]
        dq = jnp.where(first_head(), dqs[0], dqs[1])
        dk = jnp.where(first_head(), dks[0], dks[1])
        dv = jnp.where(first_head(), dvs[0], dvs[1])
        for i, item in enumerate(
            (dq * cos - swap_halves(dq) * sin, dk * cos - swap_halves(dk) * sin, dv)
        ):
            r.joint[:, rows, i * PAIR : (i + 1) * PAIR] = item.astype(BF16).reshape(RING, tok, PAIR)
        if s == 0:
            inz.from_far()
            att.to_far()

    def term(i, carry):
        r.terms[i] = contract(r.joint[i], r.qkv_c[...], 1, 1)
        return carry

    lax.fori_loop(0, RING, term, 0)
    one = scatter("one")
    one.begin()
    for j in range(OWNERS):
        grad_qkv = contract(flat(r.joint), quarter(r.a1, j), 0, 0).astype(BF16)
        for i, name in enumerate(("que", "key", "val")):
            getattr(r, name + "_g")[j // 2, j % 2] = grad_qkv[i * PAIR : (i + 1) * PAIR]
        if j == 0:
            one.first()
        if j == 2:
            one.second()
    att.from_far()
    for item in (que, key, val):
        item.to_far()
    ing.to_core()
    inz.to_high()
    ffn.to_across()

    grad_one = one.finish()
    normed, inv_one = row_norm(r.xs[h.p].astype(F32))
    r.sums[0, 0:1, :] = jnp.sum(grad_one * normed, axis=0, keepdims=True)
    r.sums[0, 2:, :] = jnp.zeros((6, D), F32)
    s_send, s_recv = r.sum_sems
    partners = ((h.b, h.core), (h.b, h.far), (h.bx, h.f), (h.bz, h.f), (h.bh, h.f))

    def sum_copy(i):
        return push(r.sums.at[i], r.sums_in.at[i], s_send.at[i], s_recv.at[i], partners[i])

    def sum_step(i):
        sum_copy(i).wait_recv()
        r.sums[i + 1] = r.sums[i] + r.sums_in[i]
        if i < 4:
            sum_copy(i + 1).start()

    def back(i):
        return swap(2 + i, r.back_out.at[i], r.back_in.at[i], True)

    sum_copy(0).start()
    grad_x = r.dy[...] + row_back(grad_one * r.gain_all[0:1, :], normed, inv_one)
    r.grad_x[...] = grad_x
    r.back_out[1] = grad_x.astype(BF16)

    @pl.when(moved)
    def _():
        back(1).start()

    ing.to_near()

    def out_term(i, carry):
        r.terms[i] = contract(r.fs[i], r.ffn_c[...], 1, 0)
        return carry

    lax.fori_loop(0, RING, out_term, 0)
    out = scatter("out")
    out.begin()
    sum_step(0)
    for item in (que, key, val):
        item.from_far()
    out.first()
    sum_step(1)
    ing.to_across()
    inz.to_core()
    att.to_high()
    que.to_high()
    inz.to_near()
    out.second()
    sum_step(2)
    ffn.finish()
    ffn_rows = Rows(h, r.ffn_all, r.ffn_rows, *r.ffn_rows_sems)
    ffn_rows.begin()
    att.to_core()
    key.to_high()
    val.to_high()
    sum_step(3)
    att.to_near()
    que.to_core()
    que.to_near()
    inz.to_across()
    r.back_out[0] = (r.resid[...] + out.finish()).astype(BF16)

    @pl.when(moved)
    def _():
        back(0).start()

    sum_step(4)
    r.gains[...] = r.sums[5, :, pl.ds(pl.multiple_of(h.f * 256, 256), 256)]
    att.to_across()
    key.to_core()
    key.to_near()
    que.to_across()
    val.to_core()
    val.to_near()
    att.finish()
    att_rows = Rows(h, r.att_all, r.att_rows, *r.att_rows_sems)
    att_rows.begin()
    key.to_across()
    val.to_across()

    @pl.when(moved)
    def _():
        for i in range(2):
            back(i).wait_recv()
            back(i).wait_send()
        r.output[...] = r.back_in[0]
        r.grad_x[...] = r.back_in[1].astype(F32)

    @pl.when(jnp.logical_not(moved))
    def _():
        r.output[...] = r.back_out[0]

    for name in ("ing", "inz", "que", "key", "val"):
        ch[name].finish()
    ffn_rows.finish()
    att_rows.finish()

    swap_sent(0, r.x, r.xs)
    swap_sent(1, r.cot, r.cots)
    for item in (xg, cg, ag, rg):
        item.sent()
    for item in (gain_p, qkv_p, in_p):
        item.sent()
    for k in range(5):
        attn_copy(k).wait_send()

    @pl.when(active)
    def _():
        ffn_copy(1).wait_send()

    @pl.when(jnp.logical_and(active, near_own != h.f))
    def _():
        ffn_copy(0).wait_send()

    for i in range(RING - 1):
        exchange(i).wait_send()
    for i in range(5):
        sum_copy(i).wait_send()
    for name, _ in CHUNKS:
        ch[name].sent()


def finish_kernel(ing, inz, que, key, val, ffn, att, in_o, qkv_o, ffn_o, att_o):
    for q in range(4):
        for c in range(2):
            p = 4 * c + q
            for i, ref in enumerate((ing, inz)):
                start = i * FF + p * UNITS
                first = 8 * (q % 2)
                in_o[:, start : start + UNITS] = ref[q, c].astype(F32).T[:, first : first + UNITS]
            for i, ref in enumerate((que, key, val)):
                start = i * D + p * PAIR
                qkv_o[:, start : start + PAIR] = ref[q, c].astype(F32).T
    for half in range(2):
        first = 8 * half
        ffn_o[half * UNITS : (half + 1) * UNITS, :] = ffn[half].astype(F32)[first : first + UNITS]
        att_o[half * ATTN_ROWS : (half + 1) * ATTN_ROWS, :] = att[half].astype(F32)


def finish(ing, inz, que, key, val, ffn, att):
    def slices(high):
        return pl.BlockSpec((4, 2, high, 128), lambda i: (0, 0, 0, i))

    def rows(high):
        return pl.BlockSpec((2, high, D // 2), lambda i: (0, 0, i))

    return pl.pallas_call(
        finish_kernel,
        grid=(2,),
        out_shape=[
            jax.ShapeDtypeStruct((256, 2 * FF), F32),
            jax.ShapeDtypeStruct((256, 3 * D), F32),
            jax.ShapeDtypeStruct((2 * UNITS, D), F32),
            jax.ShapeDtypeStruct((2 * ATTN_ROWS, D), F32),
        ],
        in_specs=[slices(UNIT_ROWS)] * 2 + [slices(ATTN_ROWS)] * 3 + [rows(UNIT_ROWS), rows(ATTN_ROWS)],
        out_specs=[
            pl.BlockSpec((128, 2 * FF), lambda i: (i, 0)),
            pl.BlockSpec((128, 3 * D), lambda i: (i, 0)),
            pl.BlockSpec((2 * UNITS, D // 2), lambda i: (0, i)),
            pl.BlockSpec((2 * ATTN_ROWS, D // 2), lambda i: (0, i)),
        ],
        compiler_params=pltpu.CompilerParams(vmem_limit_bytes=VMEM_BYTES),
    )(ing, inz, que, key, val, ffn, att)


def rotary_rows(length):
    half = HEAD_DIM // 2
    freq = (np.float32(ROPE_THETA) ** (-(np.arange(half, dtype=np.float32) * 2.0) / HEAD_DIM)).astype(
        np.float32
    )
    angles = np.arange(length, dtype=np.float32)[:, None] * freq[None, :]
    cos, sin = np.cos(angles), np.sin(angles)
    return np.tile(cos, (1, 4)), np.tile(np.concatenate([-sin, sin], axis=1), (1, 2))


def by_squares(inputs, gain_one, w_qkv, w_attn, gain_two, w_in, w_ffn, cotangent):
    seqs, tok, _ = inputs.shape
    rows = seqs * tok

    gains = jnp.pad(jnp.stack([gain_one, gain_two]).astype(F32), ((0, 6), (0, 0)))
    cos, sin = (jnp.asarray(t, F32) for t in rotary_rows(tok * RING))

    ins, outs, scratch = layout(seqs, tok)
    names, shapes = [], []
    for name, item in scratch.items():
        pair = item if isinstance(item, tuple) else (item,)
        names.append((name, len(pair)))
        shapes += pair

    def body(*refs):
        count = len(ins) + len(outs)
        rest = list(refs[count:])
        found = list(refs[:count])
        for _, size in names:
            taken = tuple(rest[:size])
            rest = rest[size:]
            found.append(taken if size > 1 else taken[0])
        layer_kernel(ins + list(outs) + [name for name, _ in names], *found)

    vmem = pl.BlockSpec(memory_space=pltpu.VMEM)
    hbm = pl.BlockSpec(memory_space=pl.ANY)
    done = pl.pallas_call(
        body,
        out_shape=[jax.ShapeDtypeStruct(shape, dtype) for shape, dtype in outs.values()],
        in_specs=[hbm if name in IN_HBM else vmem for name in ins],
        out_specs=[vmem] * len(outs),
        scratch_shapes=shapes,
        compiler_params=pltpu.CompilerParams(
            collective_id=0, has_side_effects=True, vmem_limit_bytes=VMEM_BYTES
        ),
    )(
        inputs.reshape(rows, D), cotangent.reshape(rows, D),
        gains, w_qkv, w_attn, w_in, w_ffn, cos, sin,
    )
    done = dict(zip(outs, done))
    grad_in, grad_qkv, grad_ffn, grad_attn = finish(
        done["ing_all"], done["inz_all"], done["que_all"], done["key_all"], done["val_all"],
        done["ffn_rows"], done["att_rows"],
    )
    return (
        done["output"].reshape(seqs, tok, D),
        done["grad_x"].reshape(seqs, tok, D),
        done["gains"][0],
        grad_qkv,
        grad_attn,
        done["gains"][1],
        grad_in,
        grad_ffn,
    )


def solution(mesh):
    split_ok = mesh.shape["ctx"] == RING and mesh.shape["fsdp"] == OWNERS

    return jax.shard_map(
        by_squares if split_ok else on_device,
        mesh=mesh,
        in_specs=(
            P("fsdp", "ctx", None),
            P("fsdp"),
            P("fsdp", None),
            P("fsdp", None),
            P("fsdp"),
            P("fsdp", None),
            P("fsdp", None),
            P("fsdp", "ctx", None),
        ),
        out_specs=(
            P("fsdp", "ctx", None),
            P("fsdp", "ctx", None),
            P("fsdp"),
            P("fsdp", None),
            P("fsdp", None),
            P("fsdp"),
            P("fsdp", None),
            P("fsdp", None),
        ),
        check_vma=False,
    )
```

```python
import math

import jax
import jax.numpy as jnp
import numpy as np
from jax import lax
from jax.experimental import pallas as pl
from jax.experimental.pallas import tpu as pltpu
from jax.sharding import PartitionSpec as P

D = 1024
HEADS = 16
HEAD_DIM = 64
FF = 2624


EPSILON = 1e-05
ROPE_THETA = 160000.0


def norm_parts(values_in):
    mean_val = jnp.mean(values_in, axis=-1, keepdims=True)
    centred = values_in - mean_val
    variance = jnp.mean(centred * centred, axis=-1, keepdims=True)
    inv_std = lax.rsqrt(variance + EPSILON)
    return (centred * inv_std, inv_std)


def norm_back(grad_normed, normed, inv_std):
    return inv_std * (
        grad_normed
        - jnp.mean(grad_normed, axis=-1, keepdims=True)
        - normed * jnp.mean(grad_normed * normed, axis=-1, keepdims=True)
    )


def rotary_tables(positions):
    half_dim = HEAD_DIM // 2
    inv_freq = ROPE_THETA ** (-(jnp.arange(half_dim, dtype=jnp.float32) * 2.0) / HEAD_DIM)
    angles = positions.astype(jnp.float32)[:, None] * inv_freq[None, :]
    cosine = jnp.concatenate([jnp.cos(angles), jnp.cos(angles)], axis=-1)[:, None, :]
    sine_part = jnp.concatenate([jnp.sin(angles), jnp.sin(angles)], axis=-1)[:, None, :]
    return (cosine, sine_part)


def rotate(values_in, cosine, sine_part):
    half_dim = values_in.shape[-1] // 2
    turned = jnp.concatenate([-values_in[..., half_dim:], values_in[..., :half_dim]], axis=-1)
    return values_in * cosine + turned * sine_part


def rotate_back(grads, cosine, sine_part):
    half_dim = grads.shape[-1] // 2
    scaled = grads * sine_part
    turned = jnp.concatenate([scaled[..., half_dim:], -scaled[..., :half_dim]], axis=-1)
    return grads * cosine + turned


def gelu_slope(inner_part):
    cumulative = 0.5 * (1.0 + jax.scipy.special.erf(inner_part * 0.7071067811865476))
    density = jnp.exp(-0.5 * inner_part * inner_part) * 0.3989422804014327
    return cumulative + inner_part * density


def attend_piece(state_in, queries, key_piece, value_piece, scale_factor):
    row_max, row_sum, weighted = state_in
    scores = (
        jnp.einsum("bthd,bshd->bths", queries, key_piece, preferred_element_type=jnp.float32)
        * scale_factor
    )
    new_max = jnp.maximum(row_max, jnp.max(scores, axis=-1))
    rescale = jnp.exp(row_max - new_max)
    exp_vals = jnp.exp(scores - new_max[..., None])
    row_sum = row_sum * rescale + jnp.sum(exp_vals, axis=-1)
    weighted = weighted * rescale[..., None] + jnp.einsum(
        "bths,bshd->bthd",
        exp_vals.astype(jnp.bfloat16),
        value_piece,
        preferred_element_type=jnp.float32,
    )
    return (new_max, row_sum, weighted)


def back_piece(queries, grad_mixed, log_sum, row_delta, key_piece, value_piece, scale_factor):
    scores = (
        jnp.einsum("bthd,bshd->bths", queries, key_piece, preferred_element_type=jnp.float32)
        * scale_factor
    )
    probs = jnp.exp(scores - log_sum[..., None])
    grad_values = jnp.einsum(
        "bths,bthd->bshd",
        probs.astype(jnp.bfloat16),
        grad_mixed,
        preferred_element_type=jnp.float32,
    )
    grad_probs = jnp.einsum(
        "bthd,bshd->bths", grad_mixed, value_piece, preferred_element_type=jnp.float32
    )
    grad_scores = (probs * (grad_probs - row_delta[..., None])).astype(jnp.bfloat16)
    grad_query = (
        jnp.einsum("bths,bshd->bthd", grad_scores, key_piece, preferred_element_type=jnp.float32)
        * scale_factor
    )
    grad_keys = (
        jnp.einsum("bths,bthd->bshd", grad_scores, queries, preferred_element_type=jnp.float32)
        * scale_factor
    )
    return (grad_query, grad_keys, grad_values)


def add_at(whole_grads, piece_grads, offset):
    old_part = lax.dynamic_slice_in_dim(whole_grads, offset, piece_grads.shape[1], 1)
    return lax.dynamic_update_slice_in_dim(whole_grads, old_part + piece_grads, offset, 1)


def on_device(inputs, gain_one, w_qkv, w_attn, gain_two, w_in, w_ffn, cotangent):
    seq_dev = inputs.shape[0]
    tok_seq = inputs.shape[1]
    row_count = seq_dev * tok_seq
    seq_len = tok_seq * lax.axis_size("ctx")
    tokens_f = inputs.reshape(row_count, D).astype(jnp.float32)
    grad_out = cotangent.reshape(row_count, D)
    scale_factor = HEAD_DIM ** (-0.5)
    block_len = math.gcd(seq_len, 512)
    blocks_num = seq_len // block_len
    gathered = (
        lax.all_gather(gain_one, "fsdp", axis=0, tiled=True),
        lax.all_gather(w_qkv, "fsdp", axis=0, tiled=True),
        lax.all_gather(w_attn, "fsdp", axis=0, tiled=True),
        lax.all_gather(gain_two, "fsdp", axis=0, tiled=True),
        lax.all_gather(w_in, "fsdp", axis=0, tiled=True),
        lax.all_gather(w_ffn, "fsdp", axis=0, tiled=True),
    )
    full_g1, full_qkv, full_attn, full_g2, full_in, full_ffn = gathered
    normed_one, inv_one = norm_parts(tokens_f)
    input_one = (normed_one * full_g1.astype(jnp.float32)).astype(jnp.bfloat16)
    project = jnp.dot(input_one, full_qkv, preferred_element_type=jnp.float32)
    positions = lax.axis_index("ctx") * tok_seq + jnp.arange(tok_seq, dtype=jnp.int32)
    cosine, sine_part = rotary_tables(positions)
    shaped = project.reshape(seq_dev, tok_seq, 3, HEADS, HEAD_DIM)
    queries = rotate(shaped[:, :, 0], cosine, sine_part).astype(jnp.bfloat16)
    key_rows = rotate(shaped[:, :, 1], cosine, sine_part).astype(jnp.bfloat16)
    value_rows = shaped[:, :, 2].astype(jnp.bfloat16)
    start_state = (
        jnp.full((seq_dev, tok_seq, HEADS), -jnp.inf, jnp.float32),
        jnp.zeros((seq_dev, tok_seq, HEADS), jnp.float32),
        jnp.zeros((seq_dev, tok_seq, HEADS, HEAD_DIM), jnp.float32),
    )
    whole_keys, whole_values = (
        lax.all_gather(key_rows, "ctx", axis=1, tiled=True),
        lax.all_gather(value_rows, "ctx", axis=1, tiled=True),
    )

    def forward_step(state_in, block_index):
        begin = block_index * block_len
        key_piece = lax.dynamic_slice_in_dim(whole_keys, begin, block_len, 1)
        value_piece = lax.dynamic_slice_in_dim(whole_values, begin, block_len, 1)
        return (attend_piece(state_in, queries, key_piece, value_piece, scale_factor), None)

    state_out, unused = lax.scan(forward_step, start_state, jnp.arange(blocks_num, dtype=jnp.int32))
    row_max, row_sum, weighted = state_out
    attn_f = weighted / row_sum[..., None]
    log_sum = row_max + jnp.log(row_sum)
    attn_b = attn_f.reshape(row_count, D).astype(jnp.bfloat16)
    resid = tokens_f + jnp.dot(attn_b, full_attn, preferred_element_type=jnp.float32)
    normed_two, inv_two = norm_parts(resid)
    input_two = (normed_two * full_g2.astype(jnp.float32)).astype(jnp.bfloat16)
    widened = jnp.dot(input_two, full_in, preferred_element_type=jnp.float32)
    inner_part = widened[:, :FF]
    gating = widened[:, FF:]
    activated = jax.nn.gelu(inner_part, approximate=False)
    hidden = (activated * gating).astype(jnp.bfloat16)
    output = (resid + jnp.dot(hidden, full_ffn, preferred_element_type=jnp.float32)).astype(
        jnp.bfloat16
    )
    back_g1, back_qkv, back_attn, back_g2, back_in, back_ffn = gathered
    grad_ffn = jnp.dot(hidden.T, grad_out, preferred_element_type=jnp.float32)
    grad_hidden = jnp.dot(grad_out, back_ffn.T, preferred_element_type=jnp.float32)
    grad_inner = grad_hidden * gating * gelu_slope(inner_part)
    grad_gating = grad_hidden * activated
    grad_wide = jnp.concatenate([grad_inner, grad_gating], axis=-1).astype(jnp.bfloat16)
    grad_in = jnp.dot(input_two.T, grad_wide, preferred_element_type=jnp.float32)
    grad_normed_two = jnp.dot(grad_wide, back_in.T, preferred_element_type=jnp.float32)
    grad_g2 = jnp.sum(grad_normed_two * normed_two, axis=0)
    grad_resid = grad_out.astype(jnp.float32) + norm_back(
        grad_normed_two * back_g2.astype(jnp.float32), normed_two, inv_two
    )
    part_g2, part_in, part_ffn = (
        lax.psum_scatter(
            grad_g2.astype(jnp.bfloat16), "fsdp", scatter_dimension=0, tiled=True
        ).astype(jnp.float32),
        lax.psum_scatter(
            grad_in.astype(jnp.bfloat16), "fsdp", scatter_dimension=0, tiled=True
        ).astype(jnp.float32),
        lax.psum_scatter(
            grad_ffn.astype(jnp.bfloat16), "fsdp", scatter_dimension=0, tiled=True
        ).astype(jnp.float32),
    )
    resid_b = grad_resid.astype(jnp.bfloat16)
    grad_attn_w = jnp.dot(attn_b.T, resid_b, preferred_element_type=jnp.float32)
    grad_mixed = (
        jnp.dot(resid_b, back_attn.T, preferred_element_type=jnp.float32)
        .astype(jnp.bfloat16)
        .reshape(seq_dev, tok_seq, HEADS, HEAD_DIM)
    )
    row_delta = jnp.sum(grad_mixed.astype(jnp.float32) * attn_f, axis=-1)
    zero_q = jnp.zeros((seq_dev, tok_seq, HEADS, HEAD_DIM), jnp.float32)
    zero_kv = jnp.zeros((seq_dev, seq_len, HEADS, HEAD_DIM), jnp.float32)

    def backward_step(state_in, block_index):
        grad_q_sum, grad_key_all, grad_value_all = state_in
        begin = block_index * block_len
        key_piece = lax.dynamic_slice_in_dim(whole_keys, begin, block_len, 1)
        value_piece = lax.dynamic_slice_in_dim(whole_values, begin, block_len, 1)
        grad_query, grad_keys, grad_values = back_piece(
            queries, grad_mixed, log_sum, row_delta, key_piece, value_piece, scale_factor
        )
        return (
            (
                grad_q_sum + grad_query,
                add_at(grad_key_all, grad_keys, begin),
                add_at(grad_value_all, grad_values, begin),
            ),
            None,
        )

    back_state, unused_back = lax.scan(
        backward_step, (zero_q, zero_kv, zero_kv), jnp.arange(blocks_num, dtype=jnp.int32)
    )
    grad_q_sum, grad_key_all, grad_value_all = back_state
    own_keys, own_values = (
        lax.psum_scatter(
            grad_key_all.astype(jnp.bfloat16), "ctx", scatter_dimension=1, tiled=True
        ).astype(jnp.float32),
        lax.psum_scatter(
            grad_value_all.astype(jnp.bfloat16), "ctx", scatter_dimension=1, tiled=True
        ).astype(jnp.float32),
    )
    grad_q_rot = rotate_back(grad_q_sum, cosine, sine_part).reshape(row_count, D)
    grad_k_rot = rotate_back(own_keys, cosine, sine_part).reshape(row_count, D)
    grad_joint = jnp.concatenate(
        [grad_q_rot, grad_k_rot, own_values.reshape(row_count, D)], axis=-1
    ).astype(jnp.bfloat16)
    grad_qkv = jnp.dot(input_one.T, grad_joint, preferred_element_type=jnp.float32)
    grad_normed_one = jnp.dot(grad_joint, back_qkv.T, preferred_element_type=jnp.float32)
    grad_g1 = jnp.sum(grad_normed_one * normed_one, axis=0)
    grad_input = grad_resid + norm_back(
        grad_normed_one * back_g1.astype(jnp.float32), normed_one, inv_one
    )
    part_g1, part_qkv, part_attn = (
        lax.psum_scatter(
            grad_g1.astype(jnp.bfloat16), "fsdp", scatter_dimension=0, tiled=True
        ).astype(jnp.float32),
        lax.psum_scatter(
            grad_qkv.astype(jnp.bfloat16), "fsdp", scatter_dimension=0, tiled=True
        ).astype(jnp.float32),
        lax.psum_scatter(
            grad_attn_w.astype(jnp.bfloat16), "fsdp", scatter_dimension=0, tiled=True
        ).astype(jnp.float32),
    )
    totals = (
        lax.psum(part_g1.astype(jnp.bfloat16), "ctx").astype(jnp.float32),
        lax.psum(part_qkv.astype(jnp.bfloat16), "ctx").astype(jnp.float32),
        lax.psum(part_attn.astype(jnp.bfloat16), "ctx").astype(jnp.float32),
        lax.psum(part_g2.astype(jnp.bfloat16), "ctx").astype(jnp.float32),
        lax.psum(part_in.astype(jnp.bfloat16), "ctx").astype(jnp.float32),
        lax.psum(part_ffn.astype(jnp.bfloat16), "ctx").astype(jnp.float32),
    )
    return (
        output.reshape(seq_dev, tok_seq, D),
        grad_input.reshape(seq_dev, tok_seq, D),
        totals[0],
        totals[1],
        totals[2],
        totals[3],
        totals[4],
        totals[5],
    )


RING = 8
OWNERS = 4
PAIR = 2 * HEAD_DIM
UNITS = FF // RING
UNITS_PAD = 384
UNIT_ROWS = 336
WINDOW = 512
ATTN_ROWS = 128
MESH = pl.DeviceIdType.MESH
VMEM_BYTES = 60 * 1024 * 1024
F32 = jnp.float32
BF16 = jnp.bfloat16


def contract(left, right, left_dim, right_dim):
    return lax.dot_general(
        left, right, (((left_dim,), (right_dim,)), ((), ())), preferred_element_type=F32
    )


class Here:
    def __init__(self):
        b, f = lax.axis_index("ctx"), lax.axis_index("fsdp")
        x, low = b % 2, (b // 2) % 2
        self.b, self.f = b, f
        self.c, self.y, self.q, self.high, self.x, self.low = f % 2, f // 2, b % 4, b // 4, x, low
        self.bx, self.bz = b + 1 - 2 * x, b + 2 - 4 * low
        self.bd, self.bh = self.bx + 2 - 4 * low, (b + 4) % RING
        self.qx, self.qz = self.q + 1 - 2 * x, self.q + 2 - 4 * low
        self.qd = self.qx + 2 - 4 * low
        self.core = f + 1 - 2 * self.c
        self.far = (f + 2) % OWNERS
        self.diag = (self.core + 2) % OWNERS
        self.p = self.c * 4 + self.q

    def mine(self, q):
        return self.c * 4 + q

    def other(self, q):
        return (1 - self.c) * 4 + q

    def mine_of(self, c):
        return c * 4 + self.q

    def greet(self):
        barrier = pltpu.get_barrier_semaphore()
        peers = [(b, f) for b in (self.b, self.bx, self.bz, self.bd) for f in (self.f, self.core)]
        peers = peers[1:] + [
            (self.b, self.far), (self.b, self.diag), (self.bh, self.f), (self.bh, self.core),
        ]
        for peer in peers:
            pl.semaphore_signal(barrier, inc=1, device_id=peer, device_id_type=MESH)
        pl.semaphore_wait(barrier, len(peers))


def push(src, dst, send, recv, device):
    return pltpu.make_async_remote_copy(
        src_ref=src, dst_ref=dst, send_sem=send, recv_sem=recv, device_id=device, device_id_type=MESH
    )


class Gather:
    def __init__(self, here, buf, send, recv, split=True):
        h = here
        self.h, self.send_sem, self.recv_sem, self.split = h, send, recv, split
        high = buf.shape[1]
        half = high // 2
        top, bottom = pl.ds(0, half if split else high), pl.ds(half, half)
        own, near_x, near_z = buf.at[h.p], buf.at[h.mine(h.qx)], buf.at[h.mine(h.qz)]
        across = buf.at[h.mine(h.qd)]
        to_x, to_z, to_core = (h.bx, h.f), (h.bz, h.f), (h.b, h.core)
        self.out = [
            (own, to_x), (own, to_z), (near_z.at[top], to_x), (near_x.at[bottom], to_z),
            (own, to_core), (near_x, to_core), (near_z, to_core), (across, to_core),
        ]
        self.inn = [
            near_x, near_z, across.at[top], across.at[bottom],
            buf.at[h.other(h.q)], buf.at[h.other(h.qx)], buf.at[h.other(h.qz)], buf.at[h.other(h.qd)],
        ]

    def copy(self, kind):
        ref, device = self.out[kind]
        return push(ref, ref, self.send_sem.at[kind], self.recv_sem.at[kind], device)

    def wait(self, kind):
        ref = self.inn[kind]
        device = self.out[kind][1]
        push(ref, ref, self.send_sem.at[kind], self.recv_sem.at[kind], device).wait_recv()

    def begin(self):
        for kind in (0, 1, 4):
            self.copy(kind).start()

    def near(self):
        self.wait(0)
        if self.split:
            self.copy(3).start()
        self.copy(5).start()
        self.wait(1)
        self.copy(2).start()
        self.copy(6).start()

    def across(self):
        self.wait(2)
        if self.split:
            self.wait(3)
        self.copy(7).start()

    def sent(self):
        for kind in range(8):
            if kind != 3 or self.split:
                self.copy(kind).wait_send()

    def each(self, work, meanwhile=None, late=False):
        h = self.h
        work(h.p)
        self.wait(4)
        work(h.other(h.q))
        self.near()
        work(h.mine(h.qx))
        work(h.mine(h.qz))
        if meanwhile is not None and not late:
            meanwhile()
        self.wait(5)
        work(h.other(h.qx))
        self.wait(6)
        work(h.other(h.qz))
        self.across()
        if late:
            meanwhile()
        work(h.mine(h.qd))
        self.wait(7)
        work(h.other(h.qd))


class Scatter:
    def __init__(self, here, terms, core_out, near_out, across_out, core_in, near_in, across_in, send, recv, split):
        h = here
        self.h, self.terms, self.send_sem, self.recv_sem, self.split = h, terms, send, recv, split
        self.core_out, self.near_out, self.across_out = core_out, near_out, across_out
        self.core_in, self.near_in, self.across_in = core_in, near_in, across_in
        to_x, to_z, to_core = (h.bx, h.f), (h.bz, h.f), (h.b, h.core)
        self.out = [(core_out.at[i], core_in.at[i], to_core) for i in range(4)] + [
            (across_out.at[0], across_in.at[0], to_x),
            (across_out.at[1], across_in.at[1], to_z if split else to_x),
            (near_out.at[0], near_in.at[0], to_x),
            (near_out.at[1], near_in.at[1], to_z),
        ]
        self.half = terms.shape[1] // 2

    def copy(self, kind):
        src, dst, device = self.out[kind]
        return push(src, dst, self.send_sem.at[kind], self.recv_sem.at[kind], device)

    def wait(self, kind):
        self.copy(kind).wait_recv()

    def begin(self, work):
        h = self.h

        def send(i, q):
            work(h.other(q))
            self.core_out[i] = self.terms[h.other(q)].astype(BF16)
            self.copy(i).start()

        send(0, h.qd)
        work(h.mine(h.qd))
        send(1, h.qz)
        send(2, h.qx)
        self.first()
        work(h.mine(h.qz))
        work(h.mine(h.qx))
        send(3, h.q)
        work(h.p)

    def pair(self, i, q):
        return self.terms[self.h.mine(q)] + self.core_in[i].astype(F32)

    def first(self):
        self.wait(0)
        part = self.pair(0, self.h.qd).astype(BF16)
        self.across_out[0] = part[: self.half]
        self.copy(4).start()
        self.across_out[1] = part[self.half :]
        self.copy(5).start()

    def second(self):
        half = self.half
        self.wait(2)
        if not self.split:
            self.near_out[0] = self.pair(2, self.h.qx).astype(BF16)
            self.copy(6).start()
            self.wait(1)
            part = self.pair(1, self.h.qz)
            for i in range(2):
                rows = slice(i * half, (i + 1) * half)
                self.wait(4 + i)
                self.near_out[1, rows] = (part[rows] + self.across_in[i].astype(F32)).astype(BF16)
            self.copy(7).start()
            return
        self.wait(5)
        part = self.pair(2, self.h.qx)
        self.near_out[0, :half] = part[:half].astype(BF16)
        self.near_out[0, half:] = (part[half:] + self.across_in[1].astype(F32)).astype(BF16)
        self.copy(6).start()
        self.wait(1)
        self.wait(4)
        part = self.pair(1, self.h.qz)
        self.near_out[1, :half] = (part[:half] + self.across_in[0].astype(F32)).astype(BF16)
        self.near_out[1, half:] = part[half:].astype(BF16)
        self.copy(7).start()

    def finish(self):
        self.wait(3)
        total = self.pair(3, self.h.q)
        self.wait(6)
        self.wait(7)
        total = total + self.near_in[0].astype(F32) + self.near_in[1].astype(F32)
        for kind in range(8):
            self.copy(kind).wait_send()
        return total


class Grads:
    def __init__(self, here, g, far_in, high_in, core_out, whole, send, recv, split=False):
        h = here
        self.kinds = 7 if split else 6
        high = g.shape[2]
        top = high // 32 * 16 if split else high
        self.h, self.g, self.far_in, self.high_in = h, g, far_in, high_in
        self.core_out, self.whole, self.send_sem, self.recv_sem = core_out, whole, send, recv
        self.out = [
            (g.at[1 - h.y], far_in, (h.b, h.far)),
            (g.at[h.y], high_in, (h.bh, h.f)),
            (core_out, whole.at[h.q, h.c], (h.b, h.core)),
            (whole.at[h.q], whole.at[h.q], (h.bx, h.f)),
            (whole.at[h.q], whole.at[h.q], (h.bz, h.f)),
        ]
        for q, device, rows in (
            (h.qz, (h.bx, h.f), pl.ds(0, top)), (h.qx, (h.bz, h.f), pl.ds(top, high - top)),
        )[: self.kinds - 5]:
            self.out.append((whole.at[q, :, rows], whole.at[q, :, rows], device))
        self.inn = [far_in, high_in, whole.at[h.q, 1 - h.c], whole.at[h.qx], whole.at[h.qz]]
        for rows in (pl.ds(0, top), pl.ds(top, high - top))[: self.kinds - 5]:
            self.inn.append(whole.at[h.qd, :, rows])

    def copy(self, kind):
        src, dst, device = self.out[kind]
        return push(src, dst, self.send_sem.at[kind], self.recv_sem.at[kind], device)

    def wait(self, kind):
        ref, device = self.inn[kind], self.out[kind][2]
        push(ref, ref, self.send_sem.at[kind], self.recv_sem.at[kind], device).wait_recv()

    def to_far(self):
        self.copy(0).start()

    def from_far(self):
        self.wait(0)
        y = self.h.y
        self.g[y] = (self.g[y].astype(F32) + self.far_in[...].astype(F32)).astype(BF16)

    def to_high(self):
        self.copy(1).start()

    def total(self, c):
        return (self.g[self.h.y, c].astype(F32) + self.high_in[c].astype(F32)).astype(BF16)

    def to_core(self):
        self.wait(1)
        h = self.h
        self.core_out[...] = self.total(1 - h.c)
        self.copy(2).start()
        self.whole[h.q, h.c] = self.total(h.c)

    def to_near(self):
        self.wait(2)
        self.copy(3).start()
        self.copy(4).start()

    def to_across(self):
        self.wait(4)
        self.copy(5).start()
        self.wait(3)
        if self.kinds == 7:
            self.copy(6).start()

    def finish(self):
        for kind in range(5, self.kinds):
            self.wait(kind)

    def sent(self):
        for kind in range(self.kinds):
            self.copy(kind).wait_send()


class Rows:
    def __init__(self, here, whole, rows, send, recv):
        self.h, self.whole, self.rows, self.send_sem, self.recv_sem = here, whole, rows, send, recv

    def place(self, half, owner):
        return self.rows.at[half, :, pl.ds(pl.multiple_of(owner * 256, 256), 256)]

    def copy(self, q, c):
        h = self.h
        return push(
            self.whole.at[q, c], self.place(q % 2, h.f),
            self.send_sem.at[q, c], self.recv_sem.at[h.f, q % 2], (h.b, 2 * c + q // 2),
        )

    def begin(self):
        h = self.h
        for q in range(4):
            for c in range(2):
                owner = 2 * c + q // 2

                @pl.when(h.f != owner)
                def _(q=q, c=c):
                    self.copy(q, c).start()

                @pl.when(h.f == owner)
                def _(q=q, c=c, owner=owner):
                    self.rows[q % 2, :, owner * 256 : (owner + 1) * 256] = self.whole[q, c]

    def finish(self):
        h = self.h
        for owner in range(OWNERS):

            @pl.when(h.f != owner)
            def _(owner=owner):
                for half in range(2):
                    ref = self.place(half, owner)
                    push(
                        ref, ref, self.send_sem.at[0, 0], self.recv_sem.at[owner, half],
                        (h.b, owner),
                    ).wait_recv()

        for q in range(4):
            for c in range(2):

                @pl.when(h.f != 2 * c + q // 2)
                def _(q=q, c=c):
                    self.copy(q, c).wait_send()


def row_norm(rows):
    mean = jnp.mean(rows, axis=-1, keepdims=True)
    centred = rows - mean
    inv = lax.rsqrt(jnp.mean(centred * centred, axis=-1, keepdims=True) + EPSILON)
    return centred * inv, inv


def row_back(grad, normed, inv):
    return inv * (
        grad
        - jnp.mean(grad, axis=-1, keepdims=True)
        - normed * jnp.mean(grad * normed, axis=-1, keepdims=True)
    )


def first_half():
    lane = lax.broadcasted_iota(jnp.int32, (1, PAIR), 1)
    return lane % HEAD_DIM < HEAD_DIM // 2


def first_head():
    return lax.broadcasted_iota(jnp.int32, (1, PAIR), 1) < HEAD_DIM


def swap_halves(rows):
    up = pltpu.roll(rows, PAIR - HEAD_DIM // 2, 1)
    down = pltpu.roll(rows, HEAD_DIM // 2, 1)
    return jnp.where(first_half(), up, down)


def only(rows, head):
    keep = first_head() if head == 0 else jnp.logical_not(first_head())
    return jnp.where(keep, rows, jnp.zeros_like(rows))


def quarter(ref, j):
    tile = ref[:, :, j * 256 : (j + 1) * 256]
    return tile.reshape(tile.shape[0] * tile.shape[1], 256)


def flat(ref):
    rows = ref[...]
    return rows.reshape(rows.shape[0] * rows.shape[1], rows.shape[2])


class Box:
    pass


IN_HBM = ("w_qkv", "w_in", "w_ffn")
GATHERS = ("xg", "cg", "ag", "rg")
SCATTERS = ("two", "out", "one")
CHUNKS = (
    ("ffn", UNIT_ROWS), ("ing", UNIT_ROWS), ("inz", UNIT_ROWS),
    ("att", ATTN_ROWS), ("que", ATTN_ROWS), ("key", ATTN_ROWS), ("val", ATTN_ROWS),
)


def layout(seqs, tok):
    rows, length = seqs * tok, tok * RING
    whole = (RING, rows, D)
    half = rows // 2
    ins = [
        "x", "cot", "gain_one", "gain_two", "w_qkv", "attn_w", "w_in", "w_ffn", "cos", "sin",
    ]
    outs = {
        "output": ((rows, D), BF16),
        "grad_x": ((rows, D), F32),
        "gains": ((8, 256), F32),
        "ffn_rows": ((2, UNIT_ROWS, D), BF16),
        "att_rows": ((2, ATTN_ROWS, D), BF16),
    }
    for name, high in CHUNKS:
        if name not in ("ffn", "att"):
            outs[name + "_all"] = ((4, 2, high, 256), BF16)
    sem = pltpu.SemaphoreType.DMA
    vm = pltpu.VMEM
    scratch = {
        "xs": vm(whole, BF16), "cots": vm(whole, BF16), "a1": vm(whole, BF16), "a2": vm(whole, BF16),
        "resids": vm(whole, BF16), "terms": vm(whole, F32),
        "qkv_w": vm((2, 256, 3 * PAIR), BF16), "in_w": vm((2, 256, 2 * UNITS_PAD), BF16),
        "ffn_w": vm((UNIT_ROWS, D), BF16), "windows": vm((2, 2, 256, WINDOW), BF16),
        "gain": vm((8, 256), F32), "gain_all": vm((8, D), F32), "qkv_c": vm((D, 3 * PAIR), BF16), "attn_all": vm((D, D), BF16),
        "in_c": vm((D, 2 * UNITS_PAD), BF16), "ffn_c": vm((UNITS_PAD, D), BF16),
        "qs": vm((seqs, length, PAIR), BF16), "ks": vm((seqs, length, PAIR), BF16),
        "vs": vm((seqs, length, PAIR), BF16), "os": vm((seqs, length, PAIR), F32),
        "lse": vm((seqs, length, PAIR), F32), "heads": vm((RING, rows, PAIR), BF16),
        "own_heads": vm((RING, rows, PAIR), BF16), "mixed": vm((RING, rows, PAIR), BF16),
        "joint": vm((RING, rows, 3 * PAIR), BF16),
        "fs": vm((RING, rows, UNITS_PAD), BF16), "dus": vm((RING, rows, 2 * UNITS_PAD), BF16),
        "n2": vm((rows, D), F32), "resid": vm((rows, D), F32), "dy": vm((rows, D), F32),
        "core_out": vm((4, rows, D), BF16), "near_out": vm((2, rows, D), BF16),
        "across_out": vm((2, half, D), BF16),
        "back_out": vm((2, rows, D), BF16), "back_in": vm((2, rows, D), BF16),
        "sums": vm((6, 8, D), F32), "sums_in": vm((5, 8, D), F32),
        "ffn_all": vm((4, 2, UNIT_ROWS, 256), BF16), "att_all": vm((4, 2, ATTN_ROWS, 256), BF16),
    }
    for name in GATHERS:
        scratch[name + "_sems"] = (sem((8,)), sem((8,)))
    for name in SCATTERS:
        scratch[name + "_core"] = vm((4, rows, D), BF16)
        scratch[name + "_near"] = vm((2, rows, D), BF16)
        scratch[name + "_across"] = vm((2, half, D), BF16)
        scratch[name + "_sems"] = (sem((8,)), sem((8,)))
    for name, high in CHUNKS:
        scratch[name + "_g"] = vm((2, 2, high, 256), BF16)
        scratch[name + "_far"] = vm((2, high, 256), BF16)
        scratch[name + "_high"] = vm((2, high, 256), BF16)
        scratch[name + "_core"] = vm((high, 256), BF16)
        scratch[name + "_sems"] = (sem((7,)), sem((7,)))
    for name, count in (("swap", 4), ("part", 9), ("attn", 5), ("head", RING - 1), ("sum", 5)):
        scratch[name + "_sems"] = (sem((count,)), sem((count,)))
    scratch["ffn_w_sems"] = (sem((2,)), sem((1,)))
    scratch["cut_sems"] = (sem((2, 3)), sem((2, 2)), sem((1,)))
    for name in ("ffn_rows", "att_rows"):
        scratch[name + "_sems"] = (sem((4, 2)), sem((4, 2)))
    return ins, outs, scratch


def layer_kernel(names, *refs):
    r = Box()
    for name, ref in zip(names, refs):
        setattr(r, name, ref)
    h = Here()
    seqs, length = r.qs.shape[0], r.qs.shape[1]
    tok = length // RING
    scale = HEAD_DIM ** (-0.5)
    moved = h.high != h.c
    there = (h.bh, h.core)
    there_p = h.high * 4 + h.q
    cut_q, cut_i, cut_f = r.cut_sems

    def cut_qkv(c, i):
        start = i * D + h.mine_of(c) * PAIR
        return pltpu.make_async_copy(
            r.w_qkv.at[:, pl.ds(pl.multiple_of(start, PAIR), PAIR)],
            r.qkv_w.at[c, :, i * PAIR : (i + 1) * PAIR], cut_q.at[c, i],
        )

    def window(c, i):
        start = i * FF + h.mine_of(c) * UNITS
        return start, jnp.minimum(start // PAIR * PAIR, 2 * FF - WINDOW)

    def cut_in(c, i):
        return pltpu.make_async_copy(
            r.w_in.at[:, pl.ds(pl.multiple_of(window(c, i)[1], PAIR), WINDOW)],
            r.windows.at[c, i], cut_i.at[c, i],
        )

    cut_ffn = pltpu.make_async_copy(
        r.w_ffn.at[pl.ds(pl.multiple_of(h.x * (UNITS - 8), 16), UNIT_ROWS)], r.ffn_w, cut_f.at[0]
    )
    for c in range(2):
        for i in range(3):
            cut_qkv(c, i).start()
    for c in range(2):
        for i in range(2):
            cut_in(c, i).start()
    cut_ffn.start()

    h.greet()

    def swap(i, src, dst, back):
        send, recv = r.swap_sems
        return push(src, dst, send.at[i], recv.at[i], there)

    def swap_in(i, src, whole):
        @pl.when(moved)
        def _():
            swap(i, src, whole.at[there_p], False).start()

        @pl.when(jnp.logical_not(moved))
        def _():
            whole[h.p] = src[...]

    def swap_got(i, src, whole):
        @pl.when(moved)
        def _():
            swap(i, whole.at[h.p], whole.at[h.p], False).wait_recv()

    def swap_sent(i, src, whole):
        @pl.when(moved)
        def _():
            swap(i, src, whole.at[there_p], False).wait_send()

    swap_in(0, r.x, r.xs)

    p_send, p_recv = r.part_sems
    peers = (h.far, h.core, h.diag)

    def part_at(whole, owner, lanes):
        if lanes:
            return whole.at[:, pl.ds(pl.multiple_of(owner * 256, 256), 256)]
        return whole.at[pl.ds(pl.multiple_of(owner * 256, 256), 256)]

    def part(i, src, whole, lanes, sliced):
        def copy(k):
            mine = (h.c, 1 - h.c, 1 - h.c)[k]
            return push(
                src.at[mine] if sliced else src, part_at(whole, h.f, lanes),
                p_send.at[3 * i + k], p_recv.at[3 * i + k], (h.b, peers[k]),
            )

        box = Box()

        def begin():
            for k in range(3):
                copy(k).start()
            place = part_at(whole, h.f, lanes)
            place[...] = src[h.c] if sliced else src[...]

        def got():
            for k in range(3):
                ref = part_at(whole, peers[k], lanes)
                push(ref, ref, p_send.at[3 * i + k], p_recv.at[3 * i + k], (h.b, peers[k])).wait_recv()

        def sent():
            for k in range(3):
                copy(k).wait_send()

        box.begin, box.got, box.sent = begin, got, sent
        return box

    gain_p = part(0, r.gain, r.gain_all, True, False)
    qkv_p = part(1, r.qkv_w, r.qkv_c, False, True)
    in_p = part(2, r.in_w, r.in_c, False, True)

    def attn_half(owner, half):
        return r.attn_all.at[pl.ds(pl.multiple_of(owner * 256 + half * 128, 128), 128)]

    def attn_copy(k):
        own_half = pl.ds(pl.multiple_of(h.x * 128, 128), 128)
        came, later = attn_half(h.far, h.x), attn_half(h.far, 1 - h.x)
        src, dst, device = (
            (r.attn_w.at[own_half], attn_half(h.f, h.x), (h.b, h.far)),
            (r.attn_w, part_at(r.attn_all, h.f, False), (h.b, h.core)),
            (came, came, (h.bx, h.f)),
            (came, came, (h.b, h.core)),
            (later, later, (h.b, h.core)),
        )[k]
        return push(src, dst, a_send.at[k], a_recv.at[k], device)

    def attn_wait(k):
        ref = (
            attn_half(h.far, h.x), part_at(r.attn_all, h.core, False), attn_half(h.far, 1 - h.x),
            attn_half(h.diag, h.x), attn_half(h.diag, 1 - h.x),
        )[k]
        push(ref, ref, a_send.at[k], a_recv.at[k], (h.b, h.core)).wait_recv()

    a_send, a_recv = r.attn_sems
    f_send, f_recv = r.ffn_w_sems
    active = h.c == h.low
    near_own = 2 * h.y + h.y
    far_own = 2 * (1 - h.y) + h.y
    ffn_owner = 2 * h.c + h.low
    unit_rows = pl.ds(0, UNIT_ROWS)

    def ffn_copy(k):
        return push(
            r.ffn_w.at[unit_rows], r.ffn_c.at[unit_rows],
            f_send.at[k], f_recv.at[0], (h.b, (near_own, far_own)[k]),
        )

    r.gain[...] = jnp.zeros((8, 256), F32)
    r.gain[0:1, :] = r.gain_one[...].astype(F32)
    r.gain[1:2, :] = r.gain_two[...].astype(F32)
    gain_p.begin()
    for c in range(2):
        for i in range(3):
            cut_qkv(c, i).wait()
    qkv_p.begin()
    lane = lax.broadcasted_iota(jnp.int32, (1, WINDOW), 1)
    inside = jnp.logical_and(lane >= 8 * h.x, lane < 8 * h.x + UNITS)
    for c in range(2):
        for i in range(2):
            cut_in(c, i).wait()
            start, left = window(c, i)
            turned = pltpu.roll(
                r.windows[c, i].astype(F32), lax.rem(left - start + 8 * h.x + WINDOW, WINDOW), 1
            )
            kept = jnp.where(inside, turned, 0.0)[:, :UNITS_PAD]
            r.in_w[c, :, i * UNITS_PAD : (i + 1) * UNITS_PAD] = kept.astype(BF16)
    cut_ffn.wait()
    swap_got(0, r.x, r.xs)
    swap_in(1, r.cot, r.cots)
    xg = Gather(h, r.xs, *r.xg_sems)
    xg.begin()
    cg = Gather(h, r.cots, *r.cg_sems)

    @pl.when(jnp.logical_not(moved))
    def _():
        cg.begin()

    gain_p.got()
    qkv_p.got()
    attn_copy(0).start()
    attn_copy(1).start()
    at_own = part_at(r.attn_all, h.f, False)
    at_own[...] = r.attn_w[...]
    r.ffn_c[UNIT_ROWS:, :] = jnp.zeros((UNITS_PAD - UNIT_ROWS, D), BF16)

    @pl.when(ffn_owner == h.f)
    def _():
        r.ffn_c[unit_rows, :] = r.ffn_w[unit_rows, :]

    def project(index):
        normed, _ = row_norm(r.xs[index].astype(F32))
        a1 = (normed * r.gain_all[0:1, :]).astype(BF16)
        r.a1[index] = a1
        r.terms[index, :, : 3 * PAIR] = contract(a1, r.qkv_c[...], 1, 0)

    def more_weights():
        attn_wait(0)
        attn_copy(2).start()
        attn_copy(3).start()
        in_p.begin()

        @pl.when(jnp.logical_not(moved))
        def _():
            cg.near()

    xg.each(project, more_weights)

    for s in range(seqs):
        rows = slice(s * tok, (s + 1) * tok)

        def columns(i):
            return r.terms[:, rows, i * PAIR : (i + 1) * PAIR].reshape(length, PAIR)

        cos, sin = r.cos[...], r.sin[...]
        query, key = columns(0), columns(1)
        q = (query * cos + swap_halves(query) * sin).astype(BF16)
        k = (key * cos + swap_halves(key) * sin).astype(BF16)
        v = columns(2).astype(BF16)
        r.qs[s] = q
        r.ks[s] = k
        r.vs[s] = v
        outs, lses = [], []
        for head in range(2):
            scores = contract(only(q, head), k, 1, 1) * scale
            top = jnp.max(scores, axis=-1, keepdims=True)
            e = jnp.exp(scores - top)
            total = jnp.sum(e, axis=-1, keepdims=True)
            outs.append(contract(e.astype(BF16), v, 1, 0) / total)
            lses.append(top + jnp.log(total))
        of = jnp.where(first_head(), outs[0], outs[1])
        r.os[s] = of
        r.lse[s] = jnp.where(first_head(), lses[0], lses[1])
        r.heads[:, rows, :] = of.astype(BF16).reshape(RING, tok, PAIR)

    h_send, h_recv = r.head_sems
    around = []
    for b, q in ((h.b, h.q), (h.bx, h.qx), (h.bz, h.qz), (h.bd, h.qd)):
        around += [((b, h.f), h.mine(q)), ((b, h.core), h.other(q))]

    def exchange(i):
        device, p = around[i + 1]
        return push(r.heads.at[p], r.own_heads.at[h.p], h_send.at[i], h_recv.at[i], device)

    for i in range(RING - 1):
        exchange(i).start()
    r.own_heads[h.p] = r.heads[h.p]
    @pl.when(moved)
    def _():
        swap(1, r.cots.at[h.p], r.cots.at[h.p], False).wait_recv()
        cg.begin()

    attn_wait(2)
    attn_copy(4).start()
    attn_wait(1)
    attn_wait(3)
    attn_wait(4)
    for i in range(RING - 1):
        device, p = around[i + 1]
        ref = r.own_heads.at[p]
        push(ref, ref, h_send.at[i], h_recv.at[i], device).wait_recv()

    @pl.when(moved)
    def _():
        cg.near()

    g2 = r.gain_all[1:2, :]
    mixed_heads = jnp.concatenate([r.own_heads[d] for d in range(RING)], axis=1)
    resid = r.xs[h.p].astype(F32) + contract(mixed_heads, r.attn_all[...], 1, 0)
    r.resid[...] = resid
    normed, inv_two = row_norm(resid)
    r.n2[...] = normed
    r.a2[h.p] = (normed * g2).astype(BF16)
    ag = Gather(h, r.a2, *r.ag_sems)
    ag.begin()

    @pl.when(active)
    def _():
        ffn_copy(1).start()

    @pl.when(jnp.logical_and(active, near_own != h.f))
    def _():
        ffn_copy(0).start()

    in_p.got()

    def widen(index):
        r.terms[index, :, : 2 * UNITS_PAD] = contract(r.a2[index], r.in_c[...], 1, 0)

    ag.each(widen)
    cg.across()
    for kind in range(4, 8):
        cg.wait(kind)
    @pl.when(ffn_owner != h.f)
    def _():
        ffn_copy(0).wait_recv()

    def feed(index):
        inner = r.terms[index, :, :UNITS_PAD]
        gating = r.terms[index, :, UNITS_PAD : 2 * UNITS_PAD]
        below = 0.5 * (1.0 + lax.erf(inner * 0.7071067811865476))
        density = jnp.exp(-0.5 * inner * inner) * 0.3989422804014327
        active = inner * below
        r.fs[index] = (active * gating).astype(BF16)
        grad_hidden = contract(r.cots[index], r.ffn_c[...], 1, 1)
        du = jnp.concatenate(
            [grad_hidden * gating * (below + inner * density), grad_hidden * active], axis=1
        ).astype(BF16)
        r.dus[index] = du
        r.terms[index] = contract(du, r.in_c[...], 1, 1)

    def scatter(name, split):
        return Scatter(
            h, r.terms, r.core_out, r.near_out, r.across_out,
            getattr(r, name + "_core"), getattr(r, name + "_near"), getattr(r, name + "_across"),
            *getattr(r, name + "_sems"), split,
        )

    ch = {}
    for name, _ in CHUNKS:
        ch[name] = Grads(
            h, getattr(r, name + "_g"), getattr(r, name + "_far"), getattr(r, name + "_high"),
            getattr(r, name + "_core"), getattr(r, name + "_all"), *getattr(r, name + "_sems"),
            name not in ("ffn", "ing"),
        )

    ffn, ing, inz, att = ch["ffn"], ch["ing"], ch["inz"], ch["att"]
    que, key, val = ch["que"], ch["key"], ch["val"]
    two = scatter("two", False)
    two.begin(feed)
    for j in range(OWNERS):
        r.ffn_g[j // 2, j % 2] = contract(flat(r.fs), quarter(r.cots, j), 0, 0)[:UNIT_ROWS].astype(BF16)
    ffn.to_far()
    two.second()
    for j in range(OWNERS):
        c, y = j % 2, j // 2
        grad_in = contract(flat(r.dus), quarter(r.a2, j), 0, 0).astype(BF16)
        r.ing_g[y, c] = grad_in[:UNIT_ROWS]
        r.inz_g[y, c] = grad_in[UNITS_PAD : UNITS_PAD + UNIT_ROWS]
    grad_two = two.finish()

    normed = r.n2[...]
    r.sums[0, 1:2, :] = jnp.sum(grad_two * normed, axis=0, keepdims=True)
    own_grad = r.cots[h.p].astype(F32) + row_back(grad_two * g2, normed, inv_two)
    r.dy[...] = own_grad
    r.resids[h.p] = own_grad.astype(BF16)
    rg = Gather(h, r.resids, *r.rg_sems, False)
    rg.begin()
    ffn.from_far()
    ffn.to_high()
    ing.to_far()

    attn_c = r.attn_all.at[pl.ds(pl.multiple_of(h.p * PAIR, PAIR), PAIR)]

    def mix(index):
        r.mixed[index] = contract(r.resids[index], attn_c[...], 1, 1).astype(BF16)

    def ing_far():
        ing.from_far()
        inz.to_far()

    rg.each(mix, ing_far)
    ffn.to_core()
    ing.to_high()
    for j in range(OWNERS):
        r.att_g[j // 2, j % 2] = contract(flat(r.heads), quarter(r.resids, j), 0, 0).astype(BF16)
    ffn.to_near()

    for s in range(seqs):
        rows = slice(s * tok, (s + 1) * tok)
        q, k, v = r.qs[s], r.ks[s], r.vs[s]
        do = r.mixed[:, rows, :].reshape(length, PAIR)
        weighed = do.astype(F32) * r.os[s]
        dqs, dks, dvs = [], [], []
        for head in range(2):
            delta = jnp.sum(only(weighed, head), axis=-1, keepdims=True)
            lse = r.lse[s, :, head * HEAD_DIM : head * HEAD_DIM + 1]
            probs = jnp.exp(contract(only(q, head), k, 1, 1) * scale - lse)
            dvs.append(contract(probs.astype(BF16), do, 0, 0))
            grad_probs = contract(only(do, head), v, 1, 1)
            ds = (probs * (grad_probs - delta)).astype(BF16)
            dqs.append(contract(ds, k, 1, 0) * scale)
            dks.append(contract(ds, q, 0, 0) * scale)
        cos, sin = r.cos[...], r.sin[...]
        dq = jnp.where(first_head(), dqs[0], dqs[1])
        dk = jnp.where(first_head(), dks[0], dks[1])
        dv = jnp.where(first_head(), dvs[0], dvs[1])
        for i, item in enumerate(
            (dq * cos - swap_halves(dq) * sin, dk * cos - swap_halves(dk) * sin, dv)
        ):
            r.joint[:, rows, i * PAIR : (i + 1) * PAIR] = item.astype(BF16).reshape(RING, tok, PAIR)
        if s == 0:
            inz.from_far()
            att.to_far()

    def term(i):
        r.terms[i] = contract(r.joint[i], r.qkv_c[...], 1, 1)

    one = scatter("one", False)
    one.begin(term)
    for j in range(OWNERS):
        grad_qkv = contract(flat(r.joint), quarter(r.a1, j), 0, 0).astype(BF16)
        for i, name in enumerate(("que", "key", "val")):
            getattr(r, name + "_g")[j // 2, j % 2] = grad_qkv[i * PAIR : (i + 1) * PAIR]
        if j == 0:
            one.second()
    att.from_far()
    for item in (que, key, val):
        item.to_far()
    ing.to_core()
    inz.to_high()
    ffn.to_across()

    grad_one = one.finish()
    normed, inv_one = row_norm(r.xs[h.p].astype(F32))
    r.sums[0, 0:1, :] = jnp.sum(grad_one * normed, axis=0, keepdims=True)
    r.sums[0, 2:, :] = jnp.zeros((6, D), F32)
    s_send, s_recv = r.sum_sems
    partners = ((h.b, h.core), (h.b, h.far), (h.bx, h.f), (h.bz, h.f), (h.bh, h.f))

    def sum_copy(i):
        return push(r.sums.at[i], r.sums_in.at[i], s_send.at[i], s_recv.at[i], partners[i])

    def sum_step(i):
        sum_copy(i).wait_recv()
        r.sums[i + 1] = r.sums[i] + r.sums_in[i]
        if i < 4:
            sum_copy(i + 1).start()

    def back(i):
        return swap(2 + i, r.back_out.at[i], r.back_in.at[i], True)

    sum_copy(0).start()
    grad_x = r.dy[...] + row_back(grad_one * r.gain_all[0:1, :], normed, inv_one)
    r.grad_x[...] = grad_x
    r.back_out[1] = grad_x.astype(BF16)

    @pl.when(moved)
    def _():
        back(1).start()

    ing.to_near()

    def out_term(i):
        r.terms[i] = contract(r.fs[i], r.ffn_c[...], 1, 0)

    out = scatter("out", True)
    out.begin(out_term)
    sum_step(0)
    for item in (que, key, val):
        item.from_far()
    sum_step(1)
    inz.to_core()
    att.to_high()
    que.to_high()
    ing.to_across()
    inz.to_near()
    out.second()
    sum_step(2)
    ffn.finish()
    ffn_rows = Rows(h, r.ffn_all, r.ffn_rows, *r.ffn_rows_sems)
    ffn_rows.begin()
    att.to_core()
    key.to_high()
    val.to_high()
    sum_step(3)
    att.to_near()
    que.to_core()
    que.to_near()
    inz.to_across()
    r.back_out[0] = (r.resid[...] + out.finish()).astype(BF16)

    @pl.when(moved)
    def _():
        back(0).start()

    sum_step(4)
    r.gains[...] = r.sums[5, :, pl.ds(pl.multiple_of(h.f * 256, 256), 256)]
    att.to_across()
    key.to_core()
    key.to_near()
    que.to_across()
    val.to_core()
    val.to_near()
    att.finish()
    att_rows = Rows(h, r.att_all, r.att_rows, *r.att_rows_sems)
    att_rows.begin()
    key.to_across()
    val.to_across()

    @pl.when(moved)
    def _():
        for i in range(2):
            back(i).wait_recv()
            back(i).wait_send()
        r.output[...] = r.back_in[0]
        r.grad_x[...] = r.back_in[1].astype(F32)

    @pl.when(jnp.logical_not(moved))
    def _():
        r.output[...] = r.back_out[0]

    for name in ("ing", "inz", "que", "key", "val"):
        ch[name].finish()
    ffn_rows.finish()
    att_rows.finish()

    swap_sent(0, r.x, r.xs)
    swap_sent(1, r.cot, r.cots)
    for item in (xg, cg, ag, rg):
        item.sent()
    for item in (gain_p, qkv_p):
        item.sent()
    in_p.sent()
    for k in range(5):
        attn_copy(k).wait_send()

    @pl.when(active)
    def _():
        ffn_copy(1).wait_send()

    @pl.when(jnp.logical_and(active, near_own != h.f))
    def _():
        ffn_copy(0).wait_send()

    for i in range(RING - 1):
        exchange(i).wait_send()
    for i in range(5):
        sum_copy(i).wait_send()
    for name, _ in CHUNKS:
        ch[name].sent()


def finish_kernel(
    ing, inz, que, key, val, ffn, att, gains, y, dx, in_o, qkv_o, ffn_o, att_o, one_o, two_o, y_o, dx_o
):
    one_o[...] = gains[0:1, :]
    two_o[...] = gains[1:2, :]
    y_o[...] = y[...]
    dx_o[...] = dx[...]
    for q in range(4):
        for c in range(2):
            p = 4 * c + q
            for i, ref in enumerate((ing, inz)):
                start = i * FF + p * UNITS
                first = 8 * (q % 2)
                in_o[:, start : start + UNITS] = ref[q, c].astype(F32).T[:, first : first + UNITS]
            for i, ref in enumerate((que, key, val)):
                start = i * D + p * PAIR
                qkv_o[:, start : start + PAIR] = ref[q, c].astype(F32).T
    for half in range(2):
        first = 8 * half
        ffn_o[half * UNITS : (half + 1) * UNITS, :] = ffn[half].astype(F32)[first : first + UNITS]
        att_o[half * ATTN_ROWS : (half + 1) * ATTN_ROWS, :] = att[half].astype(F32)


def finish(ing, inz, que, key, val, ffn, att, gains, y, dx):
    def slices(high):
        return pl.BlockSpec((4, 2, high, 128), lambda i: (0, 0, 0, i))

    def rows(high):
        return pl.BlockSpec((2, high, D // 2), lambda i: (0, 0, i))

    own = pl.BlockSpec((y.shape[0] // 2, D), lambda i: (i, 0))
    return pl.pallas_call(
        finish_kernel,
        grid=(2,),
        out_shape=[
            jax.ShapeDtypeStruct((256, 2 * FF), F32),
            jax.ShapeDtypeStruct((256, 3 * D), F32),
            jax.ShapeDtypeStruct((2 * UNITS, D), F32),
            jax.ShapeDtypeStruct((2 * ATTN_ROWS, D), F32),
            jax.ShapeDtypeStruct((1, 256), F32),
            jax.ShapeDtypeStruct((1, 256), F32),
            jax.ShapeDtypeStruct(y.shape, BF16),
            jax.ShapeDtypeStruct(dx.shape, F32),
        ],
        in_specs=[slices(UNIT_ROWS)] * 2
        + [slices(ATTN_ROWS)] * 3
        + [rows(UNIT_ROWS), rows(ATTN_ROWS), pl.BlockSpec((8, 128), lambda i: (0, i)), own, own],
        out_specs=[
            pl.BlockSpec((128, 2 * FF), lambda i: (i, 0)),
            pl.BlockSpec((128, 3 * D), lambda i: (i, 0)),
            pl.BlockSpec((2 * UNITS, D // 2), lambda i: (0, i)),
            pl.BlockSpec((2 * ATTN_ROWS, D // 2), lambda i: (0, i)),
            pl.BlockSpec((1, 128), lambda i: (0, i)),
            pl.BlockSpec((1, 128), lambda i: (0, i)),
            own,
            own,
        ],
        compiler_params=pltpu.CompilerParams(vmem_limit_bytes=VMEM_BYTES),
    )(ing, inz, que, key, val, ffn, att, gains, y, dx)


def rotary_rows(length):
    half = HEAD_DIM // 2
    freq = (np.float32(ROPE_THETA) ** (-(np.arange(half, dtype=np.float32) * 2.0) / HEAD_DIM)).astype(
        np.float32
    )
    angles = np.arange(length, dtype=np.float32)[:, None] * freq[None, :]
    cos, sin = np.cos(angles), np.sin(angles)
    return np.tile(cos, (1, 4)), np.tile(np.concatenate([-sin, sin], axis=1), (1, 2))


def by_squares(inputs, gain_one, w_qkv, w_attn, gain_two, w_in, w_ffn, cotangent):
    seqs, tok, _ = inputs.shape
    rows = seqs * tok

    cos, sin = (jnp.asarray(t, F32) for t in rotary_rows(tok * RING))

    ins, outs, scratch = layout(seqs, tok)
    names, shapes = [], []
    for name, item in scratch.items():
        pair = item if isinstance(item, tuple) else (item,)
        names.append((name, len(pair)))
        shapes += pair

    def body(*refs):
        count = len(ins) + len(outs)
        rest = list(refs[count:])
        found = list(refs[:count])
        for _, size in names:
            taken = tuple(rest[:size])
            rest = rest[size:]
            found.append(taken if size > 1 else taken[0])
        layer_kernel(ins + list(outs) + [name for name, _ in names], *found)

    vmem = pl.BlockSpec(memory_space=pltpu.VMEM)
    hbm = pl.BlockSpec(memory_space=pl.ANY)
    done = pl.pallas_call(
        body,
        out_shape=[jax.ShapeDtypeStruct(shape, dtype) for shape, dtype in outs.values()],
        in_specs=[hbm if name in IN_HBM else vmem for name in ins],
        out_specs=[vmem] * len(outs),
        scratch_shapes=shapes,
        compiler_params=pltpu.CompilerParams(
            collective_id=0, has_side_effects=True, vmem_limit_bytes=VMEM_BYTES
        ),
    )(
        inputs.reshape(rows, D), cotangent.reshape(rows, D),
        gain_one.reshape(1, 256), gain_two.reshape(1, 256), w_qkv, w_attn, w_in, w_ffn, cos, sin,
    )
    done = dict(zip(outs, done))
    grad_in, grad_qkv, grad_ffn, grad_attn, grad_one, grad_two, output, grad_x = finish(
        done["ing_all"], done["inz_all"], done["que_all"], done["key_all"], done["val_all"],
        done["ffn_rows"], done["att_rows"], done["gains"], done["output"], done["grad_x"],
    )
    return (
        output.reshape(seqs, tok, D),
        grad_x.reshape(seqs, tok, D),
        grad_one.reshape(256),
        grad_qkv,
        grad_attn,
        grad_two.reshape(256),
        grad_in,
        grad_ffn,
    )


def solution(mesh):
    split_ok = mesh.shape["ctx"] == RING and mesh.shape["fsdp"] == OWNERS

    return jax.shard_map(
        by_squares if split_ok else on_device,
        mesh=mesh,
        in_specs=(
            P("fsdp", "ctx", None),
            P("fsdp"),
            P("fsdp", None),
            P("fsdp", None),
            P("fsdp"),
            P("fsdp", None),
            P("fsdp", None),
            P("fsdp", "ctx", None),
        ),
        out_specs=(
            P("fsdp", "ctx", None),
            P("fsdp", "ctx", None),
            P("fsdp"),
            P("fsdp", None),
            P("fsdp", None),
            P("fsdp"),
            P("fsdp", None),
            P("fsdp", None),
        ),
        check_vma=False,
    )
```

```python
import math

import jax
import jax.numpy as jnp
import numpy as np
from jax import lax
from jax.experimental import pallas as pl
from jax.experimental.pallas import tpu as pltpu
from jax.sharding import PartitionSpec as P

D = 1024
HEADS = 16
HEAD_DIM = 64
FF = 2624


EPSILON = 1e-05
ROPE_THETA = 160000.0


def norm_parts(values_in):
    mean_val = jnp.mean(values_in, axis=-1, keepdims=True)
    centred = values_in - mean_val
    variance = jnp.mean(centred * centred, axis=-1, keepdims=True)
    inv_std = lax.rsqrt(variance + EPSILON)
    return (centred * inv_std, inv_std)


def norm_back(grad_normed, normed, inv_std):
    return inv_std * (
        grad_normed
        - jnp.mean(grad_normed, axis=-1, keepdims=True)
        - normed * jnp.mean(grad_normed * normed, axis=-1, keepdims=True)
    )


def rotary_tables(positions):
    half_dim = HEAD_DIM // 2
    inv_freq = ROPE_THETA ** (-(jnp.arange(half_dim, dtype=jnp.float32) * 2.0) / HEAD_DIM)
    angles = positions.astype(jnp.float32)[:, None] * inv_freq[None, :]
    cosine = jnp.concatenate([jnp.cos(angles), jnp.cos(angles)], axis=-1)[:, None, :]
    sine_part = jnp.concatenate([jnp.sin(angles), jnp.sin(angles)], axis=-1)[:, None, :]
    return (cosine, sine_part)


def rotate(values_in, cosine, sine_part):
    half_dim = values_in.shape[-1] // 2
    turned = jnp.concatenate([-values_in[..., half_dim:], values_in[..., :half_dim]], axis=-1)
    return values_in * cosine + turned * sine_part


def rotate_back(grads, cosine, sine_part):
    half_dim = grads.shape[-1] // 2
    scaled = grads * sine_part
    turned = jnp.concatenate([scaled[..., half_dim:], -scaled[..., :half_dim]], axis=-1)
    return grads * cosine + turned


def gelu_slope(inner_part):
    cumulative = 0.5 * (1.0 + jax.scipy.special.erf(inner_part * 0.7071067811865476))
    density = jnp.exp(-0.5 * inner_part * inner_part) * 0.3989422804014327
    return cumulative + inner_part * density


def attend_piece(state_in, queries, key_piece, value_piece, scale_factor):
    row_max, row_sum, weighted = state_in
    scores = (
        jnp.einsum("bthd,bshd->bths", queries, key_piece, preferred_element_type=jnp.float32)
        * scale_factor
    )
    new_max = jnp.maximum(row_max, jnp.max(scores, axis=-1))
    rescale = jnp.exp(row_max - new_max)
    exp_vals = jnp.exp(scores - new_max[..., None])
    row_sum = row_sum * rescale + jnp.sum(exp_vals, axis=-1)
    weighted = weighted * rescale[..., None] + jnp.einsum(
        "bths,bshd->bthd",
        exp_vals.astype(jnp.bfloat16),
        value_piece,
        preferred_element_type=jnp.float32,
    )
    return (new_max, row_sum, weighted)


def back_piece(queries, grad_mixed, log_sum, row_delta, key_piece, value_piece, scale_factor):
    scores = (
        jnp.einsum("bthd,bshd->bths", queries, key_piece, preferred_element_type=jnp.float32)
        * scale_factor
    )
    probs = jnp.exp(scores - log_sum[..., None])
    grad_values = jnp.einsum(
        "bths,bthd->bshd",
        probs.astype(jnp.bfloat16),
        grad_mixed,
        preferred_element_type=jnp.float32,
    )
    grad_probs = jnp.einsum(
        "bthd,bshd->bths", grad_mixed, value_piece, preferred_element_type=jnp.float32
    )
    grad_scores = (probs * (grad_probs - row_delta[..., None])).astype(jnp.bfloat16)
    grad_query = (
        jnp.einsum("bths,bshd->bthd", grad_scores, key_piece, preferred_element_type=jnp.float32)
        * scale_factor
    )
    grad_keys = (
        jnp.einsum("bths,bthd->bshd", grad_scores, queries, preferred_element_type=jnp.float32)
        * scale_factor
    )
    return (grad_query, grad_keys, grad_values)


def add_at(whole_grads, piece_grads, offset):
    old_part = lax.dynamic_slice_in_dim(whole_grads, offset, piece_grads.shape[1], 1)
    return lax.dynamic_update_slice_in_dim(whole_grads, old_part + piece_grads, offset, 1)


def on_device(inputs, gain_one, w_qkv, w_attn, gain_two, w_in, w_ffn, cotangent):
    seq_dev = inputs.shape[0]
    tok_seq = inputs.shape[1]
    row_count = seq_dev * tok_seq
    seq_len = tok_seq * lax.axis_size("ctx")
    tokens_f = inputs.reshape(row_count, D).astype(jnp.float32)
    grad_out = cotangent.reshape(row_count, D)
    scale_factor = HEAD_DIM ** (-0.5)
    block_len = math.gcd(seq_len, 512)
    blocks_num = seq_len // block_len
    gathered = (
        lax.all_gather(gain_one, "fsdp", axis=0, tiled=True),
        lax.all_gather(w_qkv, "fsdp", axis=0, tiled=True),
        lax.all_gather(w_attn, "fsdp", axis=0, tiled=True),
        lax.all_gather(gain_two, "fsdp", axis=0, tiled=True),
        lax.all_gather(w_in, "fsdp", axis=0, tiled=True),
        lax.all_gather(w_ffn, "fsdp", axis=0, tiled=True),
    )
    full_g1, full_qkv, full_attn, full_g2, full_in, full_ffn = gathered
    normed_one, inv_one = norm_parts(tokens_f)
    input_one = (normed_one * full_g1.astype(jnp.float32)).astype(jnp.bfloat16)
    project = jnp.dot(input_one, full_qkv, preferred_element_type=jnp.float32)
    positions = lax.axis_index("ctx") * tok_seq + jnp.arange(tok_seq, dtype=jnp.int32)
    cosine, sine_part = rotary_tables(positions)
    shaped = project.reshape(seq_dev, tok_seq, 3, HEADS, HEAD_DIM)
    queries = rotate(shaped[:, :, 0], cosine, sine_part).astype(jnp.bfloat16)
    key_rows = rotate(shaped[:, :, 1], cosine, sine_part).astype(jnp.bfloat16)
    value_rows = shaped[:, :, 2].astype(jnp.bfloat16)
    start_state = (
        jnp.full((seq_dev, tok_seq, HEADS), -jnp.inf, jnp.float32),
        jnp.zeros((seq_dev, tok_seq, HEADS), jnp.float32),
        jnp.zeros((seq_dev, tok_seq, HEADS, HEAD_DIM), jnp.float32),
    )
    whole_keys, whole_values = (
        lax.all_gather(key_rows, "ctx", axis=1, tiled=True),
        lax.all_gather(value_rows, "ctx", axis=1, tiled=True),
    )

    def forward_step(state_in, block_index):
        begin = block_index * block_len
        key_piece = lax.dynamic_slice_in_dim(whole_keys, begin, block_len, 1)
        value_piece = lax.dynamic_slice_in_dim(whole_values, begin, block_len, 1)
        return (attend_piece(state_in, queries, key_piece, value_piece, scale_factor), None)

    state_out, unused = lax.scan(forward_step, start_state, jnp.arange(blocks_num, dtype=jnp.int32))
    row_max, row_sum, weighted = state_out
    attn_f = weighted / row_sum[..., None]
    log_sum = row_max + jnp.log(row_sum)
    attn_b = attn_f.reshape(row_count, D).astype(jnp.bfloat16)
    resid = tokens_f + jnp.dot(attn_b, full_attn, preferred_element_type=jnp.float32)
    normed_two, inv_two = norm_parts(resid)
    input_two = (normed_two * full_g2.astype(jnp.float32)).astype(jnp.bfloat16)
    widened = jnp.dot(input_two, full_in, preferred_element_type=jnp.float32)
    inner_part = widened[:, :FF]
    gating = widened[:, FF:]
    activated = jax.nn.gelu(inner_part, approximate=False)
    hidden = (activated * gating).astype(jnp.bfloat16)
    output = (resid + jnp.dot(hidden, full_ffn, preferred_element_type=jnp.float32)).astype(
        jnp.bfloat16
    )
    back_g1, back_qkv, back_attn, back_g2, back_in, back_ffn = gathered
    grad_ffn = jnp.dot(hidden.T, grad_out, preferred_element_type=jnp.float32)
    grad_hidden = jnp.dot(grad_out, back_ffn.T, preferred_element_type=jnp.float32)
    grad_inner = grad_hidden * gating * gelu_slope(inner_part)
    grad_gating = grad_hidden * activated
    grad_wide = jnp.concatenate([grad_inner, grad_gating], axis=-1).astype(jnp.bfloat16)
    grad_in = jnp.dot(input_two.T, grad_wide, preferred_element_type=jnp.float32)
    grad_normed_two = jnp.dot(grad_wide, back_in.T, preferred_element_type=jnp.float32)
    grad_g2 = jnp.sum(grad_normed_two * normed_two, axis=0)
    grad_resid = grad_out.astype(jnp.float32) + norm_back(
        grad_normed_two * back_g2.astype(jnp.float32), normed_two, inv_two
    )
    part_g2, part_in, part_ffn = (
        lax.psum_scatter(
            grad_g2.astype(jnp.bfloat16), "fsdp", scatter_dimension=0, tiled=True
        ).astype(jnp.float32),
        lax.psum_scatter(
            grad_in.astype(jnp.bfloat16), "fsdp", scatter_dimension=0, tiled=True
        ).astype(jnp.float32),
        lax.psum_scatter(
            grad_ffn.astype(jnp.bfloat16), "fsdp", scatter_dimension=0, tiled=True
        ).astype(jnp.float32),
    )
    resid_b = grad_resid.astype(jnp.bfloat16)
    grad_attn_w = jnp.dot(attn_b.T, resid_b, preferred_element_type=jnp.float32)
    grad_mixed = (
        jnp.dot(resid_b, back_attn.T, preferred_element_type=jnp.float32)
        .astype(jnp.bfloat16)
        .reshape(seq_dev, tok_seq, HEADS, HEAD_DIM)
    )
    row_delta = jnp.sum(grad_mixed.astype(jnp.float32) * attn_f, axis=-1)
    zero_q = jnp.zeros((seq_dev, tok_seq, HEADS, HEAD_DIM), jnp.float32)
    zero_kv = jnp.zeros((seq_dev, seq_len, HEADS, HEAD_DIM), jnp.float32)

    def backward_step(state_in, block_index):
        grad_q_sum, grad_key_all, grad_value_all = state_in
        begin = block_index * block_len
        key_piece = lax.dynamic_slice_in_dim(whole_keys, begin, block_len, 1)
        value_piece = lax.dynamic_slice_in_dim(whole_values, begin, block_len, 1)
        grad_query, grad_keys, grad_values = back_piece(
            queries, grad_mixed, log_sum, row_delta, key_piece, value_piece, scale_factor
        )
        return (
            (
                grad_q_sum + grad_query,
                add_at(grad_key_all, grad_keys, begin),
                add_at(grad_value_all, grad_values, begin),
            ),
            None,
        )

    back_state, unused_back = lax.scan(
        backward_step, (zero_q, zero_kv, zero_kv), jnp.arange(blocks_num, dtype=jnp.int32)
    )
    grad_q_sum, grad_key_all, grad_value_all = back_state
    own_keys, own_values = (
        lax.psum_scatter(
            grad_key_all.astype(jnp.bfloat16), "ctx", scatter_dimension=1, tiled=True
        ).astype(jnp.float32),
        lax.psum_scatter(
            grad_value_all.astype(jnp.bfloat16), "ctx", scatter_dimension=1, tiled=True
        ).astype(jnp.float32),
    )
    grad_q_rot = rotate_back(grad_q_sum, cosine, sine_part).reshape(row_count, D)
    grad_k_rot = rotate_back(own_keys, cosine, sine_part).reshape(row_count, D)
    grad_joint = jnp.concatenate(
        [grad_q_rot, grad_k_rot, own_values.reshape(row_count, D)], axis=-1
    ).astype(jnp.bfloat16)
    grad_qkv = jnp.dot(input_one.T, grad_joint, preferred_element_type=jnp.float32)
    grad_normed_one = jnp.dot(grad_joint, back_qkv.T, preferred_element_type=jnp.float32)
    grad_g1 = jnp.sum(grad_normed_one * normed_one, axis=0)
    grad_input = grad_resid + norm_back(
        grad_normed_one * back_g1.astype(jnp.float32), normed_one, inv_one
    )
    part_g1, part_qkv, part_attn = (
        lax.psum_scatter(
            grad_g1.astype(jnp.bfloat16), "fsdp", scatter_dimension=0, tiled=True
        ).astype(jnp.float32),
        lax.psum_scatter(
            grad_qkv.astype(jnp.bfloat16), "fsdp", scatter_dimension=0, tiled=True
        ).astype(jnp.float32),
        lax.psum_scatter(
            grad_attn_w.astype(jnp.bfloat16), "fsdp", scatter_dimension=0, tiled=True
        ).astype(jnp.float32),
    )
    totals = (
        lax.psum(part_g1.astype(jnp.bfloat16), "ctx").astype(jnp.float32),
        lax.psum(part_qkv.astype(jnp.bfloat16), "ctx").astype(jnp.float32),
        lax.psum(part_attn.astype(jnp.bfloat16), "ctx").astype(jnp.float32),
        lax.psum(part_g2.astype(jnp.bfloat16), "ctx").astype(jnp.float32),
        lax.psum(part_in.astype(jnp.bfloat16), "ctx").astype(jnp.float32),
        lax.psum(part_ffn.astype(jnp.bfloat16), "ctx").astype(jnp.float32),
    )
    return (
        output.reshape(seq_dev, tok_seq, D),
        grad_input.reshape(seq_dev, tok_seq, D),
        totals[0],
        totals[1],
        totals[2],
        totals[3],
        totals[4],
        totals[5],
    )


RING = 8
OWNERS = 4
PAIR = 2 * HEAD_DIM
UNITS = FF // RING
UNITS_PAD = 384
UNIT_ROWS = 336
WINDOW = 512
ATTN_ROWS = 128
MESH = pl.DeviceIdType.MESH
VMEM_BYTES = 60 * 1024 * 1024
F32 = jnp.float32
BF16 = jnp.bfloat16


def contract(left, right, left_dim, right_dim):
    return lax.dot_general(
        left, right, (((left_dim,), (right_dim,)), ((), ())), preferred_element_type=F32
    )


class Here:
    def __init__(self):
        b, f = lax.axis_index("ctx"), lax.axis_index("fsdp")
        x, low = b % 2, (b // 2) % 2
        self.b, self.f = b, f
        self.c, self.y, self.q, self.high, self.x, self.low = f % 2, f // 2, b % 4, b // 4, x, low
        self.bx, self.bz = b + 1 - 2 * x, b + 2 - 4 * low
        self.bd, self.bh = self.bx + 2 - 4 * low, (b + 4) % RING
        self.qx, self.qz = self.q + 1 - 2 * x, self.q + 2 - 4 * low
        self.qd = self.qx + 2 - 4 * low
        self.core = f + 1 - 2 * self.c
        self.far = (f + 2) % OWNERS
        self.diag = (self.core + 2) % OWNERS
        self.p = self.c * 4 + self.q

    def mine(self, q):
        return self.c * 4 + q

    def other(self, q):
        return (1 - self.c) * 4 + q

    def mine_of(self, c):
        return c * 4 + self.q

    def greet(self):
        barrier = pltpu.get_barrier_semaphore()
        peers = [(b, f) for b in (self.b, self.bx, self.bz, self.bd) for f in (self.f, self.core)]
        peers = peers[1:] + [
            (self.b, self.far), (self.b, self.diag), (self.bh, self.f), (self.bh, self.core),
        ]
        for peer in peers:
            pl.semaphore_signal(barrier, inc=1, device_id=peer, device_id_type=MESH)
        pl.semaphore_wait(barrier, len(peers))


def push(src, dst, send, recv, device):
    return pltpu.make_async_remote_copy(
        src_ref=src, dst_ref=dst, send_sem=send, recv_sem=recv, device_id=device, device_id_type=MESH
    )


class Gather:
    def __init__(self, here, buf, send, recv, split=True):
        h = here
        self.h, self.send_sem, self.recv_sem, self.split = h, send, recv, split
        high = buf.shape[1]
        half = high // 2
        top, bottom = pl.ds(0, half if split else high), pl.ds(half, half)
        own, near_x, near_z = buf.at[h.p], buf.at[h.mine(h.qx)], buf.at[h.mine(h.qz)]
        across = buf.at[h.mine(h.qd)]
        to_x, to_z, to_core = (h.bx, h.f), (h.bz, h.f), (h.b, h.core)
        self.out = [
            (own, to_x), (own, to_z), (near_z.at[top], to_x), (near_x.at[bottom], to_z),
            (own, to_core), (near_x, to_core), (near_z, to_core), (across, to_core),
        ]
        self.inn = [
            near_x, near_z, across.at[top], across.at[bottom],
            buf.at[h.other(h.q)], buf.at[h.other(h.qx)], buf.at[h.other(h.qz)], buf.at[h.other(h.qd)],
        ]

    def copy(self, kind):
        ref, device = self.out[kind]
        return push(ref, ref, self.send_sem.at[kind], self.recv_sem.at[kind], device)

    def wait(self, kind):
        ref = self.inn[kind]
        device = self.out[kind][1]
        push(ref, ref, self.send_sem.at[kind], self.recv_sem.at[kind], device).wait_recv()

    def begin(self):
        for kind in (0, 1, 4):
            self.copy(kind).start()

    def near(self):
        self.wait(0)
        if self.split:
            self.copy(3).start()
        self.copy(5).start()
        self.wait(1)
        self.copy(2).start()
        self.copy(6).start()

    def across(self):
        self.wait(2)
        if self.split:
            self.wait(3)
        self.copy(7).start()

    def sent(self):
        for kind in range(8):
            if kind != 3 or self.split:
                self.copy(kind).wait_send()

    def each(self, work, meanwhile=None, late=None):
        h = self.h
        work(h.p)
        self.wait(4)
        work(h.other(h.q))
        self.near()
        work(h.mine(h.qx))
        work(h.mine(h.qz))
        if meanwhile is not None:
            meanwhile()
        self.wait(5)
        work(h.other(h.qx))
        self.wait(6)
        work(h.other(h.qz))
        self.across()
        if late is not None:
            late()
        work(h.mine(h.qd))
        self.wait(7)
        work(h.other(h.qd))


class Scatter:
    def __init__(self, here, terms, core_out, near_out, across_out, core_in, near_in, across_in, send, recv, split):
        h = here
        self.h, self.terms, self.send_sem, self.recv_sem, self.split = h, terms, send, recv, split
        self.core_out, self.near_out, self.across_out = core_out, near_out, across_out
        self.core_in, self.near_in, self.across_in = core_in, near_in, across_in
        to_x, to_z, to_core = (h.bx, h.f), (h.bz, h.f), (h.b, h.core)
        self.out = [(core_out.at[i], core_in.at[i], to_core) for i in range(4)] + [
            (across_out.at[0], across_in.at[0], to_x),
            (across_out.at[1], across_in.at[1], to_z if split else to_x),
            (near_out.at[0], near_in.at[0], to_x),
            (near_out.at[1], near_in.at[1], to_z),
        ]
        self.half = terms.shape[1] // 2

    def copy(self, kind):
        src, dst, device = self.out[kind]
        return push(src, dst, self.send_sem.at[kind], self.recv_sem.at[kind], device)

    def wait(self, kind):
        self.copy(kind).wait_recv()

    def begin(self, work):
        h = self.h

        def send(i, q):
            work(h.other(q))
            self.core_out[i] = self.terms[h.other(q)].astype(BF16)
            self.copy(i).start()

        send(0, h.qd)
        work(h.mine(h.qd))
        send(1, h.qz)
        send(2, h.qx)
        self.first()
        work(h.mine(h.qz))
        work(h.mine(h.qx))
        send(3, h.q)
        work(h.p)

    def pair(self, i, q):
        return self.terms[self.h.mine(q)] + self.core_in[i].astype(F32)

    def first(self):
        self.wait(0)
        part = self.pair(0, self.h.qd).astype(BF16)
        self.across_out[0] = part[: self.half]
        self.copy(4).start()
        self.across_out[1] = part[self.half :]
        self.copy(5).start()

    def second(self):
        half = self.half
        self.wait(2)
        if not self.split:
            self.near_out[0] = self.pair(2, self.h.qx).astype(BF16)
            self.copy(6).start()
            self.wait(1)
            part = self.pair(1, self.h.qz)
            for i in range(2):
                rows = slice(i * half, (i + 1) * half)
                self.wait(4 + i)
                self.near_out[1, rows] = (part[rows] + self.across_in[i].astype(F32)).astype(BF16)
            self.copy(7).start()
            return
        self.wait(5)
        part = self.pair(2, self.h.qx)
        self.near_out[0, :half] = part[:half].astype(BF16)
        self.near_out[0, half:] = (part[half:] + self.across_in[1].astype(F32)).astype(BF16)
        self.copy(6).start()
        self.wait(1)
        self.wait(4)
        part = self.pair(1, self.h.qz)
        self.near_out[1, :half] = (part[:half] + self.across_in[0].astype(F32)).astype(BF16)
        self.near_out[1, half:] = part[half:].astype(BF16)
        self.copy(7).start()

    def finish(self):
        self.wait(3)
        total = self.pair(3, self.h.q)
        self.wait(6)
        self.wait(7)
        total = total + self.near_in[0].astype(F32) + self.near_in[1].astype(F32)
        for kind in range(8):
            self.copy(kind).wait_send()
        return total


class Grads:
    def __init__(self, here, g, far_in, high_in, core_out, whole, send, recv, split=False):
        h = here
        self.kinds = 7 if split else 6
        high = g.shape[2]
        top = high // 32 * 16 if split else high
        self.h, self.g, self.far_in, self.high_in = h, g, far_in, high_in
        self.core_out, self.whole, self.send_sem, self.recv_sem = core_out, whole, send, recv
        self.out = [
            (g.at[1 - h.y], far_in, (h.b, h.far)),
            (g.at[h.y], high_in, (h.bh, h.f)),
            (core_out, whole.at[h.q, h.c], (h.b, h.core)),
            (whole.at[h.q], whole.at[h.q], (h.bx, h.f)),
            (whole.at[h.q], whole.at[h.q], (h.bz, h.f)),
        ]
        for q, device, rows in (
            (h.qz, (h.bx, h.f), pl.ds(0, top)), (h.qx, (h.bz, h.f), pl.ds(top, high - top)),
        )[: self.kinds - 5]:
            self.out.append((whole.at[q, :, rows], whole.at[q, :, rows], device))
        self.inn = [far_in, high_in, whole.at[h.q, 1 - h.c], whole.at[h.qx], whole.at[h.qz]]
        for rows in (pl.ds(0, top), pl.ds(top, high - top))[: self.kinds - 5]:
            self.inn.append(whole.at[h.qd, :, rows])

    def copy(self, kind):
        src, dst, device = self.out[kind]
        return push(src, dst, self.send_sem.at[kind], self.recv_sem.at[kind], device)

    def wait(self, kind):
        ref, device = self.inn[kind], self.out[kind][2]
        push(ref, ref, self.send_sem.at[kind], self.recv_sem.at[kind], device).wait_recv()

    def to_far(self):
        self.copy(0).start()

    def from_far(self):
        self.wait(0)
        y = self.h.y
        self.g[y] = (self.g[y].astype(F32) + self.far_in[...].astype(F32)).astype(BF16)

    def to_high(self):
        self.copy(1).start()

    def total(self, c):
        return (self.g[self.h.y, c].astype(F32) + self.high_in[c].astype(F32)).astype(BF16)

    def to_core(self):
        self.wait(1)
        h = self.h
        self.core_out[...] = self.total(1 - h.c)
        self.copy(2).start()
        self.whole[h.q, h.c] = self.total(h.c)

    def to_near(self):
        self.wait(2)
        self.copy(3).start()
        self.copy(4).start()

    def to_across(self):
        self.wait(4)
        self.copy(5).start()
        self.wait(3)
        if self.kinds == 7:
            self.copy(6).start()

    def finish(self):
        for kind in range(5, self.kinds):
            self.wait(kind)

    def sent(self):
        for kind in range(self.kinds):
            self.copy(kind).wait_send()


class Rows:
    def __init__(self, here, whole, rows, send, recv):
        self.h, self.whole, self.rows, self.send_sem, self.recv_sem = here, whole, rows, send, recv

    def place(self, half, owner):
        return self.rows.at[half, :, pl.ds(pl.multiple_of(owner * 256, 256), 256)]

    def copy(self, q, c):
        h = self.h
        return push(
            self.whole.at[q, c], self.place(q % 2, h.f),
            self.send_sem.at[q, c], self.recv_sem.at[h.f, q % 2], (h.b, 2 * c + q // 2),
        )

    def begin(self):
        h = self.h
        for q in range(4):
            for c in range(2):
                owner = 2 * c + q // 2

                @pl.when(h.f != owner)
                def _(q=q, c=c):
                    self.copy(q, c).start()

                @pl.when(h.f == owner)
                def _(q=q, c=c, owner=owner):
                    self.rows[q % 2, :, owner * 256 : (owner + 1) * 256] = self.whole[q, c]

    def finish(self):
        h = self.h
        for owner in range(OWNERS):

            @pl.when(h.f != owner)
            def _(owner=owner):
                for half in range(2):
                    ref = self.place(half, owner)
                    push(
                        ref, ref, self.send_sem.at[0, 0], self.recv_sem.at[owner, half],
                        (h.b, owner),
                    ).wait_recv()

        for q in range(4):
            for c in range(2):

                @pl.when(h.f != 2 * c + q // 2)
                def _(q=q, c=c):
                    self.copy(q, c).wait_send()


def row_norm(rows):
    mean = jnp.mean(rows, axis=-1, keepdims=True)
    centred = rows - mean
    inv = lax.rsqrt(jnp.mean(centred * centred, axis=-1, keepdims=True) + EPSILON)
    return centred * inv, inv


def row_back(grad, normed, inv):
    return inv * (
        grad
        - jnp.mean(grad, axis=-1, keepdims=True)
        - normed * jnp.mean(grad * normed, axis=-1, keepdims=True)
    )


def first_half():
    lane = lax.broadcasted_iota(jnp.int32, (1, PAIR), 1)
    return lane % HEAD_DIM < HEAD_DIM // 2


def first_head():
    return lax.broadcasted_iota(jnp.int32, (1, PAIR), 1) < HEAD_DIM


def swap_halves(rows):
    up = pltpu.roll(rows, PAIR - HEAD_DIM // 2, 1)
    down = pltpu.roll(rows, HEAD_DIM // 2, 1)
    return jnp.where(first_half(), up, down)


def only(rows, head):
    keep = first_head() if head == 0 else jnp.logical_not(first_head())
    return jnp.where(keep, rows, jnp.zeros_like(rows))


def quarter(ref, j):
    tile = ref[:, :, j * 256 : (j + 1) * 256]
    return tile.reshape(tile.shape[0] * tile.shape[1], 256)


def flat(ref):
    rows = ref[...]
    return rows.reshape(rows.shape[0] * rows.shape[1], rows.shape[2])


class Box:
    pass


IN_HBM = ("w_qkv", "w_in", "w_ffn")
GATHERS = ("xg", "cg", "ag", "rg")
SCATTERS = ("two", "out", "one")
CHUNKS = (
    ("ffn", UNIT_ROWS), ("ing", UNIT_ROWS), ("inz", UNIT_ROWS),
    ("att", ATTN_ROWS), ("que", ATTN_ROWS), ("key", ATTN_ROWS), ("val", ATTN_ROWS),
)


def layout(seqs, tok):
    rows, length = seqs * tok, tok * RING
    whole = (RING, rows, D)
    half = rows // 2
    ins = [
        "x", "cot", "gain_one", "gain_two", "w_qkv", "attn_w", "w_in", "w_ffn", "cos", "sin",
    ]
    outs = {
        "output": ((rows, D), BF16),
        "grad_x": ((rows, D), F32),
        "gains": ((8, 256), F32),
        "ffn_rows": ((2, UNIT_ROWS, D), BF16),
        "att_rows": ((2, ATTN_ROWS, D), BF16),
    }
    for name, high in CHUNKS:
        if name not in ("ffn", "att"):
            outs[name + "_all"] = ((4, 2, high, 256), BF16)
    sem = pltpu.SemaphoreType.DMA
    vm = pltpu.VMEM
    scratch = {
        "xs": vm(whole, BF16), "cots": vm(whole, BF16), "a1": vm(whole, BF16), "a2": vm(whole, BF16),
        "resids": vm(whole, BF16), "terms": vm(whole, F32),
        "qkv_w": vm((2, 256, 3 * PAIR), BF16), "in_w": vm((2, 256, 2 * UNITS_PAD), BF16),
        "ffn_w": vm((UNIT_ROWS, D), BF16), "windows": vm((2, 2, 256, WINDOW), BF16),
        "gain": vm((8, 256), F32), "gain_all": vm((8, D), F32), "qkv_c": vm((D, 3 * PAIR), BF16), "attn_all": vm((D, D), BF16),
        "in_c": vm((D, 2 * UNITS_PAD), BF16), "ffn_c": vm((UNITS_PAD, D), BF16),
        "qs": vm((seqs, length, PAIR), BF16), "ks": vm((seqs, length, PAIR), BF16),
        "vs": vm((seqs, length, PAIR), BF16), "os": vm((seqs, length, PAIR), F32),
        "lse": vm((seqs, length, PAIR), F32), "heads": vm((RING, rows, PAIR), BF16),
        "own_heads": vm((RING, rows, PAIR), BF16), "mixed": vm((RING, rows, PAIR), BF16),
        "joint": vm((RING, rows, 3 * PAIR), BF16),
        "fs": vm((RING, rows, UNITS_PAD), BF16), "dus": vm((RING, rows, 2 * UNITS_PAD), BF16),
        "n2": vm((rows, D), F32), "resid": vm((rows, D), F32), "dy": vm((rows, D), F32),
        "core_out": vm((4, rows, D), BF16), "near_out": vm((2, rows, D), BF16),
        "across_out": vm((2, half, D), BF16),
        "back_out": vm((2, rows, D), BF16), "back_in": vm((2, rows, D), BF16),
        "sums": vm((6, 8, D), F32), "sums_in": vm((5, 8, D), F32),
        "ffn_all": vm((4, 2, UNIT_ROWS, 256), BF16), "att_all": vm((4, 2, ATTN_ROWS, 256), BF16),
    }
    for name in GATHERS:
        scratch[name + "_sems"] = (sem((8,)), sem((8,)))
    for name in SCATTERS:
        scratch[name + "_core"] = vm((4, rows, D), BF16)
        scratch[name + "_near"] = vm((2, rows, D), BF16)
        scratch[name + "_across"] = vm((2, half, D), BF16)
        scratch[name + "_sems"] = (sem((8,)), sem((8,)))
    for name, high in CHUNKS:
        scratch[name + "_g"] = vm((2, 2, high, 256), BF16)
        scratch[name + "_far"] = vm((2, high, 256), BF16)
        scratch[name + "_high"] = vm((2, high, 256), BF16)
        scratch[name + "_core"] = vm((high, 256), BF16)
        scratch[name + "_sems"] = (sem((7,)), sem((7,)))
    for name, count in (("swap", 4), ("part", 9), ("attn", 5), ("head", RING - 1), ("sum", 5)):
        scratch[name + "_sems"] = (sem((count,)), sem((count,)))
    scratch["ffn_w_sems"] = (sem((2,)), sem((1,)))
    scratch["cut_sems"] = (sem((2, 3)), sem((2, 2)), sem((1,)))
    for name in ("ffn_rows", "att_rows"):
        scratch[name + "_sems"] = (sem((4, 2)), sem((4, 2)))
    return ins, outs, scratch


def layer_kernel(names, *refs):
    r = Box()
    for name, ref in zip(names, refs):
        setattr(r, name, ref)
    h = Here()
    seqs, length = r.qs.shape[0], r.qs.shape[1]
    tok = length // RING
    scale = HEAD_DIM ** (-0.5)
    moved = h.high != h.c
    there = (h.bh, h.core)
    there_p = h.high * 4 + h.q
    cut_q, cut_i, cut_f = r.cut_sems

    def cut_qkv(c, i):
        start = i * D + h.mine_of(c) * PAIR
        return pltpu.make_async_copy(
            r.w_qkv.at[:, pl.ds(pl.multiple_of(start, PAIR), PAIR)],
            r.qkv_w.at[c, :, i * PAIR : (i + 1) * PAIR], cut_q.at[c, i],
        )

    def window(c, i):
        start = i * FF + h.mine_of(c) * UNITS
        return start, jnp.minimum(start // PAIR * PAIR, 2 * FF - WINDOW)

    def cut_in(c, i):
        return pltpu.make_async_copy(
            r.w_in.at[:, pl.ds(pl.multiple_of(window(c, i)[1], PAIR), WINDOW)],
            r.windows.at[c, i], cut_i.at[c, i],
        )

    cut_ffn = pltpu.make_async_copy(
        r.w_ffn.at[pl.ds(pl.multiple_of(h.x * (UNITS - 8), 16), UNIT_ROWS)], r.ffn_w, cut_f.at[0]
    )
    for c in range(2):
        for i in range(3):
            cut_qkv(c, i).start()
    for c in range(2):
        for i in range(2):
            cut_in(c, i).start()
    cut_ffn.start()

    h.greet()

    def swap(i, src, dst, back):
        send, recv = r.swap_sems
        return push(src, dst, send.at[i], recv.at[i], there)

    def swap_in(i, src, whole):
        @pl.when(moved)
        def _():
            swap(i, src, whole.at[there_p], False).start()

        @pl.when(jnp.logical_not(moved))
        def _():
            whole[h.p] = src[...]

    def swap_got(i, src, whole):
        @pl.when(moved)
        def _():
            swap(i, whole.at[h.p], whole.at[h.p], False).wait_recv()

    def swap_sent(i, src, whole):
        @pl.when(moved)
        def _():
            swap(i, src, whole.at[there_p], False).wait_send()

    swap_in(0, r.x, r.xs)

    p_send, p_recv = r.part_sems
    peers = (h.far, h.core, h.diag)

    def part_at(whole, owner, lanes):
        if lanes:
            return whole.at[:, pl.ds(pl.multiple_of(owner * 256, 256), 256)]
        return whole.at[pl.ds(pl.multiple_of(owner * 256, 256), 256)]

    def part(i, src, whole, lanes, sliced):
        def copy(k):
            mine = (h.c, 1 - h.c, 1 - h.c)[k]
            return push(
                src.at[mine] if sliced else src, part_at(whole, h.f, lanes),
                p_send.at[3 * i + k], p_recv.at[3 * i + k], (h.b, peers[k]),
            )

        box = Box()

        def begin():
            for k in range(3):
                copy(k).start()
            place = part_at(whole, h.f, lanes)
            place[...] = src[h.c] if sliced else src[...]

        def got():
            for k in range(3):
                ref = part_at(whole, peers[k], lanes)
                push(ref, ref, p_send.at[3 * i + k], p_recv.at[3 * i + k], (h.b, peers[k])).wait_recv()

        def sent():
            for k in range(3):
                copy(k).wait_send()

        box.begin, box.got, box.sent = begin, got, sent
        return box

    gain_p = part(0, r.gain, r.gain_all, True, False)
    qkv_p = part(1, r.qkv_w, r.qkv_c, False, True)
    in_p = part(2, r.in_w, r.in_c, False, True)

    def attn_half(owner, half):
        return r.attn_all.at[pl.ds(pl.multiple_of(owner * 256 + half * 128, 128), 128)]

    def attn_copy(k):
        own_half = pl.ds(pl.multiple_of(h.x * 128, 128), 128)
        came, later = attn_half(h.far, h.x), attn_half(h.far, 1 - h.x)
        src, dst, device = (
            (r.attn_w.at[own_half], attn_half(h.f, h.x), (h.b, h.far)),
            (r.attn_w, part_at(r.attn_all, h.f, False), (h.b, h.core)),
            (came, came, (h.bx, h.f)),
            (came, came, (h.b, h.core)),
            (later, later, (h.b, h.core)),
        )[k]
        return push(src, dst, a_send.at[k], a_recv.at[k], device)

    def attn_wait(k):
        ref = (
            attn_half(h.far, h.x), part_at(r.attn_all, h.core, False), attn_half(h.far, 1 - h.x),
            attn_half(h.diag, h.x), attn_half(h.diag, 1 - h.x),
        )[k]
        push(ref, ref, a_send.at[k], a_recv.at[k], (h.b, h.core)).wait_recv()

    a_send, a_recv = r.attn_sems
    f_send, f_recv = r.ffn_w_sems
    active = h.c == h.low
    near_own = 2 * h.y + h.y
    far_own = 2 * (1 - h.y) + h.y
    ffn_owner = 2 * h.c + h.low
    unit_rows = pl.ds(0, UNIT_ROWS)

    def ffn_copy(k):
        return push(
            r.ffn_w.at[unit_rows], r.ffn_c.at[unit_rows],
            f_send.at[k], f_recv.at[0], (h.b, (near_own, far_own)[k]),
        )

    r.gain[...] = jnp.zeros((8, 256), F32)
    r.gain[0:1, :] = r.gain_one[...].astype(F32).reshape(1, 256)
    r.gain[1:2, :] = r.gain_two[...].astype(F32).reshape(1, 256)
    gain_p.begin()
    for c in range(2):
        for i in range(3):
            cut_qkv(c, i).wait()
    qkv_p.begin()
    lane = lax.broadcasted_iota(jnp.int32, (1, WINDOW), 1)
    inside = jnp.logical_and(lane >= 8 * h.x, lane < 8 * h.x + UNITS)
    for c in range(2):
        for i in range(2):
            cut_in(c, i).wait()
            start, left = window(c, i)
            turned = pltpu.roll(
                r.windows[c, i].astype(F32), lax.rem(left - start + 8 * h.x + WINDOW, WINDOW), 1
            )
            kept = jnp.where(inside, turned, 0.0)[:, :UNITS_PAD]
            r.in_w[c, :, i * UNITS_PAD : (i + 1) * UNITS_PAD] = kept.astype(BF16)
    cut_ffn.wait()
    swap_got(0, r.x, r.xs)
    swap_in(1, r.cot, r.cots)
    xg = Gather(h, r.xs, *r.xg_sems)
    xg.begin()
    cg = Gather(h, r.cots, *r.cg_sems)

    @pl.when(jnp.logical_not(moved))
    def _():
        cg.begin()

    gain_p.got()
    qkv_p.got()
    attn_copy(0).start()
    attn_copy(1).start()
    at_own = part_at(r.attn_all, h.f, False)
    at_own[...] = r.attn_w[...]
    r.ffn_c[UNIT_ROWS:, :] = jnp.zeros((UNITS_PAD - UNIT_ROWS, D), BF16)

    @pl.when(ffn_owner == h.f)
    def _():
        r.ffn_c[unit_rows, :] = r.ffn_w[unit_rows, :]

    def project(index):
        normed, _ = row_norm(r.xs[index].astype(F32))
        a1 = (normed * r.gain_all[0:1, :]).astype(BF16)
        r.a1[index] = a1
        r.terms[index, :, : 3 * PAIR] = contract(a1, r.qkv_c[...], 1, 0)

    def more_weights():
        attn_wait(0)
        attn_copy(2).start()
        attn_copy(3).start()
        in_p.begin()

        @pl.when(jnp.logical_not(moved))
        def _():
            cg.near()

    xg.each(project, more_weights)

    for s in range(seqs):
        rows = slice(s * tok, (s + 1) * tok)

        def columns(i):
            return r.terms[:, rows, i * PAIR : (i + 1) * PAIR].reshape(length, PAIR)

        cos, sin = r.cos[...], r.sin[...]
        query, key = columns(0), columns(1)
        q = (query * cos + swap_halves(query) * sin).astype(BF16)
        k = (key * cos + swap_halves(key) * sin).astype(BF16)
        v = columns(2).astype(BF16)
        r.qs[s] = q
        r.ks[s] = k
        r.vs[s] = v
        outs, lses = [], []
        for head in range(2):
            scores = contract(only(q, head), k, 1, 1) * scale
            top = jnp.max(scores, axis=-1, keepdims=True)
            e = jnp.exp(scores - top)
            total = jnp.sum(e, axis=-1, keepdims=True)
            outs.append(contract(e.astype(BF16), v, 1, 0) / total)
            lses.append(top + jnp.log(total))
        of = jnp.where(first_head(), outs[0], outs[1])
        r.os[s] = of
        r.lse[s] = jnp.where(first_head(), lses[0], lses[1])
        r.heads[:, rows, :] = of.astype(BF16).reshape(RING, tok, PAIR)

    h_send, h_recv = r.head_sems
    around = []
    for b, q in ((h.b, h.q), (h.bx, h.qx), (h.bz, h.qz), (h.bd, h.qd)):
        around += [((b, h.f), h.mine(q)), ((b, h.core), h.other(q))]

    def exchange(i):
        device, p = around[i + 1]
        return push(r.heads.at[p], r.own_heads.at[h.p], h_send.at[i], h_recv.at[i], device)

    for i in range(RING - 1):
        exchange(i).start()
    r.own_heads[h.p] = r.heads[h.p]
    @pl.when(moved)
    def _():
        swap(1, r.cots.at[h.p], r.cots.at[h.p], False).wait_recv()
        cg.begin()

    attn_wait(2)
    attn_copy(4).start()
    attn_wait(1)
    attn_wait(3)
    attn_wait(4)
    for i in range(RING - 1):
        device, p = around[i + 1]
        ref = r.own_heads.at[p]
        push(ref, ref, h_send.at[i], h_recv.at[i], device).wait_recv()

    @pl.when(moved)
    def _():
        cg.near()

    g2 = r.gain_all[1:2, :]
    mixed_heads = jnp.concatenate([r.own_heads[d] for d in range(RING)], axis=1)
    resid = r.xs[h.p].astype(F32) + contract(mixed_heads, r.attn_all[...], 1, 0)
    r.resid[...] = resid
    normed, inv_two = row_norm(resid)
    r.n2[...] = normed
    r.a2[h.p] = (normed * g2).astype(BF16)
    ag = Gather(h, r.a2, *r.ag_sems)
    ag.begin()

    @pl.when(active)
    def _():
        ffn_copy(1).start()

    @pl.when(jnp.logical_and(active, near_own != h.f))
    def _():
        ffn_copy(0).start()

    in_p.got()

    def widen(index):
        r.terms[index, :, : 2 * UNITS_PAD] = contract(r.a2[index], r.in_c[...], 1, 0)

    ag.each(widen)
    cg.across()
    for kind in range(4, 8):
        cg.wait(kind)
    @pl.when(ffn_owner != h.f)
    def _():
        ffn_copy(0).wait_recv()

    def feed(index):
        inner = r.terms[index, :, :UNITS_PAD]
        gating = r.terms[index, :, UNITS_PAD : 2 * UNITS_PAD]
        below = 0.5 * (1.0 + lax.erf(inner * 0.7071067811865476))
        density = jnp.exp(-0.5 * inner * inner) * 0.3989422804014327
        active = inner * below
        r.fs[index] = (active * gating).astype(BF16)
        grad_hidden = contract(r.cots[index], r.ffn_c[...], 1, 1)
        du = jnp.concatenate(
            [grad_hidden * gating * (below + inner * density), grad_hidden * active], axis=1
        ).astype(BF16)
        r.dus[index] = du
        r.terms[index] = contract(du, r.in_c[...], 1, 1)

    def scatter(name, split):
        return Scatter(
            h, r.terms, r.core_out, r.near_out, r.across_out,
            getattr(r, name + "_core"), getattr(r, name + "_near"), getattr(r, name + "_across"),
            *getattr(r, name + "_sems"), split,
        )

    ch = {}
    for name, _ in CHUNKS:
        ch[name] = Grads(
            h, getattr(r, name + "_g"), getattr(r, name + "_far"), getattr(r, name + "_high"),
            getattr(r, name + "_core"), getattr(r, name + "_all"), *getattr(r, name + "_sems"),
            name not in ("ffn", "ing"),
        )

    ffn, ing, inz, att = ch["ffn"], ch["ing"], ch["inz"], ch["att"]
    que, key, val = ch["que"], ch["key"], ch["val"]
    two = scatter("two", True)
    two.begin(feed)
    for j in range(OWNERS):
        r.ffn_g[j // 2, j % 2] = contract(flat(r.fs), quarter(r.cots, j), 0, 0)[:UNIT_ROWS].astype(BF16)
    ffn.to_far()
    two.second()
    for j in range(OWNERS):
        c, y = j % 2, j // 2
        grad_in = contract(flat(r.dus), quarter(r.a2, j), 0, 0).astype(BF16)
        r.ing_g[y, c] = grad_in[:UNIT_ROWS]
        r.inz_g[y, c] = grad_in[UNITS_PAD : UNITS_PAD + UNIT_ROWS]
    grad_two = two.finish()

    normed = r.n2[...]
    r.sums[0, 1:2, :] = jnp.sum(grad_two * normed, axis=0, keepdims=True)
    own_grad = r.cots[h.p].astype(F32) + row_back(grad_two * g2, normed, inv_two)
    r.dy[...] = own_grad
    r.resids[h.p] = own_grad.astype(BF16)
    rg = Gather(h, r.resids, *r.rg_sems, False)
    rg.begin()
    ffn.from_far()
    ffn.to_high()
    ing.to_far()

    attn_c = r.attn_all.at[pl.ds(pl.multiple_of(h.p * PAIR, PAIR), PAIR)]

    def mix(index):
        r.mixed[index] = contract(r.resids[index], attn_c[...], 1, 1).astype(BF16)

    def ing_far():
        ing.from_far()
        inz.to_far()

    def ffn_on():
        ffn.to_core()
        ing.to_high()

    rg.each(mix, ing_far, ffn_on)
    for j in range(OWNERS):
        r.att_g[j // 2, j % 2] = contract(flat(r.heads), quarter(r.resids, j), 0, 0).astype(BF16)
    ffn.to_near()

    for s in range(seqs):
        rows = slice(s * tok, (s + 1) * tok)
        q, k, v = r.qs[s], r.ks[s], r.vs[s]
        do = r.mixed[:, rows, :].reshape(length, PAIR)
        weighed = do.astype(F32) * r.os[s]
        dqs, dks, dvs = [], [], []
        for head in range(2):
            delta = jnp.sum(only(weighed, head), axis=-1, keepdims=True)
            lse = r.lse[s, :, head * HEAD_DIM : head * HEAD_DIM + 1]
            probs = jnp.exp(contract(only(q, head), k, 1, 1) * scale - lse)
            dvs.append(contract(probs.astype(BF16), do, 0, 0))
            grad_probs = contract(only(do, head), v, 1, 1)
            ds = (probs * (grad_probs - delta)).astype(BF16)
            dqs.append(contract(ds, k, 1, 0) * scale)
            dks.append(contract(ds, q, 0, 0) * scale)
        cos, sin = r.cos[...], r.sin[...]
        dq = jnp.where(first_head(), dqs[0], dqs[1])
        dk = jnp.where(first_head(), dks[0], dks[1])
        dv = jnp.where(first_head(), dvs[0], dvs[1])
        for i, item in enumerate(
            (dq * cos - swap_halves(dq) * sin, dk * cos - swap_halves(dk) * sin, dv)
        ):
            r.joint[:, rows, i * PAIR : (i + 1) * PAIR] = item.astype(BF16).reshape(RING, tok, PAIR)
        if s == 0:
            inz.from_far()
            att.to_far()

    def term(i):
        r.terms[i] = contract(r.joint[i], r.qkv_c[...], 1, 1)

    one = scatter("one", False)
    one.begin(term)
    for j in range(OWNERS):
        grad_qkv = contract(flat(r.joint), quarter(r.a1, j), 0, 0).astype(BF16)
        for i, name in enumerate(("que", "key", "val")):
            getattr(r, name + "_g")[j // 2, j % 2] = grad_qkv[i * PAIR : (i + 1) * PAIR]
    ffn.to_across()
    ing.to_core()
    inz.to_high()
    one.second()
    att.from_far()
    for item in (que, key, val):
        item.to_far()

    grad_one = one.finish()
    normed, inv_one = row_norm(r.xs[h.p].astype(F32))
    r.sums[0, 0:1, :] = jnp.sum(grad_one * normed, axis=0, keepdims=True)
    r.sums[0, 2:, :] = jnp.zeros((6, D), F32)
    s_send, s_recv = r.sum_sems
    partners = ((h.b, h.core), (h.b, h.far), (h.bx, h.f), (h.bz, h.f), (h.bh, h.f))

    def sum_copy(i):
        return push(r.sums.at[i], r.sums_in.at[i], s_send.at[i], s_recv.at[i], partners[i])

    def sum_step(i):
        sum_copy(i).wait_recv()
        r.sums[i + 1] = r.sums[i] + r.sums_in[i]
        if i < 4:
            sum_copy(i + 1).start()

    def back(i):
        return swap(2 + i, r.back_out.at[i], r.back_in.at[i], True)

    sum_copy(0).start()
    grad_x = r.dy[...] + row_back(grad_one * r.gain_all[0:1, :], normed, inv_one)
    r.grad_x[...] = grad_x
    r.back_out[1] = grad_x.astype(BF16)

    @pl.when(moved)
    def _():
        back(1).start()

    ing.to_near()
    for item in (que, key, val):
        item.from_far()
    for item in (att, que, key, val):
        item.to_high()

    def out_term(i):
        r.terms[i] = contract(r.fs[i], r.ffn_c[...], 1, 0)

    out = scatter("out", False)
    out.begin(out_term)
    sum_step(0)
    sum_step(1)
    ing.to_across()
    out.second()
    sum_step(2)
    att.to_core()
    att.to_near()
    que.to_core()
    que.to_near()
    sum_step(3)
    inz.to_core()
    inz.to_near()
    att.to_across()
    ffn.finish()
    ffn_rows = Rows(h, r.ffn_all, r.ffn_rows, *r.ffn_rows_sems)
    ffn_rows.begin()
    key.to_core()
    key.to_near()
    inz.to_across()
    sum_step(4)
    r.gains[...] = r.sums[5, :, pl.ds(pl.multiple_of(h.f * 256, 256), 256)]
    val.to_core()
    val.to_near()
    r.back_out[0] = (r.resid[...] + out.finish()).astype(BF16)

    @pl.when(moved)
    def _():
        back(0).start()

    que.to_across()
    att.finish()
    att_rows = Rows(h, r.att_all, r.att_rows, *r.att_rows_sems)
    att_rows.begin()
    key.to_across()
    val.to_across()

    @pl.when(moved)
    def _():
        for i in range(2):
            back(i).wait_recv()
            back(i).wait_send()
        r.output[...] = r.back_in[0]
        r.grad_x[...] = r.back_in[1].astype(F32)

    @pl.when(jnp.logical_not(moved))
    def _():
        r.output[...] = r.back_out[0]

    for name in ("ing", "inz", "que", "key", "val"):
        ch[name].finish()
    ffn_rows.finish()
    att_rows.finish()

    swap_sent(0, r.x, r.xs)
    swap_sent(1, r.cot, r.cots)
    for item in (xg, cg, ag, rg):
        item.sent()
    for item in (gain_p, qkv_p):
        item.sent()
    in_p.sent()
    for k in range(5):
        attn_copy(k).wait_send()

    @pl.when(active)
    def _():
        ffn_copy(1).wait_send()

    @pl.when(jnp.logical_and(active, near_own != h.f))
    def _():
        ffn_copy(0).wait_send()

    for i in range(RING - 1):
        exchange(i).wait_send()
    for i in range(5):
        sum_copy(i).wait_send()
    for name, _ in CHUNKS:
        ch[name].sent()


def finish_kernel(
    ing, inz, que, key, val, ffn, att, gains, y, dx, in_o, qkv_o, ffn_o, att_o, one_o, two_o, y_o, dx_o
):
    one_o[...] = gains[0:1, :]
    two_o[...] = gains[1:2, :]
    y_o[...] = y[...]
    dx_o[...] = dx[...]
    for q in range(4):
        for c in range(2):
            p = 4 * c + q
            for i, ref in enumerate((ing, inz)):
                start = i * FF + p * UNITS
                first = 8 * (q % 2)
                in_o[:, start : start + UNITS] = ref[q, c].astype(F32).T[:, first : first + UNITS]
            for i, ref in enumerate((que, key, val)):
                start = i * D + p * PAIR
                qkv_o[:, start : start + PAIR] = ref[q, c].astype(F32).T
    for half in range(2):
        first = 8 * half
        ffn_o[half * UNITS : (half + 1) * UNITS, :] = ffn[half].astype(F32)[first : first + UNITS]
        att_o[half * ATTN_ROWS : (half + 1) * ATTN_ROWS, :] = att[half].astype(F32)


def finish(ing, inz, que, key, val, ffn, att, gains, y, dx):
    def slices(high):
        return pl.BlockSpec((4, 2, high, 128), lambda i: (0, 0, 0, i))

    def rows(high):
        return pl.BlockSpec((2, high, D // 2), lambda i: (0, 0, i))

    own = pl.BlockSpec((y.shape[0] // 2, D), lambda i: (i, 0))
    return pl.pallas_call(
        finish_kernel,
        grid=(2,),
        out_shape=[
            jax.ShapeDtypeStruct((256, 2 * FF), F32),
            jax.ShapeDtypeStruct((256, 3 * D), F32),
            jax.ShapeDtypeStruct((2 * UNITS, D), F32),
            jax.ShapeDtypeStruct((2 * ATTN_ROWS, D), F32),
            jax.ShapeDtypeStruct((1, 256), F32),
            jax.ShapeDtypeStruct((1, 256), F32),
            jax.ShapeDtypeStruct(y.shape, BF16),
            jax.ShapeDtypeStruct(dx.shape, F32),
        ],
        in_specs=[slices(UNIT_ROWS)] * 2
        + [slices(ATTN_ROWS)] * 3
        + [rows(UNIT_ROWS), rows(ATTN_ROWS), pl.BlockSpec((8, 128), lambda i: (0, i)), own, own],
        out_specs=[
            pl.BlockSpec((128, 2 * FF), lambda i: (i, 0)),
            pl.BlockSpec((128, 3 * D), lambda i: (i, 0)),
            pl.BlockSpec((2 * UNITS, D // 2), lambda i: (0, i)),
            pl.BlockSpec((2 * ATTN_ROWS, D // 2), lambda i: (0, i)),
            pl.BlockSpec((1, 128), lambda i: (0, i)),
            pl.BlockSpec((1, 128), lambda i: (0, i)),
            own,
            own,
        ],
        compiler_params=pltpu.CompilerParams(vmem_limit_bytes=VMEM_BYTES),
    )(ing, inz, que, key, val, ffn, att, gains, y, dx)


def rotary_rows(length):
    half = HEAD_DIM // 2
    freq = (np.float32(ROPE_THETA) ** (-(np.arange(half, dtype=np.float32) * 2.0) / HEAD_DIM)).astype(
        np.float32
    )
    angles = np.arange(length, dtype=np.float32)[:, None] * freq[None, :]
    cos, sin = np.cos(angles), np.sin(angles)
    return np.tile(cos, (1, 4)), np.tile(np.concatenate([-sin, sin], axis=1), (1, 2))


def by_squares(inputs, gain_one, w_qkv, w_attn, gain_two, w_in, w_ffn, cotangent):
    seqs, tok, _ = inputs.shape
    rows = seqs * tok

    cos, sin = (jnp.asarray(t, F32) for t in rotary_rows(tok * RING))

    ins, outs, scratch = layout(seqs, tok)
    names, shapes = [], []
    for name, item in scratch.items():
        pair = item if isinstance(item, tuple) else (item,)
        names.append((name, len(pair)))
        shapes += pair

    def body(*refs):
        count = len(ins) + len(outs)
        rest = list(refs[count:])
        found = list(refs[:count])
        for _, size in names:
            taken = tuple(rest[:size])
            rest = rest[size:]
            found.append(taken if size > 1 else taken[0])
        layer_kernel(ins + list(outs) + [name for name, _ in names], *found)

    vmem = pl.BlockSpec(memory_space=pltpu.VMEM)
    hbm = pl.BlockSpec(memory_space=pl.ANY)
    done = pl.pallas_call(
        body,
        out_shape=[jax.ShapeDtypeStruct(shape, dtype) for shape, dtype in outs.values()],
        in_specs=[hbm if name in IN_HBM else vmem for name in ins],
        out_specs=[vmem] * len(outs),
        scratch_shapes=shapes,
        compiler_params=pltpu.CompilerParams(
            collective_id=0, has_side_effects=True, vmem_limit_bytes=VMEM_BYTES
        ),
    )(
        inputs.reshape(rows, D), cotangent.reshape(rows, D),
        gain_one, gain_two, w_qkv, w_attn, w_in, w_ffn, cos, sin,
    )
    done = dict(zip(outs, done))
    grad_in, grad_qkv, grad_ffn, grad_attn, grad_one, grad_two, output, grad_x = finish(
        done["ing_all"], done["inz_all"], done["que_all"], done["key_all"], done["val_all"],
        done["ffn_rows"], done["att_rows"], done["gains"], done["output"], done["grad_x"],
    )
    return (
        output.reshape(seqs, tok, D),
        grad_x.reshape(seqs, tok, D),
        grad_one.reshape(256),
        grad_qkv,
        grad_attn,
        grad_two.reshape(256),
        grad_in,
        grad_ffn,
    )


def solution(mesh):
    split_ok = mesh.shape["ctx"] == RING and mesh.shape["fsdp"] == OWNERS

    return jax.shard_map(
        by_squares if split_ok else on_device,
        mesh=mesh,
        in_specs=(
            P("fsdp", "ctx", None),
            P("fsdp"),
            P("fsdp", None),
            P("fsdp", None),
            P("fsdp"),
            P("fsdp", None),
            P("fsdp", None),
            P("fsdp", "ctx", None),
        ),
        out_specs=(
            P("fsdp", "ctx", None),
            P("fsdp", "ctx", None),
            P("fsdp"),
            P("fsdp", None),
            P("fsdp", None),
            P("fsdp"),
            P("fsdp", None),
            P("fsdp", None),
        ),
        check_vma=False,
    )
```

```python
import math

import jax
import jax.numpy as jnp
import numpy as np
from jax import lax
from jax.experimental import pallas as pl
from jax.experimental.pallas import tpu as pltpu
from jax.sharding import PartitionSpec as P

D = 1024
HEADS = 16
HEAD_DIM = 64
FF = 2624


EPSILON = 1e-05
ROPE_THETA = 160000.0


def norm_parts(values_in):
    mean_val = jnp.mean(values_in, axis=-1, keepdims=True)
    centred = values_in - mean_val
    variance = jnp.mean(centred * centred, axis=-1, keepdims=True)
    inv_std = lax.rsqrt(variance + EPSILON)
    return (centred * inv_std, inv_std)


def norm_back(grad_normed, normed, inv_std):
    return inv_std * (
        grad_normed
        - jnp.mean(grad_normed, axis=-1, keepdims=True)
        - normed * jnp.mean(grad_normed * normed, axis=-1, keepdims=True)
    )


def rotary_tables(positions):
    half_dim = HEAD_DIM // 2
    inv_freq = ROPE_THETA ** (-(jnp.arange(half_dim, dtype=jnp.float32) * 2.0) / HEAD_DIM)
    angles = positions.astype(jnp.float32)[:, None] * inv_freq[None, :]
    cosine = jnp.concatenate([jnp.cos(angles), jnp.cos(angles)], axis=-1)[:, None, :]
    sine_part = jnp.concatenate([jnp.sin(angles), jnp.sin(angles)], axis=-1)[:, None, :]
    return (cosine, sine_part)


def rotate(values_in, cosine, sine_part):
    half_dim = values_in.shape[-1] // 2
    turned = jnp.concatenate([-values_in[..., half_dim:], values_in[..., :half_dim]], axis=-1)
    return values_in * cosine + turned * sine_part


def rotate_back(grads, cosine, sine_part):
    half_dim = grads.shape[-1] // 2
    scaled = grads * sine_part
    turned = jnp.concatenate([scaled[..., half_dim:], -scaled[..., :half_dim]], axis=-1)
    return grads * cosine + turned


def gelu_slope(inner_part):
    cumulative = 0.5 * (1.0 + jax.scipy.special.erf(inner_part * 0.7071067811865476))
    density = jnp.exp(-0.5 * inner_part * inner_part) * 0.3989422804014327
    return cumulative + inner_part * density


def attend_piece(state_in, queries, key_piece, value_piece, scale_factor):
    row_max, row_sum, weighted = state_in
    scores = (
        jnp.einsum("bthd,bshd->bths", queries, key_piece, preferred_element_type=jnp.float32)
        * scale_factor
    )
    new_max = jnp.maximum(row_max, jnp.max(scores, axis=-1))
    rescale = jnp.exp(row_max - new_max)
    exp_vals = jnp.exp(scores - new_max[..., None])
    row_sum = row_sum * rescale + jnp.sum(exp_vals, axis=-1)
    weighted = weighted * rescale[..., None] + jnp.einsum(
        "bths,bshd->bthd",
        exp_vals.astype(jnp.bfloat16),
        value_piece,
        preferred_element_type=jnp.float32,
    )
    return (new_max, row_sum, weighted)


def back_piece(queries, grad_mixed, log_sum, row_delta, key_piece, value_piece, scale_factor):
    scores = (
        jnp.einsum("bthd,bshd->bths", queries, key_piece, preferred_element_type=jnp.float32)
        * scale_factor
    )
    probs = jnp.exp(scores - log_sum[..., None])
    grad_values = jnp.einsum(
        "bths,bthd->bshd",
        probs.astype(jnp.bfloat16),
        grad_mixed,
        preferred_element_type=jnp.float32,
    )
    grad_probs = jnp.einsum(
        "bthd,bshd->bths", grad_mixed, value_piece, preferred_element_type=jnp.float32
    )
    grad_scores = (probs * (grad_probs - row_delta[..., None])).astype(jnp.bfloat16)
    grad_query = (
        jnp.einsum("bths,bshd->bthd", grad_scores, key_piece, preferred_element_type=jnp.float32)
        * scale_factor
    )
    grad_keys = (
        jnp.einsum("bths,bthd->bshd", grad_scores, queries, preferred_element_type=jnp.float32)
        * scale_factor
    )
    return (grad_query, grad_keys, grad_values)


def add_at(whole_grads, piece_grads, offset):
    old_part = lax.dynamic_slice_in_dim(whole_grads, offset, piece_grads.shape[1], 1)
    return lax.dynamic_update_slice_in_dim(whole_grads, old_part + piece_grads, offset, 1)


def on_device(inputs, gain_one, w_qkv, w_attn, gain_two, w_in, w_ffn, cotangent):
    seq_dev = inputs.shape[0]
    tok_seq = inputs.shape[1]
    row_count = seq_dev * tok_seq
    seq_len = tok_seq * lax.axis_size("ctx")
    tokens_f = inputs.reshape(row_count, D).astype(jnp.float32)
    grad_out = cotangent.reshape(row_count, D)
    scale_factor = HEAD_DIM ** (-0.5)
    block_len = math.gcd(seq_len, 512)
    blocks_num = seq_len // block_len
    gathered = (
        lax.all_gather(gain_one, "fsdp", axis=0, tiled=True),
        lax.all_gather(w_qkv, "fsdp", axis=0, tiled=True),
        lax.all_gather(w_attn, "fsdp", axis=0, tiled=True),
        lax.all_gather(gain_two, "fsdp", axis=0, tiled=True),
        lax.all_gather(w_in, "fsdp", axis=0, tiled=True),
        lax.all_gather(w_ffn, "fsdp", axis=0, tiled=True),
    )
    full_g1, full_qkv, full_attn, full_g2, full_in, full_ffn = gathered
    normed_one, inv_one = norm_parts(tokens_f)
    input_one = (normed_one * full_g1.astype(jnp.float32)).astype(jnp.bfloat16)
    project = jnp.dot(input_one, full_qkv, preferred_element_type=jnp.float32)
    positions = lax.axis_index("ctx") * tok_seq + jnp.arange(tok_seq, dtype=jnp.int32)
    cosine, sine_part = rotary_tables(positions)
    shaped = project.reshape(seq_dev, tok_seq, 3, HEADS, HEAD_DIM)
    queries = rotate(shaped[:, :, 0], cosine, sine_part).astype(jnp.bfloat16)
    key_rows = rotate(shaped[:, :, 1], cosine, sine_part).astype(jnp.bfloat16)
    value_rows = shaped[:, :, 2].astype(jnp.bfloat16)
    start_state = (
        jnp.full((seq_dev, tok_seq, HEADS), -jnp.inf, jnp.float32),
        jnp.zeros((seq_dev, tok_seq, HEADS), jnp.float32),
        jnp.zeros((seq_dev, tok_seq, HEADS, HEAD_DIM), jnp.float32),
    )
    whole_keys, whole_values = (
        lax.all_gather(key_rows, "ctx", axis=1, tiled=True),
        lax.all_gather(value_rows, "ctx", axis=1, tiled=True),
    )

    def forward_step(state_in, block_index):
        begin = block_index * block_len
        key_piece = lax.dynamic_slice_in_dim(whole_keys, begin, block_len, 1)
        value_piece = lax.dynamic_slice_in_dim(whole_values, begin, block_len, 1)
        return (attend_piece(state_in, queries, key_piece, value_piece, scale_factor), None)

    state_out, unused = lax.scan(forward_step, start_state, jnp.arange(blocks_num, dtype=jnp.int32))
    row_max, row_sum, weighted = state_out
    attn_f = weighted / row_sum[..., None]
    log_sum = row_max + jnp.log(row_sum)
    attn_b = attn_f.reshape(row_count, D).astype(jnp.bfloat16)
    resid = tokens_f + jnp.dot(attn_b, full_attn, preferred_element_type=jnp.float32)
    normed_two, inv_two = norm_parts(resid)
    input_two = (normed_two * full_g2.astype(jnp.float32)).astype(jnp.bfloat16)
    widened = jnp.dot(input_two, full_in, preferred_element_type=jnp.float32)
    inner_part = widened[:, :FF]
    gating = widened[:, FF:]
    activated = jax.nn.gelu(inner_part, approximate=False)
    hidden = (activated * gating).astype(jnp.bfloat16)
    output = (resid + jnp.dot(hidden, full_ffn, preferred_element_type=jnp.float32)).astype(
        jnp.bfloat16
    )
    back_g1, back_qkv, back_attn, back_g2, back_in, back_ffn = gathered
    grad_ffn = jnp.dot(hidden.T, grad_out, preferred_element_type=jnp.float32)
    grad_hidden = jnp.dot(grad_out, back_ffn.T, preferred_element_type=jnp.float32)
    grad_inner = grad_hidden * gating * gelu_slope(inner_part)
    grad_gating = grad_hidden * activated
    grad_wide = jnp.concatenate([grad_inner, grad_gating], axis=-1).astype(jnp.bfloat16)
    grad_in = jnp.dot(input_two.T, grad_wide, preferred_element_type=jnp.float32)
    grad_normed_two = jnp.dot(grad_wide, back_in.T, preferred_element_type=jnp.float32)
    grad_g2 = jnp.sum(grad_normed_two * normed_two, axis=0)
    grad_resid = grad_out.astype(jnp.float32) + norm_back(
        grad_normed_two * back_g2.astype(jnp.float32), normed_two, inv_two
    )
    part_g2, part_in, part_ffn = (
        lax.psum_scatter(
            grad_g2.astype(jnp.bfloat16), "fsdp", scatter_dimension=0, tiled=True
        ).astype(jnp.float32),
        lax.psum_scatter(
            grad_in.astype(jnp.bfloat16), "fsdp", scatter_dimension=0, tiled=True
        ).astype(jnp.float32),
        lax.psum_scatter(
            grad_ffn.astype(jnp.bfloat16), "fsdp", scatter_dimension=0, tiled=True
        ).astype(jnp.float32),
    )
    resid_b = grad_resid.astype(jnp.bfloat16)
    grad_attn_w = jnp.dot(attn_b.T, resid_b, preferred_element_type=jnp.float32)
    grad_mixed = (
        jnp.dot(resid_b, back_attn.T, preferred_element_type=jnp.float32)
        .astype(jnp.bfloat16)
        .reshape(seq_dev, tok_seq, HEADS, HEAD_DIM)
    )
    row_delta = jnp.sum(grad_mixed.astype(jnp.float32) * attn_f, axis=-1)
    zero_q = jnp.zeros((seq_dev, tok_seq, HEADS, HEAD_DIM), jnp.float32)
    zero_kv = jnp.zeros((seq_dev, seq_len, HEADS, HEAD_DIM), jnp.float32)

    def backward_step(state_in, block_index):
        grad_q_sum, grad_key_all, grad_value_all = state_in
        begin = block_index * block_len
        key_piece = lax.dynamic_slice_in_dim(whole_keys, begin, block_len, 1)
        value_piece = lax.dynamic_slice_in_dim(whole_values, begin, block_len, 1)
        grad_query, grad_keys, grad_values = back_piece(
            queries, grad_mixed, log_sum, row_delta, key_piece, value_piece, scale_factor
        )
        return (
            (
                grad_q_sum + grad_query,
                add_at(grad_key_all, grad_keys, begin),
                add_at(grad_value_all, grad_values, begin),
            ),
            None,
        )

    back_state, unused_back = lax.scan(
        backward_step, (zero_q, zero_kv, zero_kv), jnp.arange(blocks_num, dtype=jnp.int32)
    )
    grad_q_sum, grad_key_all, grad_value_all = back_state
    own_keys, own_values = (
        lax.psum_scatter(
            grad_key_all.astype(jnp.bfloat16), "ctx", scatter_dimension=1, tiled=True
        ).astype(jnp.float32),
        lax.psum_scatter(
            grad_value_all.astype(jnp.bfloat16), "ctx", scatter_dimension=1, tiled=True
        ).astype(jnp.float32),
    )
    grad_q_rot = rotate_back(grad_q_sum, cosine, sine_part).reshape(row_count, D)
    grad_k_rot = rotate_back(own_keys, cosine, sine_part).reshape(row_count, D)
    grad_joint = jnp.concatenate(
        [grad_q_rot, grad_k_rot, own_values.reshape(row_count, D)], axis=-1
    ).astype(jnp.bfloat16)
    grad_qkv = jnp.dot(input_one.T, grad_joint, preferred_element_type=jnp.float32)
    grad_normed_one = jnp.dot(grad_joint, back_qkv.T, preferred_element_type=jnp.float32)
    grad_g1 = jnp.sum(grad_normed_one * normed_one, axis=0)
    grad_input = grad_resid + norm_back(
        grad_normed_one * back_g1.astype(jnp.float32), normed_one, inv_one
    )
    part_g1, part_qkv, part_attn = (
        lax.psum_scatter(
            grad_g1.astype(jnp.bfloat16), "fsdp", scatter_dimension=0, tiled=True
        ).astype(jnp.float32),
        lax.psum_scatter(
            grad_qkv.astype(jnp.bfloat16), "fsdp", scatter_dimension=0, tiled=True
        ).astype(jnp.float32),
        lax.psum_scatter(
            grad_attn_w.astype(jnp.bfloat16), "fsdp", scatter_dimension=0, tiled=True
        ).astype(jnp.float32),
    )
    totals = (
        lax.psum(part_g1.astype(jnp.bfloat16), "ctx").astype(jnp.float32),
        lax.psum(part_qkv.astype(jnp.bfloat16), "ctx").astype(jnp.float32),
        lax.psum(part_attn.astype(jnp.bfloat16), "ctx").astype(jnp.float32),
        lax.psum(part_g2.astype(jnp.bfloat16), "ctx").astype(jnp.float32),
        lax.psum(part_in.astype(jnp.bfloat16), "ctx").astype(jnp.float32),
        lax.psum(part_ffn.astype(jnp.bfloat16), "ctx").astype(jnp.float32),
    )
    return (
        output.reshape(seq_dev, tok_seq, D),
        grad_input.reshape(seq_dev, tok_seq, D),
        totals[0],
        totals[1],
        totals[2],
        totals[3],
        totals[4],
        totals[5],
    )


RING = 8
OWNERS = 4
PAIR = 2 * HEAD_DIM
UNITS = FF // RING
UNITS_PAD = 384
UNIT_ROWS = 336
WINDOW = 512
ATTN_ROWS = 128
MESH = pl.DeviceIdType.MESH
VMEM_BYTES = 60 * 1024 * 1024
F32 = jnp.float32
BF16 = jnp.bfloat16


def contract(left, right, left_dim, right_dim):
    return lax.dot_general(
        left, right, (((left_dim,), (right_dim,)), ((), ())), preferred_element_type=F32
    )


class Here:
    def __init__(self):
        b, f = lax.axis_index("ctx"), lax.axis_index("fsdp")
        x, low = b % 2, (b // 2) % 2
        self.b, self.f = b, f
        self.c, self.y, self.q, self.high, self.x, self.low = f % 2, f // 2, b % 4, b // 4, x, low
        self.bx, self.bz = b + 1 - 2 * x, b + 2 - 4 * low
        self.bd, self.bh = self.bx + 2 - 4 * low, (b + 4) % RING
        self.qx, self.qz = self.q + 1 - 2 * x, self.q + 2 - 4 * low
        self.qd = self.qx + 2 - 4 * low
        self.core = f + 1 - 2 * self.c
        self.far = (f + 2) % OWNERS
        self.diag = (self.core + 2) % OWNERS
        self.p = self.c * 4 + self.q

    def mine(self, q):
        return self.c * 4 + q

    def other(self, q):
        return (1 - self.c) * 4 + q

    def mine_of(self, c):
        return c * 4 + self.q

    def greet(self):
        barrier = pltpu.get_barrier_semaphore()
        peers = [(b, f) for b in (self.b, self.bx, self.bz, self.bd) for f in (self.f, self.core)]
        peers = peers[1:] + [
            (self.b, self.far), (self.b, self.diag), (self.bh, self.f), (self.bh, self.core),
        ]
        for peer in peers:
            pl.semaphore_signal(barrier, inc=1, device_id=peer, device_id_type=MESH)
        pl.semaphore_wait(barrier, len(peers))


def push(src, dst, send, recv, device):
    return pltpu.make_async_remote_copy(
        src_ref=src, dst_ref=dst, send_sem=send, recv_sem=recv, device_id=device, device_id_type=MESH
    )


class Gather:
    def __init__(self, here, buf, send, recv, split=True):
        h = here
        self.h, self.send_sem, self.recv_sem, self.split = h, send, recv, split
        high = buf.shape[1]
        half = high // 2
        top, bottom = pl.ds(0, half if split else high), pl.ds(half, half)
        own, near_x, near_z = buf.at[h.p], buf.at[h.mine(h.qx)], buf.at[h.mine(h.qz)]
        across = buf.at[h.mine(h.qd)]
        to_x, to_z, to_core = (h.bx, h.f), (h.bz, h.f), (h.b, h.core)
        self.out = [
            (own, to_x), (own, to_z), (near_z.at[top], to_x), (near_x.at[bottom], to_z),
            (own, to_core), (near_x, to_core), (near_z, to_core), (across, to_core),
        ]
        self.inn = [
            near_x, near_z, across.at[top], across.at[bottom],
            buf.at[h.other(h.q)], buf.at[h.other(h.qx)], buf.at[h.other(h.qz)], buf.at[h.other(h.qd)],
        ]

    def copy(self, kind):
        ref, device = self.out[kind]
        return push(ref, ref, self.send_sem.at[kind], self.recv_sem.at[kind], device)

    def wait(self, kind):
        ref = self.inn[kind]
        device = self.out[kind][1]
        push(ref, ref, self.send_sem.at[kind], self.recv_sem.at[kind], device).wait_recv()

    def begin(self):
        for kind in (0, 1, 4):
            self.copy(kind).start()

    def near(self):
        self.wait(0)
        if self.split:
            self.copy(3).start()
        self.copy(5).start()
        self.wait(1)
        self.copy(2).start()
        self.copy(6).start()

    def across(self):
        self.wait(2)
        if self.split:
            self.wait(3)
        self.copy(7).start()

    def sent(self):
        for kind in range(8):
            if kind != 3 or self.split:
                self.copy(kind).wait_send()

    def each(self, work, meanwhile=None, late=None):
        h = self.h
        work(h.p)
        self.wait(4)
        work(h.other(h.q))
        self.near()
        work(h.mine(h.qx))
        work(h.mine(h.qz))
        if meanwhile is not None:
            meanwhile()
        self.wait(5)
        work(h.other(h.qx))
        self.wait(6)
        work(h.other(h.qz))
        self.across()
        if late is not None:
            late()
        work(h.mine(h.qd))
        self.wait(7)
        work(h.other(h.qd))


class Scatter:
    def __init__(self, here, terms, core_out, near_out, across_out, core_in, near_in, across_in, send, recv, split):
        h = here
        self.h, self.terms, self.send_sem, self.recv_sem, self.split = h, terms, send, recv, split
        self.core_out, self.near_out, self.across_out = core_out, near_out, across_out
        self.core_in, self.near_in, self.across_in = core_in, near_in, across_in
        to_x, to_z, to_core = (h.bx, h.f), (h.bz, h.f), (h.b, h.core)
        self.out = [(core_out.at[i], core_in.at[i], to_core) for i in range(4)] + [
            (across_out.at[0], across_in.at[0], to_x),
            (across_out.at[1], across_in.at[1], to_z if split else to_x),
            (near_out.at[0], near_in.at[0], to_x),
            (near_out.at[1], near_in.at[1], to_z),
        ]
        self.half = terms.shape[1] // 2

    def copy(self, kind):
        src, dst, device = self.out[kind]
        return push(src, dst, self.send_sem.at[kind], self.recv_sem.at[kind], device)

    def wait(self, kind):
        self.copy(kind).wait_recv()

    def begin(self, work):
        h = self.h

        def send(i, q):
            work(h.other(q))
            self.core_out[i] = self.terms[h.other(q)].astype(BF16)
            self.copy(i).start()

        send(0, h.qd)
        work(h.mine(h.qd))
        send(1, h.qz)
        send(2, h.qx)
        self.first()
        work(h.mine(h.qz))
        work(h.mine(h.qx))
        send(3, h.q)
        work(h.p)

    def pair(self, i, q):
        return self.terms[self.h.mine(q)] + self.core_in[i].astype(F32)

    def first(self):
        self.wait(0)
        part = self.pair(0, self.h.qd).astype(BF16)
        self.across_out[0] = part[: self.half]
        self.copy(4).start()
        self.across_out[1] = part[self.half :]
        self.copy(5).start()

    def second(self):
        half = self.half
        self.wait(2)
        if not self.split:
            self.near_out[0] = self.pair(2, self.h.qx).astype(BF16)
            self.copy(6).start()
            self.wait(1)
            part = self.pair(1, self.h.qz)
            for i in range(2):
                rows = slice(i * half, (i + 1) * half)
                self.wait(4 + i)
                self.near_out[1, rows] = (part[rows] + self.across_in[i].astype(F32)).astype(BF16)
            self.copy(7).start()
            return
        self.wait(5)
        part = self.pair(2, self.h.qx)
        self.near_out[0, :half] = part[:half].astype(BF16)
        self.near_out[0, half:] = (part[half:] + self.across_in[1].astype(F32)).astype(BF16)
        self.copy(6).start()
        self.wait(1)
        self.wait(4)
        part = self.pair(1, self.h.qz)
        self.near_out[1, :half] = (part[:half] + self.across_in[0].astype(F32)).astype(BF16)
        self.near_out[1, half:] = part[half:].astype(BF16)
        self.copy(7).start()

    def finish(self):
        self.wait(3)
        total = self.pair(3, self.h.q)
        self.wait(6)
        self.wait(7)
        total = total + self.near_in[0].astype(F32) + self.near_in[1].astype(F32)
        for kind in range(8):
            self.copy(kind).wait_send()
        return total


class Grads:
    def __init__(self, here, g, far_in, high_in, core_out, whole, send, recv, split=False):
        h = here
        self.kinds = 7 if split else 6
        high = g.shape[2]
        top = high // 32 * 16 if split else high
        self.h, self.g, self.far_in, self.high_in = h, g, far_in, high_in
        self.core_out, self.whole, self.send_sem, self.recv_sem = core_out, whole, send, recv
        self.out = [
            (g.at[1 - h.y], far_in, (h.b, h.far)),
            (g.at[h.y], high_in, (h.bh, h.f)),
            (core_out, whole.at[h.q, h.c], (h.b, h.core)),
            (whole.at[h.q], whole.at[h.q], (h.bx, h.f)),
            (whole.at[h.q], whole.at[h.q], (h.bz, h.f)),
        ]
        for q, device, rows in (
            (h.qz, (h.bx, h.f), pl.ds(0, top)), (h.qx, (h.bz, h.f), pl.ds(top, high - top)),
        )[: self.kinds - 5]:
            self.out.append((whole.at[q, :, rows], whole.at[q, :, rows], device))
        self.inn = [far_in, high_in, whole.at[h.q, 1 - h.c], whole.at[h.qx], whole.at[h.qz]]
        for rows in (pl.ds(0, top), pl.ds(top, high - top))[: self.kinds - 5]:
            self.inn.append(whole.at[h.qd, :, rows])

    def copy(self, kind):
        src, dst, device = self.out[kind]
        return push(src, dst, self.send_sem.at[kind], self.recv_sem.at[kind], device)

    def wait(self, kind):
        ref, device = self.inn[kind], self.out[kind][2]
        push(ref, ref, self.send_sem.at[kind], self.recv_sem.at[kind], device).wait_recv()

    def to_far(self):
        self.copy(0).start()

    def from_far(self):
        self.wait(0)
        y = self.h.y
        self.g[y] = (self.g[y].astype(F32) + self.far_in[...].astype(F32)).astype(BF16)

    def to_high(self):
        self.copy(1).start()

    def total(self, c):
        return (self.g[self.h.y, c].astype(F32) + self.high_in[c].astype(F32)).astype(BF16)

    def to_core(self):
        self.wait(1)
        h = self.h
        self.core_out[...] = self.total(1 - h.c)
        self.copy(2).start()
        self.whole[h.q, h.c] = self.total(h.c)

    def to_near(self):
        self.wait(2)
        self.copy(3).start()
        self.copy(4).start()

    def to_across(self):
        self.wait(4)
        self.copy(5).start()
        self.wait(3)
        if self.kinds == 7:
            self.copy(6).start()

    def finish(self):
        for kind in range(5, self.kinds):
            self.wait(kind)

    def sent(self):
        for kind in range(self.kinds):
            self.copy(kind).wait_send()


class Rows:
    def __init__(self, here, whole, rows, send, recv):
        self.h, self.whole, self.rows, self.send_sem, self.recv_sem = here, whole, rows, send, recv

    def place(self, half, owner):
        return self.rows.at[half, :, pl.ds(pl.multiple_of(owner * 256, 256), 256)]

    def copy(self, q, c):
        h = self.h
        return push(
            self.whole.at[q, c], self.place(q % 2, h.f),
            self.send_sem.at[q, c], self.recv_sem.at[h.f, q % 2], (h.b, 2 * c + q // 2),
        )

    def begin(self):
        h = self.h
        for q in range(4):
            for c in range(2):
                owner = 2 * c + q // 2

                @pl.when(h.f != owner)
                def _(q=q, c=c):
                    self.copy(q, c).start()

                @pl.when(h.f == owner)
                def _(q=q, c=c, owner=owner):
                    self.rows[q % 2, :, owner * 256 : (owner + 1) * 256] = self.whole[q, c]

    def finish(self):
        h = self.h
        for owner in range(OWNERS):

            @pl.when(h.f != owner)
            def _(owner=owner):
                for half in range(2):
                    ref = self.place(half, owner)
                    push(
                        ref, ref, self.send_sem.at[0, 0], self.recv_sem.at[owner, half],
                        (h.b, owner),
                    ).wait_recv()

        for q in range(4):
            for c in range(2):

                @pl.when(h.f != 2 * c + q // 2)
                def _(q=q, c=c):
                    self.copy(q, c).wait_send()


def row_norm(rows):
    mean = jnp.mean(rows, axis=-1, keepdims=True)
    centred = rows - mean
    inv = lax.rsqrt(jnp.mean(centred * centred, axis=-1, keepdims=True) + EPSILON)
    return centred * inv, inv


def row_back(grad, normed, inv):
    return inv * (
        grad
        - jnp.mean(grad, axis=-1, keepdims=True)
        - normed * jnp.mean(grad * normed, axis=-1, keepdims=True)
    )


def first_half():
    lane = lax.broadcasted_iota(jnp.int32, (1, PAIR), 1)
    return lane % HEAD_DIM < HEAD_DIM // 2


def first_head():
    return lax.broadcasted_iota(jnp.int32, (1, PAIR), 1) < HEAD_DIM


def swap_halves(rows):
    up = pltpu.roll(rows, PAIR - HEAD_DIM // 2, 1)
    down = pltpu.roll(rows, HEAD_DIM // 2, 1)
    return jnp.where(first_half(), up, down)


def only(rows, head):
    keep = first_head() if head == 0 else jnp.logical_not(first_head())
    return jnp.where(keep, rows, jnp.zeros_like(rows))


def quarter(ref, j):
    tile = ref[:, :, j * 256 : (j + 1) * 256]
    return tile.reshape(tile.shape[0] * tile.shape[1], 256)


def flat(ref):
    rows = ref[...]
    return rows.reshape(rows.shape[0] * rows.shape[1], rows.shape[2])


class Box:
    pass


IN_HBM = ("w_qkv", "w_in", "w_ffn")
GATHERS = ("xg", "cg", "ag", "rg")
SCATTERS = ("two", "out", "one")
CHUNKS = (
    ("ffn", UNIT_ROWS), ("ing", UNIT_ROWS), ("inz", UNIT_ROWS),
    ("att", ATTN_ROWS), ("que", ATTN_ROWS), ("key", ATTN_ROWS), ("val", ATTN_ROWS),
)


def layout(seqs, tok):
    rows, length = seqs * tok, tok * RING
    whole = (RING, rows, D)
    half = rows // 2
    ins = [
        "x", "cot", "gain_one", "gain_two", "w_qkv", "attn_w", "w_in", "w_ffn", "cos", "sin",
    ]
    outs = {
        "output": ((rows, D), BF16),
        "grad_x": ((rows, D), F32),
        "gains": ((8, 256), F32),
        "ffn_rows": ((2, UNIT_ROWS, D), BF16),
        "att_rows": ((2, ATTN_ROWS, D), BF16),
    }
    for name, high in CHUNKS:
        if name not in ("ffn", "att"):
            outs[name + "_all"] = ((4, 2, high, 256), BF16)
    sem = pltpu.SemaphoreType.DMA
    vm = pltpu.VMEM
    scratch = {
        "xs": vm(whole, BF16), "cots": vm(whole, BF16), "a1": vm(whole, BF16), "a2": vm(whole, BF16),
        "resids": vm(whole, BF16), "terms": vm(whole, F32),
        "qkv_w": vm((2, 256, 3 * PAIR), BF16), "in_w": vm((2, 256, 2 * UNITS_PAD), BF16),
        "ffn_w": vm((UNIT_ROWS, D), BF16), "windows": vm((2, 2, 256, WINDOW), BF16),
        "gain": vm((8, 256), F32), "gain_all": vm((8, D), F32), "qkv_c": vm((D, 3 * PAIR), BF16), "attn_all": vm((D, D), BF16),
        "in_c": vm((D, 2 * UNITS_PAD), BF16), "ffn_c": vm((UNITS_PAD, D), BF16),
        "qs": vm((seqs, length, PAIR), BF16), "ks": vm((seqs, length, PAIR), BF16),
        "vs": vm((seqs, length, PAIR), BF16), "os": vm((seqs, length, PAIR), F32),
        "lse": vm((seqs, length, PAIR), F32), "heads": vm((RING, rows, PAIR), BF16),
        "own_heads": vm((RING, rows, PAIR), BF16), "mixed": vm((RING, rows, PAIR), BF16),
        "joint": vm((RING, rows, 3 * PAIR), BF16),
        "fs": vm((RING, rows, UNITS_PAD), BF16), "dus": vm((RING, rows, 2 * UNITS_PAD), BF16),
        "n2": vm((rows, D), F32), "resid": vm((rows, D), F32), "dy": vm((rows, D), F32),
        "core_out": vm((4, rows, D), BF16), "near_out": vm((2, rows, D), BF16),
        "across_out": vm((2, half, D), BF16),
        "back_out": vm((2, rows, D), BF16), "back_in": vm((2, rows, D), BF16),
        "sums": vm((6, 8, D), F32), "sums_in": vm((5, 8, D), F32),
        "ffn_all": vm((4, 2, UNIT_ROWS, 256), BF16), "att_all": vm((4, 2, ATTN_ROWS, 256), BF16),
    }
    for name in GATHERS:
        scratch[name + "_sems"] = (sem((8,)), sem((8,)))
    for name in SCATTERS:
        scratch[name + "_core"] = vm((4, rows, D), BF16)
        scratch[name + "_near"] = vm((2, rows, D), BF16)
        scratch[name + "_across"] = vm((2, half, D), BF16)
        scratch[name + "_sems"] = (sem((8,)), sem((8,)))
    for name, high in CHUNKS:
        scratch[name + "_g"] = vm((2, 2, high, 256), BF16)
        scratch[name + "_far"] = vm((2, high, 256), BF16)
        scratch[name + "_high"] = vm((2, high, 256), BF16)
        scratch[name + "_core"] = vm((high, 256), BF16)
        scratch[name + "_sems"] = (sem((7,)), sem((7,)))
    for name, count in (("swap", 4), ("part", 9), ("attn", 5), ("head", RING - 1), ("sum", 5)):
        scratch[name + "_sems"] = (sem((count,)), sem((count,)))
    scratch["ffn_w_sems"] = (sem((2,)), sem((1,)))
    scratch["cut_sems"] = (sem((2, 3)), sem((2, 2)), sem((1,)))
    for name in ("ffn_rows", "att_rows"):
        scratch[name + "_sems"] = (sem((4, 2)), sem((4, 2)))
    return ins, outs, scratch


def layer_kernel(names, *refs):
    r = Box()
    for name, ref in zip(names, refs):
        setattr(r, name, ref)
    h = Here()
    seqs, length = r.qs.shape[0], r.qs.shape[1]
    tok = length // RING
    scale = HEAD_DIM ** (-0.5)
    moved = h.high != h.c
    there = (h.bh, h.core)
    there_p = h.high * 4 + h.q
    cut_q, cut_i, cut_f = r.cut_sems

    def cut_qkv(c, i):
        start = i * D + h.mine_of(c) * PAIR
        return pltpu.make_async_copy(
            r.w_qkv.at[:, pl.ds(pl.multiple_of(start, PAIR), PAIR)],
            r.qkv_w.at[c, :, i * PAIR : (i + 1) * PAIR], cut_q.at[c, i],
        )

    def window(c, i):
        start = i * FF + h.mine_of(c) * UNITS
        return start, jnp.minimum(start // PAIR * PAIR, 2 * FF - WINDOW)

    def cut_in(c, i):
        return pltpu.make_async_copy(
            r.w_in.at[:, pl.ds(pl.multiple_of(window(c, i)[1], PAIR), WINDOW)],
            r.windows.at[c, i], cut_i.at[c, i],
        )

    cut_ffn = pltpu.make_async_copy(
        r.w_ffn.at[pl.ds(pl.multiple_of(h.x * (UNITS - 8), 16), UNIT_ROWS)], r.ffn_w, cut_f.at[0]
    )
    for c in range(2):
        for i in range(3):
            cut_qkv(c, i).start()
    for c in range(2):
        for i in range(2):
            cut_in(c, i).start()
    cut_ffn.start()

    h.greet()

    def swap(i, src, dst, back):
        send, recv = r.swap_sems
        return push(src, dst, send.at[i], recv.at[i], there)

    def swap_in(i, src, whole):
        @pl.when(moved)
        def _():
            swap(i, src, whole.at[there_p], False).start()

        @pl.when(jnp.logical_not(moved))
        def _():
            whole[h.p] = src[...]

    def swap_got(i, src, whole):
        @pl.when(moved)
        def _():
            swap(i, whole.at[h.p], whole.at[h.p], False).wait_recv()

    def swap_sent(i, src, whole):
        @pl.when(moved)
        def _():
            swap(i, src, whole.at[there_p], False).wait_send()

    swap_in(0, r.x, r.xs)

    p_send, p_recv = r.part_sems
    peers = (h.far, h.core, h.diag)

    def part_at(whole, owner, lanes):
        if lanes:
            return whole.at[:, pl.ds(pl.multiple_of(owner * 256, 256), 256)]
        return whole.at[pl.ds(pl.multiple_of(owner * 256, 256), 256)]

    def part(i, src, whole, lanes, sliced):
        def copy(k):
            mine = (h.c, 1 - h.c, 1 - h.c)[k]
            return push(
                src.at[mine] if sliced else src, part_at(whole, h.f, lanes),
                p_send.at[3 * i + k], p_recv.at[3 * i + k], (h.b, peers[k]),
            )

        box = Box()

        def begin():
            for k in range(3):
                copy(k).start()
            place = part_at(whole, h.f, lanes)
            place[...] = src[h.c] if sliced else src[...]

        def got():
            for k in range(3):
                ref = part_at(whole, peers[k], lanes)
                push(ref, ref, p_send.at[3 * i + k], p_recv.at[3 * i + k], (h.b, peers[k])).wait_recv()

        def sent():
            for k in range(3):
                copy(k).wait_send()

        box.begin, box.got, box.sent = begin, got, sent
        return box

    gain_p = part(0, r.gain, r.gain_all, True, False)
    qkv_p = part(1, r.qkv_w, r.qkv_c, False, True)
    in_p = part(2, r.in_w, r.in_c, False, True)

    def attn_half(owner, half):
        return r.attn_all.at[pl.ds(pl.multiple_of(owner * 256 + half * 128, 128), 128)]

    def attn_copy(k):
        own_half = pl.ds(pl.multiple_of(h.x * 128, 128), 128)
        came, later = attn_half(h.far, h.x), attn_half(h.far, 1 - h.x)
        src, dst, device = (
            (r.attn_w.at[own_half], attn_half(h.f, h.x), (h.b, h.far)),
            (r.attn_w, part_at(r.attn_all, h.f, False), (h.b, h.core)),
            (came, came, (h.bx, h.f)),
            (came, came, (h.b, h.core)),
            (later, later, (h.b, h.core)),
        )[k]
        return push(src, dst, a_send.at[k], a_recv.at[k], device)

    def attn_wait(k):
        ref = (
            attn_half(h.far, h.x), part_at(r.attn_all, h.core, False), attn_half(h.far, 1 - h.x),
            attn_half(h.diag, h.x), attn_half(h.diag, 1 - h.x),
        )[k]
        push(ref, ref, a_send.at[k], a_recv.at[k], (h.b, h.core)).wait_recv()

    a_send, a_recv = r.attn_sems
    f_send, f_recv = r.ffn_w_sems
    active = h.c == h.low
    near_own = 2 * h.y + h.y
    far_own = 2 * (1 - h.y) + h.y
    ffn_owner = 2 * h.c + h.low
    unit_rows = pl.ds(0, UNIT_ROWS)

    def ffn_copy(k):
        return push(
            r.ffn_w.at[unit_rows], r.ffn_c.at[unit_rows],
            f_send.at[k], f_recv.at[0], (h.b, (near_own, far_own)[k]),
        )

    r.gain[...] = jnp.zeros((8, 256), F32)
    r.gain[0:1, :] = r.gain_one[...].astype(F32).reshape(1, 256)
    r.gain[1:2, :] = r.gain_two[...].astype(F32).reshape(1, 256)
    gain_p.begin()
    for c in range(2):
        for i in range(3):
            cut_qkv(c, i).wait()
    qkv_p.begin()
    lane = lax.broadcasted_iota(jnp.int32, (1, WINDOW), 1)
    inside = jnp.logical_and(lane >= 8 * h.x, lane < 8 * h.x + UNITS)
    for c in range(2):
        for i in range(2):
            cut_in(c, i).wait()
            start, left = window(c, i)
            turned = pltpu.roll(
                r.windows[c, i].astype(F32), lax.rem(left - start + 8 * h.x + WINDOW, WINDOW), 1
            )
            kept = jnp.where(inside, turned, 0.0)[:, :UNITS_PAD]
            r.in_w[c, :, i * UNITS_PAD : (i + 1) * UNITS_PAD] = kept.astype(BF16)
    cut_ffn.wait()
    swap_got(0, r.x, r.xs)
    swap_in(1, r.cot, r.cots)
    xg = Gather(h, r.xs, *r.xg_sems)
    xg.begin()
    cg = Gather(h, r.cots, *r.cg_sems)

    @pl.when(jnp.logical_not(moved))
    def _():
        cg.begin()

    gain_p.got()
    qkv_p.got()
    attn_copy(0).start()
    attn_copy(1).start()
    at_own = part_at(r.attn_all, h.f, False)
    at_own[...] = r.attn_w[...]
    r.ffn_c[UNIT_ROWS:, :] = jnp.zeros((UNITS_PAD - UNIT_ROWS, D), BF16)

    @pl.when(ffn_owner == h.f)
    def _():
        r.ffn_c[unit_rows, :] = r.ffn_w[unit_rows, :]

    def project(index):
        normed, _ = row_norm(r.xs[index].astype(F32))
        a1 = (normed * r.gain_all[0:1, :]).astype(BF16)
        r.a1[index] = a1
        r.terms[index, :, : 3 * PAIR] = contract(a1, r.qkv_c[...], 1, 0)

    def more_weights():
        attn_wait(0)
        attn_copy(2).start()
        attn_copy(3).start()
        in_p.begin()

        @pl.when(jnp.logical_not(moved))
        def _():
            cg.near()

    xg.each(project, more_weights)

    for s in range(seqs):
        rows = slice(s * tok, (s + 1) * tok)

        def columns(i):
            return r.terms[:, rows, i * PAIR : (i + 1) * PAIR].reshape(length, PAIR)

        cos, sin = r.cos[...], r.sin[...]
        query, key = columns(0), columns(1)
        q = (query * cos + swap_halves(query) * sin).astype(BF16)
        k = (key * cos + swap_halves(key) * sin).astype(BF16)
        v = columns(2).astype(BF16)
        r.qs[s] = q
        r.ks[s] = k
        r.vs[s] = v
        outs, lses = [], []
        for head in range(2):
            scores = contract(only(q, head), k, 1, 1) * scale
            top = jnp.max(scores, axis=-1, keepdims=True)
            e = jnp.exp(scores - top)
            total = jnp.sum(e, axis=-1, keepdims=True)
            outs.append(contract(e.astype(BF16), v, 1, 0) / total)
            lses.append(top + jnp.log(total))
        of = jnp.where(first_head(), outs[0], outs[1])
        r.os[s] = of
        r.lse[s] = jnp.where(first_head(), lses[0], lses[1])
        r.heads[:, rows, :] = of.astype(BF16).reshape(RING, tok, PAIR)

    h_send, h_recv = r.head_sems
    around = []
    for b, q in ((h.b, h.q), (h.bx, h.qx), (h.bz, h.qz), (h.bd, h.qd)):
        around += [((b, h.f), h.mine(q)), ((b, h.core), h.other(q))]

    def exchange(i):
        device, p = around[i + 1]
        return push(r.heads.at[p], r.own_heads.at[h.p], h_send.at[i], h_recv.at[i], device)

    for i in range(RING - 1):
        exchange(i).start()
    r.own_heads[h.p] = r.heads[h.p]
    @pl.when(moved)
    def _():
        swap(1, r.cots.at[h.p], r.cots.at[h.p], False).wait_recv()
        cg.begin()

    attn_wait(2)
    attn_copy(4).start()
    attn_wait(1)
    attn_wait(3)
    attn_wait(4)
    for i in range(RING - 1):
        device, p = around[i + 1]
        ref = r.own_heads.at[p]
        push(ref, ref, h_send.at[i], h_recv.at[i], device).wait_recv()

    @pl.when(moved)
    def _():
        cg.near()

    g2 = r.gain_all[1:2, :]
    mixed_heads = jnp.concatenate([r.own_heads[d] for d in range(RING)], axis=1)
    resid = r.xs[h.p].astype(F32) + contract(mixed_heads, r.attn_all[...], 1, 0)
    r.resid[...] = resid
    normed, inv_two = row_norm(resid)
    r.n2[...] = normed
    r.a2[h.p] = (normed * g2).astype(BF16)
    ag = Gather(h, r.a2, *r.ag_sems)
    ag.begin()

    @pl.when(active)
    def _():
        ffn_copy(1).start()

    @pl.when(jnp.logical_and(active, near_own != h.f))
    def _():
        ffn_copy(0).start()

    in_p.got()

    def widen(index):
        r.terms[index, :, : 2 * UNITS_PAD] = contract(r.a2[index], r.in_c[...], 1, 0)

    ag.each(widen)
    cg.across()
    for kind in range(4, 8):
        cg.wait(kind)
    @pl.when(ffn_owner != h.f)
    def _():
        ffn_copy(0).wait_recv()

    def feed(index):
        inner = r.terms[index, :, :UNITS_PAD]
        gating = r.terms[index, :, UNITS_PAD : 2 * UNITS_PAD]
        below = 0.5 * (1.0 + lax.erf(inner * 0.7071067811865476))
        density = jnp.exp(-0.5 * inner * inner) * 0.3989422804014327
        active = inner * below
        r.fs[index] = (active * gating).astype(BF16)
        grad_hidden = contract(r.cots[index], r.ffn_c[...], 1, 1)
        du = jnp.concatenate(
            [grad_hidden * gating * (below + inner * density), grad_hidden * active], axis=1
        ).astype(BF16)
        r.dus[index] = du
        r.terms[index] = contract(du, r.in_c[...], 1, 1)

    def scatter(name, split):
        return Scatter(
            h, r.terms, r.core_out, r.near_out, r.across_out,
            getattr(r, name + "_core"), getattr(r, name + "_near"), getattr(r, name + "_across"),
            *getattr(r, name + "_sems"), split,
        )

    ch = {}
    for name, _ in CHUNKS:
        ch[name] = Grads(
            h, getattr(r, name + "_g"), getattr(r, name + "_far"), getattr(r, name + "_high"),
            getattr(r, name + "_core"), getattr(r, name + "_all"), *getattr(r, name + "_sems"),
            name not in ("ffn", "ing"),
        )

    ffn, ing, inz, att = ch["ffn"], ch["ing"], ch["inz"], ch["att"]
    que, key, val = ch["que"], ch["key"], ch["val"]
    two = scatter("two", True)
    two.begin(feed)
    for j in range(OWNERS):
        r.ffn_g[j // 2, j % 2] = contract(flat(r.fs), quarter(r.cots, j), 0, 0)[:UNIT_ROWS].astype(BF16)
    ffn.to_far()
    two.second()
    for j in range(OWNERS):
        c, y = j % 2, j // 2
        grad_in = contract(flat(r.dus), quarter(r.a2, j), 0, 0).astype(BF16)
        r.ing_g[y, c] = grad_in[:UNIT_ROWS]
        r.inz_g[y, c] = grad_in[UNITS_PAD : UNITS_PAD + UNIT_ROWS]
    grad_two = two.finish()

    normed = r.n2[...]
    r.sums[0, 1:2, :] = jnp.sum(grad_two * normed, axis=0, keepdims=True)
    own_grad = r.cots[h.p].astype(F32) + row_back(grad_two * g2, normed, inv_two)
    r.dy[...] = own_grad
    r.resids[h.p] = own_grad.astype(BF16)
    rg = Gather(h, r.resids, *r.rg_sems, False)
    rg.begin()
    ffn.from_far()
    ffn.to_high()
    ing.to_far()

    attn_c = r.attn_all.at[pl.ds(pl.multiple_of(h.p * PAIR, PAIR), PAIR)]

    def mix(index):
        r.mixed[index] = contract(r.resids[index], attn_c[...], 1, 1).astype(BF16)

    def ing_far():
        ing.from_far()
        inz.to_far()

    def ffn_on():
        ffn.to_core()
        ing.to_high()

    rg.each(mix, ing_far, ffn_on)
    for j in range(OWNERS):
        r.att_g[j // 2, j % 2] = contract(flat(r.heads), quarter(r.resids, j), 0, 0).astype(BF16)
    ffn.to_near()

    for s in range(seqs):
        rows = slice(s * tok, (s + 1) * tok)
        q, k, v = r.qs[s], r.ks[s], r.vs[s]
        do = r.mixed[:, rows, :].reshape(length, PAIR)
        weighed = do.astype(F32) * r.os[s]
        dqs, dks, dvs = [], [], []
        for head in range(2):
            delta = jnp.sum(only(weighed, head), axis=-1, keepdims=True)
            lse = r.lse[s, :, head * HEAD_DIM : head * HEAD_DIM + 1]
            probs = jnp.exp(contract(only(q, head), k, 1, 1) * scale - lse)
            dvs.append(contract(probs.astype(BF16), do, 0, 0))
            grad_probs = contract(only(do, head), v, 1, 1)
            ds = (probs * (grad_probs - delta)).astype(BF16)
            dqs.append(contract(ds, k, 1, 0) * scale)
            dks.append(contract(ds, q, 0, 0) * scale)
        cos, sin = r.cos[...], r.sin[...]
        dq = jnp.where(first_head(), dqs[0], dqs[1])
        dk = jnp.where(first_head(), dks[0], dks[1])
        dv = jnp.where(first_head(), dvs[0], dvs[1])
        for i, item in enumerate(
            (dq * cos - swap_halves(dq) * sin, dk * cos - swap_halves(dk) * sin, dv)
        ):
            r.joint[:, rows, i * PAIR : (i + 1) * PAIR] = item.astype(BF16).reshape(RING, tok, PAIR)
        if s == 0:
            inz.from_far()
            att.to_far()

    def term(i):
        r.terms[i] = contract(r.joint[i], r.qkv_c[...], 1, 1)

    one = scatter("one", False)
    one.begin(term)
    for j in range(OWNERS):
        grad_qkv = contract(flat(r.joint), quarter(r.a1, j), 0, 0).astype(BF16)
        for i, name in enumerate(("que", "key", "val")):
            getattr(r, name + "_g")[j // 2, j % 2] = grad_qkv[i * PAIR : (i + 1) * PAIR]
    ffn.to_across()
    ing.to_core()
    inz.to_high()
    one.second()
    att.from_far()
    for item in (que, key, val):
        item.to_far()

    grad_one = one.finish()
    normed, inv_one = row_norm(r.xs[h.p].astype(F32))
    r.sums[0, 0:1, :] = jnp.sum(grad_one * normed, axis=0, keepdims=True)
    r.sums[0, 2:, :] = jnp.zeros((6, D), F32)
    s_send, s_recv = r.sum_sems
    partners = ((h.b, h.core), (h.b, h.far), (h.bx, h.f), (h.bz, h.f), (h.bh, h.f))

    def sum_copy(i):
        return push(r.sums.at[i], r.sums_in.at[i], s_send.at[i], s_recv.at[i], partners[i])

    def sum_step(i):
        sum_copy(i).wait_recv()
        r.sums[i + 1] = r.sums[i] + r.sums_in[i]
        if i < 4:
            sum_copy(i + 1).start()

    def back(i):
        return swap(2 + i, r.back_out.at[i], r.back_in.at[i], True)

    sum_copy(0).start()
    grad_x = r.dy[...] + row_back(grad_one * r.gain_all[0:1, :], normed, inv_one)
    r.grad_x[...] = grad_x
    r.back_out[1] = grad_x.astype(BF16)

    ing.to_near()
    for item in (que, key, val):
        item.from_far()
    for item in (att, que, key, val):
        item.to_high()

    def out_term(i):
        r.terms[i] = contract(r.fs[i], r.ffn_c[...], 1, 0)

    out = scatter("out", False)
    out.begin(out_term)
    sum_step(0)
    sum_step(1)
    ing.to_across()
    out.second()
    sum_step(2)
    att.to_core()
    att.to_near()
    que.to_core()
    que.to_near()
    sum_step(3)
    inz.to_core()
    inz.to_near()
    @pl.when(moved)
    def _():
        back(1).start()

    att.to_across()
    ffn.finish()
    ffn_rows = Rows(h, r.ffn_all, r.ffn_rows, *r.ffn_rows_sems)
    ffn_rows.begin()
    key.to_core()
    key.to_near()
    inz.to_across()
    sum_step(4)
    r.gains[...] = r.sums[5, :, pl.ds(pl.multiple_of(h.f * 256, 256), 256)]
    val.to_core()
    val.to_near()
    r.back_out[0] = (r.resid[...] + out.finish()).astype(BF16)

    @pl.when(moved)
    def _():
        back(0).start()

    que.to_across()
    att.finish()
    att_rows = Rows(h, r.att_all, r.att_rows, *r.att_rows_sems)
    att_rows.begin()
    key.to_across()
    val.to_across()

    @pl.when(moved)
    def _():
        for i in range(2):
            back(i).wait_recv()
            back(i).wait_send()
        r.output[...] = r.back_in[0]
        r.grad_x[...] = r.back_in[1].astype(F32)

    @pl.when(jnp.logical_not(moved))
    def _():
        r.output[...] = r.back_out[0]

    for name in ("ing", "inz", "que", "key", "val"):
        ch[name].finish()
    ffn_rows.finish()
    att_rows.finish()

    swap_sent(0, r.x, r.xs)
    swap_sent(1, r.cot, r.cots)
    for item in (xg, cg, ag, rg):
        item.sent()
    for item in (gain_p, qkv_p):
        item.sent()
    in_p.sent()
    for k in range(5):
        attn_copy(k).wait_send()

    @pl.when(active)
    def _():
        ffn_copy(1).wait_send()

    @pl.when(jnp.logical_and(active, near_own != h.f))
    def _():
        ffn_copy(0).wait_send()

    for i in range(RING - 1):
        exchange(i).wait_send()
    for i in range(5):
        sum_copy(i).wait_send()
    for name, _ in CHUNKS:
        ch[name].sent()


def finish_kernel(
    ing, inz, que, key, val, ffn, att, gains, y, dx, in_o, qkv_o, ffn_o, att_o, one_o, two_o, y_o, dx_o
):
    one_o[...] = gains[0:1, :]
    two_o[...] = gains[1:2, :]
    y_o[...] = y[...]
    dx_o[...] = dx[...]
    for q in range(4):
        for c in range(2):
            p = 4 * c + q
            for i, ref in enumerate((ing, inz)):
                start = i * FF + p * UNITS
                first = 8 * (q % 2)
                in_o[:, start : start + UNITS] = ref[q, c].astype(F32).T[:, first : first + UNITS]
            for i, ref in enumerate((que, key, val)):
                start = i * D + p * PAIR
                qkv_o[:, start : start + PAIR] = ref[q, c].astype(F32).T
    for half in range(2):
        first = 8 * half
        ffn_o[half * UNITS : (half + 1) * UNITS, :] = ffn[half].astype(F32)[first : first + UNITS]
        att_o[half * ATTN_ROWS : (half + 1) * ATTN_ROWS, :] = att[half].astype(F32)


def finish(ing, inz, que, key, val, ffn, att, gains, y, dx):
    def slices(high):
        return pl.BlockSpec((4, 2, high, 128), lambda i: (0, 0, 0, i))

    def rows(high):
        return pl.BlockSpec((2, high, D // 2), lambda i: (0, 0, i))

    own = pl.BlockSpec((y.shape[0] // 2, D), lambda i: (i, 0))
    return pl.pallas_call(
        finish_kernel,
        grid=(2,),
        out_shape=[
            jax.ShapeDtypeStruct((256, 2 * FF), F32),
            jax.ShapeDtypeStruct((256, 3 * D), F32),
            jax.ShapeDtypeStruct((2 * UNITS, D), F32),
            jax.ShapeDtypeStruct((2 * ATTN_ROWS, D), F32),
            jax.ShapeDtypeStruct((1, 256), F32),
            jax.ShapeDtypeStruct((1, 256), F32),
            jax.ShapeDtypeStruct(y.shape, BF16),
            jax.ShapeDtypeStruct(dx.shape, F32),
        ],
        in_specs=[slices(UNIT_ROWS)] * 2
        + [slices(ATTN_ROWS)] * 3
        + [rows(UNIT_ROWS), rows(ATTN_ROWS), pl.BlockSpec((8, 128), lambda i: (0, i)), own, own],
        out_specs=[
            pl.BlockSpec((128, 2 * FF), lambda i: (i, 0)),
            pl.BlockSpec((128, 3 * D), lambda i: (i, 0)),
            pl.BlockSpec((2 * UNITS, D // 2), lambda i: (0, i)),
            pl.BlockSpec((2 * ATTN_ROWS, D // 2), lambda i: (0, i)),
            pl.BlockSpec((1, 128), lambda i: (0, i)),
            pl.BlockSpec((1, 128), lambda i: (0, i)),
            own,
            own,
        ],
        compiler_params=pltpu.CompilerParams(vmem_limit_bytes=VMEM_BYTES),
    )(ing, inz, que, key, val, ffn, att, gains, y, dx)


def rotary_rows(length):
    half = HEAD_DIM // 2
    freq = (np.float32(ROPE_THETA) ** (-(np.arange(half, dtype=np.float32) * 2.0) / HEAD_DIM)).astype(
        np.float32
    )
    angles = np.arange(length, dtype=np.float32)[:, None] * freq[None, :]
    cos, sin = np.cos(angles), np.sin(angles)
    return np.tile(cos, (1, 4)), np.tile(np.concatenate([-sin, sin], axis=1), (1, 2))


def by_squares(inputs, gain_one, w_qkv, w_attn, gain_two, w_in, w_ffn, cotangent):
    seqs, tok, _ = inputs.shape
    rows = seqs * tok

    cos, sin = (jnp.asarray(t, F32) for t in rotary_rows(tok * RING))

    ins, outs, scratch = layout(seqs, tok)
    names, shapes = [], []
    for name, item in scratch.items():
        pair = item if isinstance(item, tuple) else (item,)
        names.append((name, len(pair)))
        shapes += pair

    def body(*refs):
        count = len(ins) + len(outs)
        rest = list(refs[count:])
        found = list(refs[:count])
        for _, size in names:
            taken = tuple(rest[:size])
            rest = rest[size:]
            found.append(taken if size > 1 else taken[0])
        layer_kernel(ins + list(outs) + [name for name, _ in names], *found)

    vmem = pl.BlockSpec(memory_space=pltpu.VMEM)
    hbm = pl.BlockSpec(memory_space=pl.ANY)
    done = pl.pallas_call(
        body,
        out_shape=[jax.ShapeDtypeStruct(shape, dtype) for shape, dtype in outs.values()],
        in_specs=[hbm if name in IN_HBM else vmem for name in ins],
        out_specs=[vmem] * len(outs),
        scratch_shapes=shapes,
        compiler_params=pltpu.CompilerParams(
            collective_id=0, has_side_effects=True, vmem_limit_bytes=VMEM_BYTES
        ),
    )(
        inputs.reshape(rows, D), cotangent.reshape(rows, D),
        gain_one, gain_two, w_qkv, w_attn, w_in, w_ffn, cos, sin,
    )
    done = dict(zip(outs, done))
    grad_in, grad_qkv, grad_ffn, grad_attn, grad_one, grad_two, output, grad_x = finish(
        done["ing_all"], done["inz_all"], done["que_all"], done["key_all"], done["val_all"],
        done["ffn_rows"], done["att_rows"], done["gains"], done["output"], done["grad_x"],
    )
    return (
        output.reshape(seqs, tok, D),
        grad_x.reshape(seqs, tok, D),
        grad_one.reshape(256),
        grad_qkv,
        grad_attn,
        grad_two.reshape(256),
        grad_in,
        grad_ffn,
    )


def solution(mesh):
    split_ok = mesh.shape["ctx"] == RING and mesh.shape["fsdp"] == OWNERS

    return jax.shard_map(
        by_squares if split_ok else on_device,
        mesh=mesh,
        in_specs=(
            P("fsdp", "ctx", None),
            P("fsdp"),
            P("fsdp", None),
            P("fsdp", None),
            P("fsdp"),
            P("fsdp", None),
            P("fsdp", None),
            P("fsdp", "ctx", None),
        ),
        out_specs=(
            P("fsdp", "ctx", None),
            P("fsdp", "ctx", None),
            P("fsdp"),
            P("fsdp", None),
            P("fsdp", None),
            P("fsdp"),
            P("fsdp", None),
            P("fsdp", None),
        ),
        check_vma=False,
    )
```
